32 devices in a mesh: dp: 8 (over y, x, core), mp: 4 (over z).
Axes of the slice: x: 2, y: 2, z: 4, core: 2. Of those that a mesh axis runs over, the one named last changes fastest.
Arguments:
- hidden: bfloat16 [4096, 768], P('dp'), may hold values from -6 to 6
- memory: bfloat16 [32768, 768], P('dp', 'mp'), may hold values from -6 to 6
- out_grad: bfloat16 [4096, 768], P('dp'), may hold values from -6 to 6
- dec_starts: int32 [32, 4], P('dp'), may hold values from 0 to 127, as said below
- dec_length: int32 [32], P('dp'), may hold values from 96 to 128
- mem_starts: int32 [32, 4], P('dp'), may hold values from 0 to 1023, as said below
- mem_length: int32 [32], P('dp'), may hold values from 768 to 1024
- self_qkv: bfloat16 [3, 768, 768], P(None, None, 'mp'), may hold values from -0.25 to 0.25
- self_qv_bias: float32 [2, 768], P(None, 'mp'), may hold values from -3 to 3
- self_proj: bfloat16 [768, 768], P('mp'), may hold values from -0.3125 to 0.3125
- cross_query: bfloat16 [768, 768], P(None, 'mp'), may hold values from -0.25 to 0.25
- cross_kv: bfloat16 [2, 768, 768], P(None, None, 'mp'), may hold values from -0.25 to 0.25
- cross_qv_bias: float32 [2, 768], P(None, 'mp'), may hold values from -3 to 3
- cross_proj: bfloat16 [768, 768], P('mp'), may hold values from -0.875 to 0.875
- ffn_in: bfloat16 [768, 3072], P(None, 'mp'), may hold values from -0.21875 to 0.21875
- ffn_in_bias: float32 [3072], P('mp'), may hold values from -3 to 3
- ffn_out: bfloat16 [3072, 768], P('mp'), may hold values from -0.15625 to 0.15625
- out_biases: float32 [3, 768], replicated, may hold values from -3 to 3
- norm_gains: float32 [3, 768], replicated, may hold values from 0.25 to 1.75
- norm_biases: float32 [3, 768], replicated, may hold values from -2 to 2
Outputs:
- result: bfloat16 [4096, 768], P('dp')
- hidden_grad: float32 [4096, 768], P('dp')
- memory_grad: float32 [32768, 768], P('dp', 'mp')
- self_qkv_grad: float32 [3, 768, 768], P(None, None, 'mp')
- self_qv_bias_grad: float32 [2, 768], P(None, 'mp')
- self_proj_grad: float32 [768, 768], P('mp')
- cross_query_grad: float32 [768, 768], P(None, 'mp')
- cross_kv_grad: float32 [2, 768, 768], P(None, None, 'mp')
- cross_qv_bias_grad: float32 [2, 768], P(None, 'mp')
- cross_proj_grad: float32 [768, 768], P('mp')
- ffn_in_grad: float32 [768, 3072], P(None, 'mp')
- ffn_in_bias_grad: float32 [3072], P('mp')
- ffn_out_grad: float32 [3072, 768], P('mp')
- out_biases_grad: float32 [3, 768], replicated
- norm_gains_grad: float32 [3, 768], replicated
- norm_biases_grad: float32 [3, 768], replicated
The draws below stay inside these ranges and needn't reach their ends.
Inputs may be any that keep to these rules, and one draw needn't show every extreme that they name: `dec_starts`: each packed row holds 4 pairs; its offsets start at 0, rise strictly and stay below the row's used slots, so every decoder segment holds at least one used slot; padded slots belong to the last pair. `mem_starts`: pair j's table is memory segment j of the same packed row; offsets start at 0, rise strictly and stay below the row's used slots, so every memory segment holds at least one used slot.
All inputs are finite; a program needn't handle non-finite values.
Results may differ from the reference program's by a relative error of at most 0.023.
Values may be sent and summed in bfloat16 or wider, within the bound.
No kernel may reach another device: no remote copies, remote signals or barrier semaphores. Data moves between devices by JAX's collectives and lax.ppermute only.
A program may use at most 128 MiB of HBM per device.

```python
import math
import jax
import jax.numpy as jnp
from jax import lax

D = 768
HEADS = 12
HD = 64
FF = 3072
LQ = 128
LM = 1024
NSEG = 4
ROWS = 32
TOKENS = 4096
MEM_TOKENS = 32768


def layout(key, slot_count):
    pad_key, pick_key, share_key = jax.random.split(key, 3)
    most_pad = slot_count // 4
    padding = jax.random.randint(pad_key, (ROWS,), 0, most_pad + 1)
    ordering = jax.random.permutation(pick_key, ROWS)
    padding = padding.at[ordering[0]].set(0).at[ordering[1]].set(most_pad)
    lengths = slot_count - padding
    shares = jax.random.randint(share_key, (ROWS, NSEG), 1, 4)
    before = jnp.cumsum(shares, axis=1) - shares
    totals = jnp.sum(shares, axis=1)
    starts = lengths[:, None] * before // totals[:, None]
    starts = starts.at[ordering[0], NSEG - 1].set(slot_count - 1)
    return (starts.astype(jnp.int32), lengths.astype(jnp.int32))


def draw_dec_starts(key, part):
    return layout(jax.random.fold_in(key, 11), LQ)[0]


def draw_dec_length(key, part):
    return layout(jax.random.fold_in(key, 11), LQ)[1]


def draw_mem_starts(key, part):
    return layout(jax.random.fold_in(key, 23), LM)[0]


def draw_mem_length(key, part):
    return layout(jax.random.fold_in(key, 23), LM)[1]


def block_scale(own_key, shape, cuts, low, largest):
    gain = 1.0
    for axis_at, parts in cuts:
        heights = jax.random.uniform(jax.random.fold_in(jax.random.fold_in(own_key, 6), axis_at), (parts,), jnp.float32, low / len(cuts), largest / len(cuts))
        gain = gain * jnp.repeat(jnp.exp(heights), shape[axis_at] // parts).reshape((-1,) + (1,) * (len(shape) - 1 - axis_at))
    return gain


def scatter_about(rng, dims, spread, bound, cuts=(), kind=jnp.bfloat16):
    factor_of = block_scale(rng, dims, cuts, -0.22, 0.18) if cuts else 1.0
    result = jax.random.normal(rng, dims, jnp.float32) * spread * factor_of
    return jnp.minimum(jnp.maximum(result, -bound), bound).astype(kind)


def setup_inputs(seed: int = 0) -> dict:
    seeds = jax.random.split(jax.random.key(seed), 21)
    hidden = scatter_about(seeds[0], (TOKENS, D), 1.0, 6.0, ((0, 8),))
    memory = scatter_about(seeds[1], (MEM_TOKENS, D), 1.0, 6.0, ((0, 8), (1, 4)))
    out_grad = scatter_about(seeds[2], (TOKENS, D), 1.0, 6.0, ((0, 8),))
    dec_starts = draw_dec_starts(jax.random.fold_in(seeds[20], 71), 0)
    dec_length = draw_dec_length(jax.random.fold_in(seeds[20], 71), 0)
    mem_starts = draw_mem_starts(jax.random.fold_in(seeds[20], 71), 0)
    mem_length = draw_mem_length(jax.random.fold_in(seeds[20], 71), 0)
    self_qkv = scatter_about(seeds[7], (3, D, D), (2 * D // 3) ** -0.5, 0.25, ((2, 4),))
    self_qv_bias = scatter_about(seeds[8], (2, D), 0.5, 3.0, ((1, 4),), jnp.float32)
    self_proj = scatter_about(seeds[9], (D, D), (D // 2) ** -0.5, 0.3125, ((0, 4),))
    cross_query = scatter_about(seeds[10], (D, D), (2 * D // 3) ** -0.5, 0.25, ((1, 4),))
    cross_kv = scatter_about(seeds[11], (2, D, D), (2 * D // 3) ** -0.5, 0.25, ((2, 4),))
    cross_qv_bias = scatter_about(seeds[12], (2, D), 0.5, 3.0, ((1, 4),), jnp.float32)
    cross_proj = scatter_about(seeds[13], (D, D), (D // 16) ** -0.5, 0.875, ((0, 4),))
    ffn_in = scatter_about(seeds[14], (D, FF), D ** -0.5, 0.21875, ((1, 4),))
    ffn_in_bias = scatter_about(seeds[15], (FF,), 0.5, 3.0, ((0, 4),), jnp.float32)
    ffn_out = scatter_about(seeds[16], (FF, D), (FF // 2) ** -0.5, 0.15625, ((0, 4),))
    out_biases = scatter_about(seeds[17], (3, D), 0.5, 3.0, (), jnp.float32)
    norm_gains = jnp.clip(1.0 + 0.15 * jax.random.normal(seeds[18], (3, D), jnp.float32), 0.25, 1.75)
    norm_biases = scatter_about(seeds[19], (3, D), 0.3, 2.0, (), jnp.float32)
    return dict(hidden=hidden, memory=memory, out_grad=out_grad, dec_starts=dec_starts, dec_length=dec_length, mem_starts=mem_starts, mem_length=mem_length, self_qkv=self_qkv, self_qv_bias=self_qv_bias, self_proj=self_proj, cross_query=cross_query, cross_kv=cross_kv, cross_qv_bias=cross_qv_bias, cross_proj=cross_proj, ffn_in=ffn_in, ffn_in_bias=ffn_in_bias, ffn_out=ffn_out, out_biases=out_biases, norm_gains=norm_gains, norm_biases=norm_biases)


@jax.custom_vjp
def low(v):
    return lax.optimization_barrier(v.astype(jnp.bfloat16)).astype(jnp.float32)

@jax.custom_vjp
def low_back(v):
    return v

def low_keep(v):
    return (low(v), None)

def low_pass(kept, grad):
    return (grad,)

def back_keep(v):
    return (v, None)

def back_low(kept, grad):
    return (low(grad),)
low.defvjp(low_keep, low_pass)
low_back.defvjp(back_keep, back_low)
NEG_FILL = -1000000000.0
EPSILON = 1e-05
HIGHEST_PRECISION = lax.Precision.HIGHEST

def matmul(left_side, right_side):
    return jnp.dot(left_side, right_side, precision=HIGHEST_PRECISION, preferred_element_type=jnp.float32)

def layer_norm(values, gain_row, bias_row):
    average = lax.optimization_barrier(jnp.mean(values, -1, keepdims=True))
    centered = values - average
    variance = lax.optimization_barrier(jnp.mean(centered * centered, -1, keepdims=True))
    return centered * lax.rsqrt(variance + EPSILON) * gain_row + bias_row

def segment_ids(starts, slot_count):
    places = jnp.arange(slot_count, dtype=jnp.int32)
    return lax.optimization_barrier(jnp.sum((starts[:, None, :] <= places[None, :, None]).astype(jnp.int32), -1)) - 1

def attention(queries, key_rows, value_rows, allowed):
    row_count = allowed.shape[0]
    heads_q = queries.reshape(row_count, allowed.shape[1], HEADS, HD)
    heads_k = key_rows.reshape(row_count, allowed.shape[2], HEADS, HD)
    heads_v = value_rows.reshape(row_count, allowed.shape[2], HEADS, HD)
    scores = low_back(jnp.einsum('rqhd,rkhd->rhqk', heads_q, heads_k, precision=HIGHEST_PRECISION))
    scores = jnp.where(allowed[:, None], scores, NEG_FILL)
    prob_low = low(jax.nn.softmax(scores, axis=-1))
    output = jnp.einsum('rhqk,rkhd->rqhd', prob_low, heads_v, precision=HIGHEST_PRECISION)
    return output.reshape(row_count * allowed.shape[1], HEADS * HD)

def forward(hidden_rows, memory_rows, params, self_allowed, cross_allowed):
    self_qkv, self_qv_bias, self_proj, cross_query, cross_kv, cross_qv_bias, cross_proj, ffn_in, ffn_in_bias, ffn_out, out_biases, norm_gains, norm_biases = params
    scaling = HD ** (-0.5)
    self_q = (low_back(matmul(hidden_rows, self_qkv[0])) + self_qv_bias[0]) * scaling
    self_k = low_back(matmul(hidden_rows, self_qkv[1]))
    self_v = low_back(matmul(hidden_rows, self_qkv[2])) + self_qv_bias[1]
    self_o = low(low_back(attention(low(self_q), low(self_k), low(self_v), self_allowed)))
    first = layer_norm(hidden_rows + low_back(matmul(self_o, self_proj)) + out_biases[0], norm_gains[0], norm_biases[0])
    first_low = low(first)
    cross_q = (low_back(matmul(first_low, cross_query)) + cross_qv_bias[0]) * scaling
    cross_k = low_back(matmul(memory_rows, cross_kv[0]))
    cross_v = low_back(matmul(memory_rows, cross_kv[1])) + cross_qv_bias[1]
    cross_o = low(low_back(attention(low(cross_q), low(cross_k), low(cross_v), cross_allowed)))
    second = layer_norm(first + low_back(matmul(cross_o, cross_proj)) + out_biases[1], norm_gains[1], norm_biases[1])
    second_low = low(second)
    hidden_pre = low_back(matmul(second_low, ffn_in)) + ffn_in_bias
    activated = low(jax.nn.gelu(hidden_pre, approximate=False))
    return layer_norm(second + low_back(matmul(activated, ffn_out)) + out_biases[2], norm_gains[2], norm_biases[2])

def reference(hidden, memory, out_grad, dec_starts, dec_length, mem_starts, mem_length, self_qkv, self_qv_bias, self_proj, cross_query, cross_kv, cross_qv_bias, cross_proj, ffn_in, ffn_in_bias, ffn_out, out_biases, norm_gains, norm_biases):
    row_total = dec_starts.shape[0]
    group_rows = math.gcd(row_total, 8)
    step_count = row_total // group_rows
    params = tuple((member.astype(jnp.float32) for member in (self_qkv, self_qv_bias, self_proj, cross_query, cross_kv, cross_qv_bias, cross_proj, ffn_in, ffn_in_bias, ffn_out, out_biases, norm_gains, norm_biases)))
    dec_places = jnp.arange(LQ, dtype=jnp.int32)
    mem_places = jnp.arange(LM, dtype=jnp.int32)

    def scan_step(running, pieces):
        hidden_rows, memory_rows, grad_rows, dec_first, dec_used, mem_first, mem_used = pieces
        dec_segment = segment_ids(dec_first, LQ)
        mem_segment = segment_ids(mem_first, LM)
        self_allowed = (dec_segment[:, :, None] == dec_segment[:, None, :]) & (dec_places[None, None, :] <= dec_places[None, :, None]) & (dec_places[None, None, :] < dec_used[:, None, None])
        cross_allowed = (dec_segment[:, :, None] == mem_segment[:, None, :]) & (mem_places[None, None, :] < mem_used[:, None, None])

        def group_forward(hidden_part, memory_part, weights):
            return forward(hidden_part, memory_part, weights, self_allowed, cross_allowed)
        output, pullback = jax.vjp(group_forward, hidden_rows.astype(jnp.float32), memory_rows.astype(jnp.float32), params)
        hidden_grad, memory_grad, weight_grads = pullback(grad_rows.astype(jnp.float32))
        running = jax.tree.map(lambda left_side, right_side: left_side + right_side, running, weight_grads)
        return (running, (output.astype(jnp.bfloat16), hidden_grad, memory_grad))
    initial = jax.tree.map(jnp.zeros_like, params)
    pieces = (hidden.reshape(step_count, group_rows * LQ, D), memory.reshape(step_count, group_rows * LM, D), out_grad.reshape(step_count, group_rows * LQ, D), dec_starts.reshape(step_count, group_rows, NSEG), dec_length.reshape(step_count, group_rows), mem_starts.reshape(step_count, group_rows, NSEG), mem_length.reshape(step_count, group_rows))
    totals, (outputs, hidden_grads, memory_grads) = lax.scan(scan_step, initial, pieces)
    self_qkv_grad, self_qv_bias_grad, self_proj_grad, cross_query_grad, cross_kv_grad, cross_qv_bias_grad, cross_proj_grad, ffn_in_grad, ffn_in_bias_grad, ffn_out_grad, out_biases_grad, norm_gains_grad, norm_biases_grad = totals
    return (outputs.reshape(row_total * LQ, D), hidden_grads.reshape(row_total * LQ, D), memory_grads.reshape(row_total * LM, D), self_qkv_grad, self_qv_bias_grad, self_proj_grad, cross_query_grad, cross_kv_grad, cross_qv_bias_grad, cross_proj_grad, ffn_in_grad, ffn_in_bias_grad, ffn_out_grad, out_biases_grad, norm_gains_grad, norm_biases_grad)
```

```python
import jax
import jax.numpy as jnp
from jax import lax
from jax.sharding import PartitionSpec as P

HD = 64
SUB = 8
NEG_FILL = -1000000000.0
EPSILON = 1e-05
F32 = jnp.float32
BF16 = jnp.bfloat16


def layer_norm(values, gain_row, bias_row):
    average = jnp.mean(values, -1, keepdims=True)
    centered = values - average
    variance = jnp.mean(centered * centered, -1, keepdims=True)
    return centered * lax.rsqrt(variance + EPSILON) * gain_row + bias_row


def exact_gelu(values):
    return jax.nn.gelu(values, approximate=False)


def segment_ids(starts, slot_count):
    places = jnp.arange(slot_count, dtype=jnp.int32)
    return jnp.sum((starts[None, :] <= places[:, None]).astype(jnp.int32), -1) - 1


def ein(spec, left, right):
    return jnp.einsum(spec, left, right, preferred_element_type=F32)


def attend(queries, keys_t, values_t, allowed):
    scores = ein("htd,hds->hts", queries, keys_t)
    scores = jnp.where(allowed[None], scores, NEG_FILL)
    weights = jnp.exp(scores - jnp.max(scores, -1, keepdims=True))
    probs = weights / jnp.sum(weights, -1, keepdims=True)
    return ein("hts,hds->htd", probs.astype(BF16), values_t), probs


def attend_back(queries, keys_t, values_t, probs, grad_rows):
    prob_low = probs.astype(BF16)
    values_grad = ein("hts,htd->hds", prob_low, grad_rows)
    prob_grad = ein("htd,hds->hts", grad_rows, values_t)
    offset = jnp.sum(probs * prob_grad, -1, keepdims=True)
    score_grad = (probs * (prob_grad - offset)).astype(BF16)
    return (
        ein("hts,hds->htd", score_grad, keys_t),
        ein("hts,htd->hds", score_grad, queries),
        values_grad,
    )


def solution(mesh):
    dp = mesh.shape["dp"]
    mp = mesh.shape["mp"]

    def swap(value, bit):
        return lax.ppermute(value, "dp", [(i, i ^ bit) for i in range(dp)])

    def shift(value, step):
        return lax.ppermute(value, "mp", [(i, (i + step) % mp) for i in range(mp)])

    def gather_line(own):
        return jnp.stack([own] + [shift(own, step) for step in range(1, mp)])

    def gather_plane(own, place):
        half = own.shape[0] // 2
        over_two = swap(own, 2)
        over_four = swap(own, 4)
        across = jnp.concatenate([swap(over_four[:half], 2), swap(over_two[half:], 4)])
        whole = jnp.zeros(own.shape[:1] + (SUB,) + own.shape[1:], own.dtype)
        for offset, piece in ((0, own), (2, over_two), (4, over_four), (6, across)):
            for bit in (0, 1):
                part = swap(piece, 1) if bit else piece
                start = (0, place ^ (offset | bit)) + (0,) * (own.ndim - 1)
                whole = lax.dynamic_update_slice(whole, part[:, None], start)
        return whole

    def reduce_plane(parts, place):
        def part(offset):
            return lax.dynamic_index_in_dim(parts, place ^ offset, 1, keepdims=False)

        half = parts.shape[0] // 2
        sums = {}
        for offset in (6, 2, 4, 0):
            sums[offset] = part(offset) + swap(part(offset ^ 1).astype(BF16), 1)
        far = sums[6].astype(BF16)
        near_two = swap(sums[2][:half].astype(BF16), 2)
        near_four = swap(sums[4][half:].astype(BF16), 4)
        late_four = sums[4][:half] + swap(far[:half], 2)
        late_two = sums[2][half:] + swap(far[half:], 4)
        late_two = swap(late_two.astype(BF16), 2)
        late_four = swap(late_four.astype(BF16), 4)
        return sums[0] + jnp.concatenate(
            [near_two.astype(F32) + late_four, near_four.astype(F32) + late_two]
        )

    def reduce_line(parts):
        total = parts[0]
        for step in range(1, mp):
            total = total + shift(parts[step].astype(BF16), -step)
        return total

    def reduce_outer(total):
        bit = SUB
        while bit < dp:
            total = total + swap(total, bit)
            bit *= 2
        return total

    def reduce_group(parts, place):
        total = reduce_outer(reduce_line(reduce_plane(parts, place)))
        low = total.astype(BF16)
        rows, width = low.shape
        pieces = low.reshape(2, rows // 2, width)
        whole = gather_plane(pieces, place)
        return jnp.swapaxes(whole, 0, 1).reshape(SUB, rows, width).astype(F32)

    def sum_everywhere(total):
        bit = 1
        while bit < dp:
            total = total + swap(total, bit)
            bit *= 2
        bit = 1
        while bit < mp:
            total = total + lax.ppermute(total, "mp", [(i, i ^ bit) for i in range(mp)])
            bit *= 2
        return total

    def body(
        hidden,
        memory,
        out_grad,
        dec_starts,
        dec_length,
        mem_starts,
        mem_length,
        self_qkv,
        self_qv_bias,
        self_proj,
        cross_query,
        cross_kv,
        cross_qv_bias,
        cross_proj,
        ffn_in,
        ffn_in_bias,
        ffn_out,
        out_biases,
        norm_gains,
        norm_biases,
    ):
        row_count = dec_starts.shape[0]
        assert row_count == mp
        slots = hidden.shape[0] // row_count
        mem_slots = memory.shape[0] // row_count
        width = hidden.shape[1]
        local = self_proj.shape[0]
        heads = local // HD
        inner = ffn_out.shape[0]
        scaling = HD ** (-0.5)
        line = lax.axis_index("mp")
        place = lax.axis_index("dp") % SUB
        from_line = (line - jnp.arange(mp)) % mp

        def row_of(array, size):
            return lax.dynamic_slice_in_dim(array, line * size, size, 0)

        def slice_of(array):
            size = array.shape[0] // SUB
            return lax.dynamic_slice_in_dim(array, place * size, size, 0)

        head_in = jnp.concatenate(
            [jnp.swapaxes(self_qkv, 1, 2).reshape(3 * local, width), cross_query.T]
        )
        head_out = jnp.concatenate([self_proj, cross_proj])
        key_value = jnp.swapaxes(cross_kv, 1, 2).reshape(2 * local, width)
        first_piece = jnp.concatenate([slice_of(head_in), slice_of(head_out)])
        memory_piece = slice_of(key_value)
        ffn_piece = jnp.concatenate([slice_of(ffn_in), slice_of(ffn_out)])
        biases = gather_line(
            jnp.concatenate([self_qv_bias.reshape(-1), cross_qv_bias.reshape(-1), ffn_in_bias])
        )
        first_whole = gather_plane(gather_line(first_piece), place)
        split = head_in.shape[0] // SUB
        head_in_all = first_whole[:, :, :split].reshape(mp, 4 * local, width)
        head_out_all = first_whole[:, :, split:].reshape(mp, 2 * local, width)
        self_bias = biases[:, : 2 * local].reshape(mp, 2, local)
        cross_bias = biases[:, 2 * local : 4 * local].reshape(mp, 2, local)
        inner_bias = biases[:, 4 * local :]

        memory_t = memory.T
        columns = []
        for step in range(mp):
            to = (line + step) % mp
            block = lax.dynamic_slice_in_dim(memory_t, to * mem_slots, mem_slots, 1)
            columns.append(shift(block, step) if step else block)
        memory_row = jnp.zeros((mp, local, mem_slots), BF16)
        for step in range(mp):
            memory_row = lax.dynamic_update_slice(
                memory_row, columns[step][None], (from_line[step], 0, 0)
            )
        memory_row = memory_row.reshape(width, mem_slots)
        key_value_all = gather_plane(gather_line(memory_piece), place).reshape(
            mp, 2 * local, width
        )
        ffn_whole = gather_plane(gather_line(ffn_piece), place)
        split = width // SUB
        ffn_in_all = ffn_whole[:, :, :split].reshape(mp, width, inner)
        ffn_out_all = ffn_whole[:, :, split:].reshape(mp, inner, width)

        dec_segment = segment_ids(row_of(dec_starts, 1)[0], slots)
        mem_segment = segment_ids(row_of(mem_starts, 1)[0], mem_slots)
        dec_places = jnp.arange(slots, dtype=jnp.int32)
        mem_places = jnp.arange(mem_slots, dtype=jnp.int32)
        self_allowed = (
            (dec_segment[:, None] == dec_segment[None, :])
            & (dec_places[None, :] <= dec_places[:, None])
            & (dec_places[None, :] < row_of(dec_length, 1))
        )
        cross_allowed = (dec_segment[:, None] == mem_segment[None, :]) & (
            mem_places[None, :] < row_of(mem_length, 1)
        )

        def to_heads(values):
            values = values.reshape(mp, slots, heads, HD)
            return jnp.swapaxes(values, 1, 2).reshape(mp * heads, slots, HD)

        def from_heads(values):
            values = values.reshape(mp, heads, slots, HD)
            return jnp.swapaxes(values, 1, 2).reshape(mp, slots, local)

        def to_heads_t(values):
            return values.reshape(mp * heads, HD, values.shape[-1])

        hidden_row = row_of(hidden, slots)
        grad_row = row_of(out_grad, slots)
        self_q = to_heads(
            (
                (ein("td,znd->ztn", hidden_row, head_in_all[:, :local]) + self_bias[:, None, 0])
                * scaling
            ).astype(BF16)
        )
        self_k = to_heads_t(
            ein("znd,td->znt", head_in_all[:, local : 2 * local], hidden_row).astype(BF16)
        )
        self_v = to_heads_t(
            (
                ein("znd,td->znt", head_in_all[:, 2 * local : 3 * local], hidden_row)
                + self_bias[:, 1, :, None]
            ).astype(BF16)
        )
        self_out, self_probs = attend(self_q, self_k, self_v, self_allowed)
        self_low = from_heads(self_out.astype(BF16))
        first, first_back = jax.vjp(
            layer_norm,
            hidden_row.astype(F32)
            + ein("ztn,znd->td", self_low, head_out_all[:, :local])
            + out_biases[0],
            norm_gains[0],
            norm_biases[0],
        )
        first_low = first.astype(BF16)
        cross_q = to_heads(
            (
                (ein("td,znd->ztn", first_low, head_in_all[:, 3 * local :]) + cross_bias[:, None, 0])
                * scaling
            ).astype(BF16)
        )
        memory_kv = ein("znd,ds->zns", key_value_all, memory_row)
        cross_k = to_heads_t(memory_kv[:, :local].astype(BF16))
        cross_v = to_heads_t((memory_kv[:, local:] + cross_bias[:, 1, :, None]).astype(BF16))
        cross_out, cross_probs = attend(cross_q, cross_k, cross_v, cross_allowed)
        cross_low = from_heads(cross_out.astype(BF16))
        second, second_back = jax.vjp(
            layer_norm,
            first + ein("ztn,znd->td", cross_low, head_out_all[:, local:]) + out_biases[1],
            norm_gains[1],
            norm_biases[1],
        )
        second_low = second.astype(BF16)
        hidden_pre = ein("td,zdn->ztn", second_low, ffn_in_all) + inner_bias[:, None]
        activated, gelu_back = jax.vjp(exact_gelu, hidden_pre)
        activated_low = activated.astype(BF16)
        final_norm, third_back = jax.vjp(
            layer_norm,
            second + ein("ztn,znd->td", activated_low, ffn_out_all) + out_biases[2],
            norm_gains[2],
            norm_biases[2],
        )
        result = gather_line(final_norm.astype(BF16))

        third_grad, gain_three, shift_three = third_back(grad_row.astype(F32))
        third_low = third_grad.astype(BF16)
        (pre_grad,) = gelu_back(ein("td,znd->ztn", third_low, ffn_out_all))
        pre_low = pre_grad.astype(BF16)
        ffn_parts = jnp.concatenate(
            [
                ein("td,ztn->zdn", second_low, pre_low).reshape(mp, SUB, -1, inner),
                ein("ztn,td->znd", activated_low, third_low).reshape(mp, SUB, -1, width),
            ],
            axis=2,
        )
        ffn_grads = reduce_group(ffn_parts, place)
        second_grad = third_grad + ein("ztn,zdn->td", pre_low, ffn_in_all)
        cross_grad, gain_two, shift_two = second_back(second_grad)
        cross_grad_low = cross_grad.astype(BF16)
        cross_out_grad = to_heads(
            ein("td,znd->ztn", cross_grad_low, head_out_all[:, local:]).astype(BF16)
        )
        cq_grad, ck_grad, cv_grad = attend_back(
            cross_q, cross_k, cross_v, cross_probs, cross_out_grad
        )
        cq_grad = from_heads(cq_grad) * scaling
        cq_low = cq_grad.astype(BF16)
        ck_grad = ck_grad.reshape(mp, local, mem_slots)
        cv_grad = cv_grad.reshape(mp, local, mem_slots)
        kv_low = jnp.concatenate([ck_grad, cv_grad], axis=1).astype(BF16)
        memory_grad_t = ein("znd,zns->ds", key_value_all, kv_low).astype(BF16)
        memory_blocks = memory_grad_t.reshape(mp, local, mem_slots)
        memory_out = jnp.zeros((local, mp, mem_slots), BF16)
        for step in range(mp):
            to = (line + step) % mp
            block = lax.dynamic_index_in_dim(memory_blocks, to, 0, keepdims=False)
            block = shift(block, step) if step else block
            memory_out = lax.dynamic_update_slice(
                memory_out, block[:, None], (0, from_line[step], 0)
            )
        memory_grad = memory_out.astype(F32).reshape(local, mp * mem_slots).T
        kv_parts = ein("zns,ds->znd", kv_low, memory_row).reshape(mp, SUB, -1, width)
        kv_grads = reduce_group(kv_parts, place)

        first_grad = cross_grad + ein("ztn,znd->td", cq_low, head_in_all[:, 3 * local :])
        self_grad, gain_one, shift_one = first_back(first_grad)
        self_grad_low = self_grad.astype(BF16)
        self_out_grad = to_heads(
            ein("td,znd->ztn", self_grad_low, head_out_all[:, :local]).astype(BF16)
        )
        sq_grad, sk_grad, sv_grad = attend_back(self_q, self_k, self_v, self_probs, self_out_grad)
        sq_grad = from_heads(sq_grad) * scaling
        sk_grad = jnp.swapaxes(sk_grad.reshape(mp, local, slots), 1, 2)
        sv_grad = jnp.swapaxes(sv_grad.reshape(mp, local, slots), 1, 2)
        qkv_low = jnp.concatenate([sq_grad, sk_grad, sv_grad], axis=2).astype(BF16)
        hidden_grad_row = self_grad + ein("ztn,znd->td", qkv_low, head_in_all[:, : 3 * local])
        hidden_grad = gather_line(hidden_grad_row.astype(BF16))
        head_in_parts = jnp.concatenate(
            [ein("ztn,td->znd", qkv_low, hidden_row), ein("ztn,td->znd", cq_low, first_low)], axis=1
        ).reshape(mp, SUB, -1, width)
        head_out_parts = jnp.concatenate(
            [
                ein("ztn,td->znd", self_low, self_grad_low),
                ein("ztn,td->znd", cross_low, cross_grad_low),
            ],
            axis=1,
        ).reshape(mp, SUB, -1, width)
        head_grads = reduce_group(jnp.concatenate([head_in_parts, head_out_parts], axis=2), place)

        def absolute(values):
            return jnp.take(values, from_line, axis=0)

        small = jnp.concatenate(
            [
                jnp.stack(
                    [
                        jnp.sum(self_grad, 0),
                        jnp.sum(cross_grad, 0),
                        jnp.sum(third_grad, 0),
                        gain_one,
                        gain_two,
                        gain_three,
                        shift_one,
                        shift_two,
                        shift_three,
                    ]
                ).reshape(-1),
                absolute(
                    jnp.concatenate(
                        [
                            jnp.sum(sq_grad, 1),
                            jnp.sum(sv_grad, 1),
                            jnp.sum(cq_grad, 1),
                            jnp.sum(cv_grad, 2),
                            jnp.sum(pre_grad, 1),
                        ],
                        axis=1,
                    )
                ).reshape(-1),
            ]
        )
        small = sum_everywhere(small)
        rows = small[: 9 * width].reshape(3, 3, width)
        sharded = lax.dynamic_index_in_dim(
            small[9 * width :].reshape(mp, 4 * local + inner), line, 0, keepdims=False
        )

        def in_order(gathered):
            return jnp.take(gathered, from_line, axis=0).reshape(mp * slots, width)

        split = 4 * local // SUB
        head_in_grad = head_grads[:, :split].reshape(4, local, width)
        head_out_grad = head_grads[:, split:].reshape(2, local, width)
        ffn_in_grad = ffn_grads[:, : width // SUB].reshape(width, inner)
        ffn_out_grad = ffn_grads[:, width // SUB :].reshape(inner, width)
        return (
            in_order(result),
            in_order(hidden_grad).astype(F32),
            memory_grad,
            jnp.swapaxes(head_in_grad[:3], 1, 2),
            sharded[: 2 * local].reshape(2, local),
            head_out_grad[0],
            head_in_grad[3].T,
            jnp.swapaxes(kv_grads.reshape(2, local, width), 1, 2),
            sharded[2 * local : 4 * local].reshape(2, local),
            head_out_grad[1],
            ffn_in_grad,
            sharded[4 * local :],
            ffn_out_grad,
            rows[0],
            rows[1],
            rows[2],
        )

    return jax.shard_map(
        body,
        mesh=mesh,
        in_specs=(
            P("dp", None),
            P("dp", "mp"),
            P("dp", None),
            P("dp", None),
            P("dp"),
            P("dp", None),
            P("dp"),
            P(None, None, "mp"),
            P(None, "mp"),
            P("mp", None),
            P(None, "mp"),
            P(None, None, "mp"),
            P(None, "mp"),
            P("mp", None),
            P(None, "mp"),
            P("mp"),
            P("mp", None),
            P(),
            P(),
            P(),
        ),
        out_specs=(
            P("dp", None),
            P("dp", None),
            P("dp", "mp"),
            P(None, None, "mp"),
            P(None, "mp"),
            P("mp", None),
            P(None, "mp"),
            P(None, None, "mp"),
            P(None, "mp"),
            P("mp", None),
            P(None, "mp"),
            P("mp"),
            P("mp", None),
            P(),
            P(),
            P(),
        ),
        check_vma=False,
    )
```

```python
import jax
import jax.numpy as jnp
from jax import lax
from jax.experimental import pallas as pl
from jax.experimental.pallas import tpu as pltpu
from jax.sharding import PartitionSpec as P

HD = 64
SUB = 8
NEG_FILL = -1000000000.0
EPSILON = 1e-05
F32 = jnp.float32
BF16 = jnp.bfloat16
VMEM = pltpu.VMEM
ROOT_HALF = 0.7071067811865476
ROOT_TWO_PI = 0.3989422804014327
SLOTS = ((3, 0), (1, 0), (3, 1), (2, 1), (1, 1), (2, 0), (0, 0), (0, 1))


def nn(left, right):
    return lax.dot_general(left, right, (((1,), (0,)), ((), ())), preferred_element_type=F32)


def nt(left, right):
    return lax.dot_general(left, right, (((1,), (1,)), ((), ())), preferred_element_type=F32)


def tn(left, right):
    return lax.dot_general(left, right, (((0,), (0,)), ((), ())), preferred_element_type=F32)


def normed(values):
    average = jnp.mean(values, -1, keepdims=True)
    centered = values - average
    variance = jnp.mean(centered * centered, -1, keepdims=True)
    inverse = lax.rsqrt(variance + EPSILON)
    return centered * inverse, inverse


def norm_back(unit, inverse, gain, grad):
    scaled = grad * gain
    return (
        scaled
        - jnp.mean(scaled, -1, keepdims=True)
        - unit * jnp.mean(scaled * unit, -1, keepdims=True)
    ) * inverse


def row_sum(values):
    return jnp.sum(values, 0, keepdims=True)


def segments(meta, start, count, shape, axis):
    places = lax.broadcasted_iota(jnp.int32, shape, axis)
    found = jnp.zeros(shape, jnp.int32) - 1
    for j in range(count):
        found = found + (meta[start + j] <= places).astype(jnp.int32)
    return found, places


def fetch(pieces, place, target, low, high, sem):
    size = high - low
    half = pieces[0].shape[1] // 2
    blocks = pieces[0].shape[0]
    part = low // half
    for beside in (0, 1):
        whole = pieces[5 * beside : 5 * beside + 3]
        split = pieces[5 * beside + 3 : 5 * beside + 5]
        for offset in range(4):
            row = pl.multiple_of((place ^ (offset + 4 * beside)) * size, 16)
            for block in range(blocks):
                if offset < 3:
                    source = whole[offset].at[block, pl.ds(low, size)]
                else:
                    at = 2 * block + part
                    source = split[at // blocks].at[at % blocks, pl.ds(low - half * part, size)]
                pltpu.make_async_copy(source, target.at[block + 1, pl.ds(row, size)], sem).start()


def fetch_own(source, target, low, sem):
    size = source.shape[0]
    pltpu.make_async_copy(source, target.at[0, pl.ds(low, size)], sem).start()


def arrive(target, sem):
    pltpu.make_async_copy(target, target, sem).wait()


def fetch_memory(blocks, line, target, sem):
    count = len(blocks)
    for step, block in enumerate(blocks):
        size = block.shape[0]
        row = pl.multiple_of(lax.rem(line + count - step, count) * size, 16)
        pltpu.make_async_copy(block, target.at[pl.ds(row, size)], sem).start()


def slot_of(offset, half):
    first = SLOTS.index((offset, 0))
    second = SLOTS.index((offset, 1))
    return jnp.where(half == 0, first, second)


def self_forward(dims, meta, x_ref, sb, cb, ob, gain, bias, *refs):
    mp, local, heads, scaling, nseg = dims
    pieces, (own_self, own_cq, own_sp, own_cp) = refs[:10], refs[10:14]
    qkv, low, z1, first, cq = refs[14:19]
    wa, wp, acc, sems = refs[19:]
    place = meta[0]
    fetch(pieces, place, wa, 0, 96, sems.at[0])
    fetch_own(own_self, wa, 0, sems.at[0])
    fetch_own(own_cq, wa, 3 * local, sems.at[0])
    fetch(pieces, place, wp, 96, 144, sems.at[1])
    fetch_own(own_sp, wp, 0, sems.at[1])
    fetch_own(own_cp, wp, local, sems.at[1])
    slots = x_ref.shape[0]
    shape = (slots, slots)
    query_segment, query_place = segments(meta, 4, nseg, shape, 0)
    key_segment, key_place = segments(meta, 4, nseg, shape, 1)
    allowed = (
        (query_segment == key_segment) & (key_place <= query_place) & (key_place < meta[2])
    )
    acc[...] = x_ref[...].astype(F32) + ob[0:1]
    arrive(wa, sems.at[0])
    arrive(wp, sems.at[1])

    def step(z, carry):
        flat = nt(x_ref[...], wa[z, : 3 * local])
        rows = sb[z]
        qkv[z, :, :local] = ((flat[:, :local] + rows[0:1]) * scaling).astype(BF16)
        qkv[z, :, local : 2 * local] = flat[:, local : 2 * local].astype(BF16)
        qkv[z, :, 2 * local :] = (flat[:, 2 * local :] + rows[1:2]).astype(BF16)
        for i in range(heads):
            at = HD * i
            scores = nt(
                qkv[z, :, at : at + HD], qkv[z, :, local + at : local + at + HD]
            )
            scores = jnp.where(allowed, scores, NEG_FILL)
            weights = jnp.exp(scores - jnp.max(scores, -1, keepdims=True))
            probs = (weights / jnp.sum(weights, -1, keepdims=True)).astype(BF16)
            out = nn(probs, qkv[z, :, 2 * local + at : 2 * local + at + HD])
            low[z, :, at : at + HD] = out.astype(BF16)
        acc[...] += nn(low[z], wp[z, :local])
        return carry

    lax.fori_loop(0, mp, step, 0)
    z1[...] = acc[...]
    unit, _ = normed(acc[...])
    values = unit * gain[0:1] + bias[0:1]
    first[...] = values
    values = values.astype(BF16)

    def query(z, carry):
        rows = cb[z]
        cq[z] = ((nt(values, wa[z, 3 * local :]) + rows[0:1]) * scaling).astype(BF16)
        return carry

    lax.fori_loop(0, mp, query, 0)


def cross_mask(meta, nseg, slots, mem_slots):
    query_segment, _ = segments(meta, 4, nseg, (slots, 1), 0)
    key_segment, key_place = segments(meta, 4 + nseg, nseg, (1, mem_slots), 1)
    key_segment = jnp.where(key_place < meta[3], key_segment, -1)
    return query_segment == key_segment


def cross_forward(dims, meta, cq, cb, ob, gain, bias, first, *refs):
    mp, local, heads, scaling, nseg = dims
    blocks, pieces, (own_kv, own_sp, own_cp) = refs[:mp], refs[mp : mp + 10], refs[mp + 10 : mp + 13]
    kv, low, total, z2, second = refs[mp + 13 : mp + 18]
    wk, wp, mem, acc, sems = refs[mp + 18 :]
    place = meta[0]
    fetch_memory(blocks, meta[1], mem, sems.at[2])
    fetch(pieces, place, wk, 144, 192, sems.at[0])
    fetch_own(own_kv, wk, 0, sems.at[0])
    fetch(pieces, place, wp, 96, 144, sems.at[1])
    fetch_own(own_sp, wp, 0, sems.at[1])
    fetch_own(own_cp, wp, local, sems.at[1])
    allowed = cross_mask(meta, nseg, first.shape[0], mem.shape[1])
    acc[...] = first[...] + ob[1:2]
    arrive(wk, sems.at[0])
    arrive(mem, sems.at[2])
    arrive(wp, sems.at[1])

    def step(z, carry):
        flat = nn(wk[z], mem[...])
        column = jnp.swapaxes(jnp.broadcast_to(cb[z][1:2], (8, local)), 0, 1)[:, :1]
        kv[z, :local] = flat[:local].astype(BF16)
        kv[z, local:] = (flat[local:] + column).astype(BF16)
        for i in range(heads):
            at = HD * i
            scores = nn(cq[z, :, at : at + HD], kv[z, at : at + HD])
            scores = jnp.where(allowed, scores, NEG_FILL)
            peak = jnp.max(scores, -1, keepdims=True)
            weights = jnp.exp(scores - peak)
            mass = jnp.sum(weights, -1, keepdims=True)
            probs = (weights / mass).astype(BF16)
            low[z, :, at : at + HD] = nt(probs, kv[z, local + at : local + at + HD]).astype(BF16)
            total[z * heads + i] = peak + jnp.log(mass)
        acc[...] += nn(low[z], wp[z, local:])
        return carry

    lax.fori_loop(0, mp, step, 0)
    z2[...] = acc[...]
    unit, _ = normed(acc[...])
    second[...] = unit * gain[1:2] + bias[1:2]


def put_slots(beside, mine, place, z, base, size, source):
    half = lax.div(z, 2)
    at = lax.rem(z, 2)
    for offset in range(4):
        slot = slot_of(offset, half)
        for target, flip in ((mine, 0), (beside, 4)):
            row = pl.multiple_of((place ^ (offset + flip)) * size, 16)
            target[slot, at, base : base + size] = source[pl.ds(row, size)].astype(BF16)


def ffn_both(dims, meta, second, z2, grad, ib, ob, gain, bias, *refs):
    mp, local, heads, scaling, nseg = dims
    pieces, (own_in, own_out) = refs[:10], refs[10:12]
    result, dz2, sums, beside, mine = refs[12:17]
    win, wout, acc, act, slope, dw, sems = refs[17:]
    place = meta[0]
    fetch(pieces, place, win, 0, 96, sems.at[0])
    fetch_own(own_in, win, 0, sems.at[0])
    fetch(pieces, place, wout, 96, 192, sems.at[1])
    fetch_own(own_out, wout, 0, sems.at[1])
    acc[...] = second[...] + ob[2:3]
    second_low = second[...].astype(BF16)
    arrive(win, sems.at[0])
    arrive(wout, sems.at[1])

    def forward(z, carry):
        inner = nn(second_low, win[z]) + ib[z]
        share = 0.5 * (1.0 + lax.erf(inner * ROOT_HALF))
        act[z] = (inner * share).astype(BF16)
        slope[z] = share + inner * (ROOT_TWO_PI * jnp.exp(-0.5 * inner * inner))
        acc[...] += nn(act[z], wout[z])
        return carry

    lax.fori_loop(0, mp, forward, 0)
    unit, inverse = normed(acc[...])
    result[...] = (unit * gain[2:3] + bias[2:3]).astype(BF16)
    out_grad = grad[...].astype(F32)
    third = norm_back(unit, inverse, gain[2:3], out_grad)
    sums[...] = jnp.zeros_like(sums)
    sums[0:1] = row_sum(third)
    sums[1:2] = row_sum(out_grad * unit)
    sums[2:3] = row_sum(out_grad)
    third_low = third.astype(BF16)
    acc[...] = third

    def backward(z, carry):
        inner = nt(third_low, wout[z]) * slope[z]
        sums[pl.ds(8 + z, 1)] = row_sum(inner)
        inner_low = inner.astype(BF16)
        acc[...] += nt(inner_low, win[z])
        dw[...] = tn(second_low, inner_low)
        put_slots(beside, mine, place, z, 0, 96, dw)
        dw[...] = tn(act[z], third_low)
        put_slots(beside, mine, place, z, 96, 96, dw)
        return carry

    lax.fori_loop(0, mp, backward, 0)
    unit, inverse = normed(z2[...])
    grad_rows = acc[...]
    values = norm_back(unit, inverse, gain[1:2], grad_rows)
    dz2[...] = values
    sums[3:4] = row_sum(values)
    sums[4:5] = row_sum(grad_rows * unit)
    sums[5:6] = row_sum(grad_rows)


def cross_back(dims, meta, dz2, cq, total, z1, gain, *refs):
    mp, local, heads, scaling, nseg = dims
    kv_ref, pieces, owns = refs[0], refs[1:11], refs[11:16]
    own_self, own_cq, own_kv, own_sp, own_cp = owns
    mem_out, kv_low, dcq, dz1, sums, sums_local = refs[16:22]
    wa, wk, wp, kv, dmem, acc, dout, sems = refs[22:]
    place = meta[0]
    pltpu.make_async_copy(kv_ref, kv, sems.at[3]).start()
    fetch(pieces, place, wp, 96, 144, sems.at[1])
    fetch_own(own_sp, wp, 0, sems.at[1])
    fetch_own(own_cp, wp, local, sems.at[1])
    fetch(pieces, place, wk, 144, 192, sems.at[0])
    fetch_own(own_kv, wk, 0, sems.at[0])
    fetch(pieces, place, wa, 0, 96, sems.at[2])
    fetch_own(own_self, wa, 0, sems.at[2])
    fetch_own(own_cq, wa, 3 * local, sems.at[2])
    allowed = cross_mask(meta, nseg, dz2.shape[0], kv.shape[2])
    dz2_low = dz2[...].astype(BF16)
    acc[...] = dz2[...]
    dmem[...] = jnp.zeros_like(dmem)
    arrive(kv, sems.at[3])
    arrive(wp, sems.at[1])
    arrive(wk, sems.at[0])
    arrive(wa, sems.at[2])

    def step(z, carry):
        dout[...] = nt(dz2_low, wp[z, local:]).astype(BF16)
        for i in range(heads):
            at = HD * i
            query = cq[z, :, at : at + HD]
            key = kv[z, at : at + HD]
            value = kv[z, local + at : local + at + HD]
            grad = dout[:, at : at + HD]
            scores = jnp.where(allowed, nn(query, key), NEG_FILL)
            probs = jnp.exp(scores - total[z * heads + i])
            probs_low = probs.astype(BF16)
            prob_grad = nn(grad, value)
            offset = jnp.sum(probs * prob_grad, -1, keepdims=True)
            score_grad = (probs * (prob_grad - offset)).astype(BF16)
            kv_low[z, at : at + HD] = tn(query, score_grad).astype(BF16)
            kv_low[z, local + at : local + at + HD] = tn(grad, probs_low).astype(BF16)
            mass = jnp.sum(probs_low.astype(F32), -1, keepdims=True)
            query_grad = nt(score_grad, key) * scaling
            dcq[z, :, at : at + HD] = query_grad.astype(BF16)
            sums_local[z, 0:1, at : at + HD] = row_sum(query_grad)
            sums_local[z, 1:2, at : at + HD] = row_sum(mass * grad.astype(F32))
        acc[...] += nn(dcq[z], wa[z, 3 * local :])
        dmem[...] += tn(wk[z], kv_low[z])
        return carry

    lax.fori_loop(0, mp, step, 0)
    for block in range(mp):
        row = pl.multiple_of(lax.rem(meta[1] + block, mp) * local, 16)
        mem_out[block] = dmem[pl.ds(row, local)].astype(BF16)
    unit, inverse = normed(z1[...])
    grad_rows = acc[...]
    values = norm_back(unit, inverse, gain[0:1], grad_rows)
    dz1[...] = values
    sums[...] = jnp.zeros_like(sums)
    sums[0:1] = row_sum(values)
    sums[1:2] = row_sum(grad_rows * unit)
    sums[2:3] = row_sum(grad_rows)


def self_back(dims, meta, dz1, dz2, x_ref, first, qkv, self_low, cross_low, dcq, *refs):
    mp, local, heads, scaling, nseg = dims
    kv_ref, blocks, pieces, owns = refs[0], refs[1 : 1 + mp], refs[1 + mp : 11 + mp], refs[11 + mp : 15 + mp]
    own_self, own_cq, own_sp, own_cp = owns
    dx, sums_local, beside, mine = refs[15 + mp : 19 + mp]
    wa, wp, kv, mem, acc, dout, dqkv, dwa, dwp, sems = refs[19 + mp :]
    place = meta[0]
    fetch(pieces, place, wp, 96, 144, sems.at[1])
    fetch_own(own_sp, wp, 0, sems.at[1])
    fetch_own(own_cp, wp, local, sems.at[1])
    fetch(pieces, place, wa, 0, 96, sems.at[0])
    fetch_own(own_self, wa, 0, sems.at[0])
    fetch_own(own_cq, wa, 3 * local, sems.at[0])
    pltpu.make_async_copy(kv_ref, kv, sems.at[2]).start()
    fetch_memory(blocks, meta[1], mem, sems.at[3])
    slots = x_ref.shape[0]
    shape = (slots, slots)
    query_segment, query_place = segments(meta, 4, nseg, shape, 0)
    key_segment, key_place = segments(meta, 4, nseg, shape, 1)
    allowed = (
        (query_segment == key_segment) & (key_place <= query_place) & (key_place < meta[2])
    )
    dz1_low = dz1[...].astype(BF16)
    dz2_low = dz2[...].astype(BF16)
    first_low = first[...].astype(BF16)
    acc[...] = dz1[...]
    arrive(wp, sems.at[1])
    arrive(wa, sems.at[0])
    arrive(kv, sems.at[2])
    arrive(mem, sems.at[3])

    def step(z, carry):
        dout[...] = nt(dz1_low, wp[z, :local]).astype(BF16)
        for i in range(heads):
            at = HD * i
            query = qkv[z, :, at : at + HD]
            key = qkv[z, :, local + at : local + at + HD]
            value = qkv[z, :, 2 * local + at : 2 * local + at + HD]
            grad = dout[:, at : at + HD]
            scores = jnp.where(allowed, nt(query, key), NEG_FILL)
            weights = jnp.exp(scores - jnp.max(scores, -1, keepdims=True))
            probs = weights / jnp.sum(weights, -1, keepdims=True)
            prob_grad = nt(grad, value)
            offset = jnp.sum(probs * prob_grad, -1, keepdims=True)
            score_grad = (probs * (prob_grad - offset)).astype(BF16)
            value_grad = tn(probs.astype(BF16), grad)
            query_grad = nn(score_grad, key) * scaling
            dqkv[:, at : at + HD] = query_grad.astype(BF16)
            dqkv[:, local + at : local + at + HD] = tn(score_grad, query).astype(BF16)
            dqkv[:, 2 * local + at : 2 * local + at + HD] = value_grad.astype(BF16)
            sums_local[z, 0:1, at : at + HD] = row_sum(query_grad)
            sums_local[z, 1:2, at : at + HD] = row_sum(value_grad)
        acc[...] += nn(dqkv[...], wa[z, : 3 * local])
        dwa[: 3 * local] = tn(dqkv[...], x_ref[...])
        dwa[3 * local :] = tn(dcq[z], first_low)
        put_slots(beside, mine, place, z, 0, 96, dwa)
        dwp[:local] = tn(self_low[z], dz1_low)
        dwp[local:] = tn(cross_low[z], dz2_low)
        put_slots(beside, mine, place, z, 96, 48, dwp)
        dwp[...] = nt(kv[z], mem[...])
        put_slots(beside, mine, place, z, 144, 48, dwp)
        return carry

    lax.fori_loop(0, mp, step, 0)
    dx[...] = acc[...]


def place_rows(place, ranges, low, over_two, over_four, near, far, across):
    half = near.shape[0]
    rows = low.shape[0]
    for offset in range(8):
        position = place ^ offset
        for start, size, targets in ranges:
            if offset >= 4:
                source = across[pl.ds((offset - 4) * rows + start, size)]
            elif offset == 3:
                source = (near if start < half else far)[pl.ds(start % half, size)]
            else:
                source = (low, over_two, over_four)[offset][pl.ds(start, size)]
            source = source.astype(F32)
            first = 0
            for target in targets:
                count = target.shape[0] // size

                @pl.when((position >= first) & (position < first + count))
                def _():
                    row = pl.multiple_of((position - first) * size, 8)
                    target[pl.ds(row, size)] = source

                first += count


def finish_heads(meta, low, over_two, over_four, near, far, across, gs, gq, gp, gc, gk):
    ranges = ((0, 96, (gs, gq)), (96, 48, (gp, gc)), (144, 48, (gk,)))
    place_rows(meta[0], ranges, low, over_two, over_four, near, far, across)


def finish_ffn(meta, low, over_two, over_four, near, far, across, gi, go):
    ranges = ((0, 96, (gi,)), (96, 96, (go,)))
    place_rows(meta[0], ranges, low, over_two, over_four, near, far, across)


def shaped(shape, dtype=F32):
    return jax.ShapeDtypeStruct(shape, dtype)


def in_vmem(count):
    return [pl.BlockSpec(memory_space=pltpu.VMEM)] * count


def in_place(count):
    return [pl.BlockSpec(memory_space=pl.ANY)] * count


META = pl.BlockSpec(memory_space=pltpu.SMEM)


def call(kernel, in_specs, outs, scratch, flops, moved, name):
    return pl.pallas_call(
        kernel,
        out_shape=outs,
        in_specs=in_specs,
        out_specs=in_vmem(len(outs)),
        scratch_shapes=scratch,
        name=name,
        compiler_params=pltpu.CompilerParams(vmem_limit_bytes=60 * 1024 * 1024),
        cost_estimate=pl.CostEstimate(flops=flops, bytes_accessed=moved, transcendentals=0),
    )


def solution(mesh):
    dp = mesh.shape["dp"]
    mp = mesh.shape["mp"]

    def swap(value, bit):
        return lax.ppermute(value, "dp", [(i, i ^ bit) for i in range(dp)])

    def shift(value, step):
        return lax.ppermute(value, "mp", [(i, (i + step) % mp) for i in range(mp)])

    def after(value, *others):
        return lax.optimization_barrier((value,) + others)[0]

    def gather_plane(own):
        blocks, rows, width = own.shape
        over_two = swap(own, 2)
        over_four = swap(own, 4)
        halves = (2 * blocks, rows // 2, width)
        near = swap(over_four.reshape(halves)[:blocks], 2)
        far = swap(over_two.reshape(halves)[blocks:], 4)
        mine = (own, over_two, over_four, near, far)
        return mine + tuple(swap(piece, 1) for piece in mine)

    def reduce_group(beside, mine):
        total = mine.astype(F32) + swap(beside, 1).astype(F32)
        low = total[:6].astype(BF16)
        from_two = swap(low[0:2], 2).astype(F32)
        from_four = swap(low[2:4], 4).astype(F32)
        late_four = swap((low[5].astype(F32) + from_two[0]).astype(BF16), 4)
        late_two = swap((low[4].astype(F32) + from_four[0]).astype(BF16), 2)
        top = total[6] + from_two[1] + late_four.astype(F32)
        end = total[7] + from_four[1] + late_two.astype(F32)
        bit = SUB
        while bit < dp:
            top = top + swap(top, bit)
            end = end + swap(end, bit)
            bit *= 2
        blocks = [top[0], top[1], end[0], end[1]]
        total = blocks[0]
        for step in range(1, mp):
            total = total + shift(blocks[step].astype(BF16), -step).astype(F32)
        low = total.astype(BF16)
        half = low.shape[0] // 2
        over_two = swap(low, 2)
        over_four = swap(low, 4)
        near = swap(over_four[:half], 2)
        far = swap(over_two[half:], 4)
        across = swap(jnp.concatenate([low, over_two, over_four, near, far]), 1)
        return (low, over_two, over_four, near, far, across)

    def sum_everywhere(total):
        bit = 1
        while bit < dp:
            total = total + swap(total, bit)
            bit *= 2
        bit = 1
        while bit < mp:
            total = total + lax.ppermute(total, "mp", [(i, i ^ bit) for i in range(mp)])
            bit *= 2
        return total

    def body(
        hidden,
        memory,
        out_grad,
        dec_starts,
        dec_length,
        mem_starts,
        mem_length,
        self_qkv,
        self_qv_bias,
        self_proj,
        cross_query,
        cross_kv,
        cross_qv_bias,
        cross_proj,
        ffn_in,
        ffn_in_bias,
        ffn_out,
        out_biases,
        norm_gains,
        norm_biases,
    ):
        row_count = dec_starts.shape[0]
        assert row_count == mp == 4 and dp % SUB == 0
        slots = hidden.shape[0] // row_count
        mem_slots = memory.shape[0] // row_count
        width = hidden.shape[1]
        local = self_proj.shape[0]
        heads = local // HD
        inner = ffn_out.shape[0]
        nseg = dec_starts.shape[1]
        dims = (mp, local, heads, HD ** (-0.5), nseg)
        line = lax.axis_index("mp")
        device = lax.axis_index("dp") % SUB
        place = (device & 1) * 4 + device // 2

        def row_of(array, size):
            return lax.dynamic_slice_in_dim(array, line * size, size, 0)

        def slice_of(array):
            size = array.shape[0] // SUB
            return lax.dynamic_slice_in_dim(array, place * size, size, 0)

        meta = jnp.concatenate(
            [
                jnp.stack([place, line]).astype(jnp.int32),
                row_of(dec_length, 1),
                row_of(mem_length, 1),
                row_of(dec_starts, 1)[0],
                row_of(mem_starts, 1)[0],
            ]
        )
        own_self = jnp.swapaxes(self_qkv, 1, 2).reshape(3 * local, width)
        own_cq = cross_query.T
        own_kv = jnp.swapaxes(cross_kv, 1, 2).reshape(2 * local, width)

        head_piece = jnp.concatenate(
            [
                slice_of(jnp.concatenate([own_self, own_cq])),
                slice_of(jnp.concatenate([self_proj, cross_proj])),
                slice_of(own_kv),
            ]
        )
        ffn_piece = jnp.concatenate([slice_of(ffn_in), slice_of(ffn_out)])
        bias_piece = jnp.concatenate(
            [self_qv_bias.reshape(-1), cross_qv_bias.reshape(-1), ffn_in_bias]
        )
        head_line = jnp.stack([shift(head_piece, step) for step in range(1, mp)])
        biases = jnp.stack([bias_piece] + [shift(bias_piece, step) for step in range(1, mp)])
        head_pieces = gather_plane(head_line)
        ffn_piece = after(ffn_piece, head_line)
        ffn_line = jnp.stack([shift(ffn_piece, step) for step in range(1, mp)])
        ffn_pieces = gather_plane(ffn_line)
        memory_t = after(memory.T, ffn_line)
        memory_blocks = []
        for step in range(mp):
            to = (line + step) % mp
            block = lax.dynamic_slice_in_dim(memory_t, to * mem_slots, mem_slots, 1)
            memory_blocks.append(shift(block, step) if step else block)

        self_bias = biases[:, : 2 * local].reshape(mp, 2, local)
        cross_bias = biases[:, 2 * local : 4 * local].reshape(mp, 2, local)
        inner_bias = biases[:, None, 4 * local :]
        hidden_row = row_of(hidden, slots)
        grad_row = row_of(out_grad, slots)
        params = (out_biases, norm_gains, norm_biases)
        dma = pltpu.SemaphoreType.DMA((4,))
        wa_shape = VMEM((mp, 4 * local, width), BF16)
        wp_shape = VMEM((mp, 2 * local, width), BF16)
        flat_shape = VMEM((slots, width), F32)
        row_shape = shaped((slots, width))
        low_shape = shaped((mp, slots, local), BF16)
        matmul = 2 * slots * width * width

        def bound(kernel):
            return lambda *refs: kernel(dims, *refs)

        qkv, self_low, z1, first, cross_q = call(
            bound(self_forward),
            [META] + in_vmem(6) + in_place(14),
            (
                shaped((mp, slots, 3 * local), BF16),
                low_shape,
                row_shape,
                row_shape,
                low_shape,
            ),
            [wa_shape, wp_shape, flat_shape, dma],
            5 * matmul,
            8 * width * width * 2,
            "self_forward",
        )(
            meta,
            hidden_row,
            self_bias,
            cross_bias,
            *params,
            *head_pieces,
            own_self,
            own_cq,
            self_proj,
            cross_proj,
        )
        kv, cross_low, cross_total, z2, second = call(
            bound(cross_forward),
            [META] + in_vmem(6) + in_place(mp + 13),
            (
                shaped((mp, 2 * local, mem_slots), BF16),
                low_shape,
                shaped((mp * heads, slots, 1)),
                row_shape,
                row_shape,
            ),
            [wp_shape, wp_shape, VMEM((width, mem_slots), BF16), flat_shape, dma],
            18 * matmul,
            8 * width * width * 2,
            "cross_forward",
        )(
            meta,
            cross_q,
            cross_bias,
            *params,
            first,
            *memory_blocks,
            *head_pieces,
            own_kv,
            self_proj,
            cross_proj,
        )
        slot_shape = shaped((8, 2, 2 * width // SUB, width), BF16)
        square = VMEM((width, width), F32)
        result, dz2, ffn_sums, ffn_beside, ffn_mine = call(
            bound(ffn_both),
            [META] + in_vmem(7) + in_place(12),
            (
                shaped((slots, width), BF16),
                row_shape,
                shaped((16, width)),
                slot_shape,
                slot_shape,
            ),
            [
                VMEM((mp, width, inner), BF16),
                VMEM((mp, inner, width), BF16),
                flat_shape,
                VMEM((mp, slots, inner), BF16),
                VMEM((mp, slots, inner), F32),
                square,
                dma,
            ],
            24 * matmul,
            16 * width * width * 2,
            "ffn_both",
        )(meta, second, z2, grad_row, inner_bias, *params, *ffn_pieces, ffn_in, ffn_out)
        ffn_reduced = reduce_group(ffn_beside, ffn_mine)

        memory_grads, kv_low, cross_dq, dz1, cross_sums, cross_local = call(
            bound(cross_back),
            [META] + in_vmem(5) + in_place(16),
            (
                shaped((mp, local, mem_slots), BF16),
                shaped((mp, 2 * local, mem_slots), BF16),
                low_shape,
                row_shape,
                shaped((8, width)),
                shaped((mp, 2, local)),
            ),
            [
                wa_shape,
                wp_shape,
                wp_shape,
                VMEM((mp, 2 * local, mem_slots), BF16),
                VMEM((width, mem_slots), F32),
                flat_shape,
                VMEM((slots, local), BF16),
                dma,
            ],
            24 * matmul,
            12 * width * width * 2,
            "cross_back",
        )(
            meta,
            dz2,
            cross_q,
            cross_total,
            z1,
            norm_gains,
            kv,
            *head_pieces,
            own_self,
            own_cq,
            own_kv,
            self_proj,
            cross_proj,
        )
        memory_out = jnp.zeros((local, mp * mem_slots), F32)
        for step in range(mp):
            block = shift(memory_grads[step], step) if step else memory_grads[0]
            at = ((line - step) % mp) * mem_slots
            memory_out = lax.dynamic_update_slice(memory_out, block.astype(F32), (0, at))

        hidden_grad, self_local, head_beside, head_mine = call(
            bound(self_back),
            [META] + in_vmem(8) + in_place(mp + 15),
            (row_shape, shaped((mp, 2, local)), slot_shape, slot_shape),
            [
                wa_shape,
                wp_shape,
                VMEM((mp, 2 * local, mem_slots), BF16),
                VMEM((width, mem_slots), BF16),
                flat_shape,
                VMEM((slots, local), BF16),
                VMEM((slots, 3 * local), BF16),
                square,
                VMEM((2 * local, width), F32),
                dma,
            ],
            26 * matmul,
            16 * width * width * 2,
            "self_back",
        )(
            meta,
            dz1,
            dz2,
            hidden_row,
            first,
            qkv,
            self_low,
            cross_low,
            cross_dq,
            kv_low,
            *memory_blocks,
            *head_pieces,
            own_self,
            own_cq,
            self_proj,
            cross_proj,
        )
        head_reduced = reduce_group(head_beside, head_mine)

        def spread(rows):
            low = rows.astype(BF16)
            whole = jnp.zeros((mp * slots, width), BF16)
            for step in range(mp):
                piece = shift(low, step) if step else low
                at = ((line - step) % mp) * slots
                whole = lax.dynamic_update_slice(whole, piece, (at, 0))
            return whole

        from_line = (line - jnp.arange(mp)) % mp
        partial = jnp.concatenate(
            [
                self_local.reshape(mp, -1),
                cross_local.reshape(mp, -1),
                ffn_sums[8 : 8 + mp],
            ],
            axis=1,
        )
        small = sum_everywhere(
            jnp.concatenate(
                [cross_sums[:3], ffn_sums[:6], jnp.take(partial, from_line, axis=0).reshape(-1, width)]
            )
        )
        sharded = lax.dynamic_index_in_dim(
            small[9:].reshape(mp, 4 * local + inner), line, 0, keepdims=False
        )
        grad_self, grad_cq, grad_sp, grad_cp, grad_kv = call(
            finish_heads,
            [META] + in_vmem(6),
            (
                shaped((3 * local, width)),
                shaped((local, width)),
                shaped((local, width)),
                shaped((local, width)),
                shaped((2 * local, width)),
            ),
            [],
            0,
            12 * width * width,
            "finish_heads",
        )(meta, *head_reduced)
        grad_in, grad_out = call(
            finish_ffn,
            [META] + in_vmem(6),
            (shaped((width, inner)), shaped((inner, width))),
            [],
            0,
            12 * width * width,
            "finish_ffn",
        )(meta, *ffn_reduced)
        return (
            spread(result),
            spread(hidden_grad).astype(F32),
            memory_out.T,
            jnp.swapaxes(grad_self.reshape(3, local, width), 1, 2),
            sharded[: 2 * local].reshape(2, local),
            grad_sp,
            grad_cq.T,
            jnp.swapaxes(grad_kv.reshape(2, local, width), 1, 2),
            sharded[2 * local : 4 * local].reshape(2, local),
            grad_cp,
            grad_in,
            sharded[4 * local :],
            grad_out,
            jnp.stack([small[0], small[6], small[3]]),
            jnp.stack([small[1], small[7], small[4]]),
            jnp.stack([small[2], small[8], small[5]]),
        )

    return jax.shard_map(
        body,
        mesh=mesh,
        in_specs=(
            P("dp", None),
            P("dp", "mp"),
            P("dp", None),
            P("dp", None),
            P("dp"),
            P("dp", None),
            P("dp"),
            P(None, None, "mp"),
            P(None, "mp"),
            P("mp", None),
            P(None, "mp"),
            P(None, None, "mp"),
            P(None, "mp"),
            P("mp", None),
            P(None, "mp"),
            P("mp"),
            P("mp", None),
            P(),
            P(),
            P(),
        ),
        out_specs=(
            P("dp", None),
            P("dp", None),
            P("dp", "mp"),
            P(None, None, "mp"),
            P(None, "mp"),
            P("mp", None),
            P(None, "mp"),
            P(None, None, "mp"),
            P(None, "mp"),
            P("mp", None),
            P(None, "mp"),
            P("mp"),
            P("mp", None),
            P(),
            P(),
            P(),
        ),
        check_vma=False,
    )
```

```python
import jax
import jax.numpy as jnp
from jax import lax
from jax.experimental import pallas as pl
from jax.experimental.pallas import tpu as pltpu
from jax.sharding import PartitionSpec as P

HD = 64
SUB = 8
NEG_FILL = -1000000000.0
EPSILON = 1e-05
F32 = jnp.float32
BF16 = jnp.bfloat16
VMEM = pltpu.VMEM
ROOT_HALF = 0.7071067811865476
ROOT_TWO_PI = 0.3989422804014327
SLOTS = ((3, 0), (1, 0), (3, 1), (2, 1), (1, 1), (2, 0), (0, 0), (0, 1))


def nn(left, right):
    return lax.dot_general(left, right, (((1,), (0,)), ((), ())), preferred_element_type=F32)


def nt(left, right):
    return lax.dot_general(left, right, (((1,), (1,)), ((), ())), preferred_element_type=F32)


def tn(left, right):
    return lax.dot_general(left, right, (((0,), (0,)), ((), ())), preferred_element_type=F32)


def normed(values):
    average = jnp.mean(values, -1, keepdims=True)
    centered = values - average
    variance = jnp.mean(centered * centered, -1, keepdims=True)
    inverse = lax.rsqrt(variance + EPSILON)
    return centered * inverse, inverse


def norm_back(unit, inverse, gain, grad):
    scaled = grad * gain
    return (
        scaled
        - jnp.mean(scaled, -1, keepdims=True)
        - unit * jnp.mean(scaled * unit, -1, keepdims=True)
    ) * inverse


def row_sum(values):
    return jnp.sum(values, 0, keepdims=True)


def segments(meta, start, count, shape, axis):
    places = lax.broadcasted_iota(jnp.int32, shape, axis)
    found = jnp.zeros(shape, jnp.int32) - 1
    for j in range(count):
        found = found + (meta[start + j] <= places).astype(jnp.int32)
    return found, places


def fetch(pieces, place, target, low, high, sem):
    size = high - low
    blocks, rows = pieces[0].shape[:2]
    half = rows // 2
    for beside in (0, 1):
        whole = pieces[5 * beside : 5 * beside + 3]
        split = pieces[5 * beside + 3 : 5 * beside + 5]
        for offset in range(4):
            row = (place ^ (offset + 4 * beside)) * size
            for block in range(blocks):
                if offset < 3:
                    source = whole[offset].at[block, pl.ds(low, size)]
                    to = target.at[block + 1, pl.ds(pl.multiple_of(row, 16), size)]
                    pltpu.make_async_copy(source, to, sem).start()
                    continue
                for part in range(low // half, high // half):
                    at = 2 * block + part
                    source = split[at // blocks].at[at % blocks]
                    start = pl.multiple_of(row + part * half - low, 16)
                    to = target.at[block + 1, pl.ds(start, half)]
                    pltpu.make_async_copy(source, to, sem).start()


def fetch_own(source, target, low, sem):
    size = source.shape[0]
    pltpu.make_async_copy(source, target.at[0, pl.ds(low, size)], sem).start()


def arrive(target, sem):
    pltpu.make_async_copy(target, target, sem).wait()


def fetch_memory(blocks, line, target, sem):
    count = len(blocks)
    for step, block in enumerate(blocks):
        size = block.shape[0]
        row = pl.multiple_of(lax.rem(line + count - step, count) * size, 16)
        pltpu.make_async_copy(block, target.at[pl.ds(row, size)], sem).start()


def slot_of(offset, half):
    first = SLOTS.index((offset, 0))
    second = SLOTS.index((offset, 1))
    return jnp.where(half == 0, first, second)


def self_mask(meta, nseg, slots):
    shape = (slots, slots)
    query_segment, query_place = segments(meta, 4, nseg, shape, 0)
    key_segment, key_place = segments(meta, 4, nseg, shape, 1)
    return (query_segment == key_segment) & (key_place <= query_place) & (key_place < meta[2])


def self_forward(dims, meta, x_ref, sb, ob, gain, bias, *refs):
    mp, local, heads, scaling, nseg = dims
    pieces, (own_self, own_sp) = refs[:10], refs[10:12]
    qkv, low, z1, first = refs[12:16]
    ws, acc, sems = refs[16:]
    fetch(pieces, meta[0], ws, 0, 96, sems.at[0])
    fetch_own(own_self, ws, 0, sems.at[0])
    fetch_own(own_sp, ws, 3 * local, sems.at[0])
    allowed = self_mask(meta, nseg, x_ref.shape[0])
    acc[...] = x_ref[...].astype(F32) + ob[0:1]
    arrive(ws, sems.at[0])

    def step(z, carry):
        flat = nt(x_ref[...], ws[z, : 3 * local])
        rows = sb[z]
        qkv[z, :, :local] = ((flat[:, :local] + rows[0:1]) * scaling).astype(BF16)
        qkv[z, :, local : 2 * local] = flat[:, local : 2 * local].astype(BF16)
        qkv[z, :, 2 * local :] = (flat[:, 2 * local :] + rows[1:2]).astype(BF16)
        for i in range(heads):
            at = HD * i
            scores = nt(qkv[z, :, at : at + HD], qkv[z, :, local + at : local + at + HD])
            scores = jnp.where(allowed, scores, NEG_FILL)
            weights = jnp.exp(scores - jnp.max(scores, -1, keepdims=True))
            probs = (weights / jnp.sum(weights, -1, keepdims=True)).astype(BF16)
            out = nn(probs, qkv[z, :, 2 * local + at : 2 * local + at + HD])
            low[z, :, at : at + HD] = out.astype(BF16)
        acc[...] += nn(low[z], ws[z, 3 * local :])
        return carry

    lax.fori_loop(0, mp, step, 0)
    z1[...] = acc[...]
    unit, _ = normed(acc[...])
    first[...] = unit * gain[0:1] + bias[0:1]


def cross_mask(meta, nseg, slots, mem_slots):
    query_segment, _ = segments(meta, 4, nseg, (slots, 1), 0)
    key_segment, key_place = segments(meta, 4 + nseg, nseg, (1, mem_slots), 1)
    key_segment = jnp.where(key_place < meta[3], key_segment, -1)
    return query_segment == key_segment


def fetch_cross(pieces, owns, place, target, sem):
    fetch(pieces, place, target, 96, 192, sem)
    row = 0
    for own in owns:
        fetch_own(own, target, row, sem)
        row += own.shape[0]


def cross_forward(dims, meta, cb, ob, gain, bias, first, *refs):
    mp, local, heads, scaling, nseg = dims
    blocks, pieces, owns = refs[:mp], refs[mp : mp + 10], refs[mp + 10 : mp + 13]
    cq, kv, low, total, z2, second = refs[mp + 13 : mp + 19]
    wc, mem, acc, sems = refs[mp + 19 :]
    fetch_cross(pieces, owns, meta[0], wc, sems.at[0])
    fetch_memory(blocks, meta[1], mem, sems.at[1])
    allowed = cross_mask(meta, nseg, first.shape[0], mem.shape[1])
    acc[...] = first[...] + ob[1:2]
    first_low = first[...].astype(BF16)
    arrive(wc, sems.at[0])
    arrive(mem, sems.at[1])

    def step(z, carry):
        rows = cb[z]
        cq[z] = ((nt(first_low, wc[z, :local]) + rows[0:1]) * scaling).astype(BF16)
        flat = nn(wc[z, 2 * local :], mem[...])
        column = jnp.swapaxes(jnp.broadcast_to(rows[1:2], (8, local)), 0, 1)[:, :1]
        kv[z, :local] = flat[:local].astype(BF16)
        kv[z, local:] = (flat[local:] + column).astype(BF16)
        for i in range(heads):
            at = HD * i
            scores = nn(cq[z, :, at : at + HD], kv[z, at : at + HD])
            scores = jnp.where(allowed, scores, NEG_FILL)
            peak = jnp.max(scores, -1, keepdims=True)
            weights = jnp.exp(scores - peak)
            mass = jnp.sum(weights, -1, keepdims=True)
            probs = (weights / mass).astype(BF16)
            low[z, :, at : at + HD] = nt(probs, kv[z, local + at : local + at + HD]).astype(BF16)
            total[z * heads + i] = peak + jnp.log(mass)
        acc[...] += nn(low[z], wc[z, local : 2 * local])
        return carry

    lax.fori_loop(0, mp, step, 0)
    z2[...] = acc[...]
    unit, _ = normed(acc[...])
    second[...] = unit * gain[1:2] + bias[1:2]


def put_slots(beside, mine, place, z, base, size, source):
    half = lax.div(z, 2)
    at = lax.rem(z, 2)
    for offset in range(4):
        slot = slot_of(offset, half)
        for target, flip in ((mine, 0), (beside, 4)):
            row = pl.multiple_of((place ^ (offset + flip)) * size, 16)
            target[slot, at, base : base + size] = source[pl.ds(row, size)].astype(BF16)


def ffn_both(dims, meta, second, z2, grad, ib, ob, gain, bias, *refs):
    mp, local, heads, scaling, nseg = dims
    pieces, (own_in, own_out) = refs[:10], refs[10:12]
    result, dz2, sums, beside, mine = refs[12:17]
    win, wout, acc, act, slope, dw, sems = refs[17:]
    place = meta[0]
    fetch(pieces, place, win, 0, 96, sems.at[0])
    fetch_own(own_in, win, 0, sems.at[0])
    fetch(pieces, place, wout, 96, 192, sems.at[1])
    fetch_own(own_out, wout, 0, sems.at[1])
    acc[...] = second[...] + ob[2:3]
    second_low = second[...].astype(BF16)
    arrive(win, sems.at[0])
    arrive(wout, sems.at[1])

    def forward(z, carry):
        inner = nn(second_low, win[z]) + ib[z]
        share = 0.5 * (1.0 + lax.erf(inner * ROOT_HALF))
        act[z] = (inner * share).astype(BF16)
        slope[z] = share + inner * (ROOT_TWO_PI * jnp.exp(-0.5 * inner * inner))
        acc[...] += nn(act[z], wout[z])
        return carry

    lax.fori_loop(0, mp, forward, 0)
    unit, inverse = normed(acc[...])
    result[...] = (unit * gain[2:3] + bias[2:3]).astype(BF16)
    out_grad = grad[...].astype(F32)
    third = norm_back(unit, inverse, gain[2:3], out_grad)
    sums[...] = jnp.zeros_like(sums)
    sums[0:1] = row_sum(third)
    sums[1:2] = row_sum(out_grad * unit)
    sums[2:3] = row_sum(out_grad)
    third_low = third.astype(BF16)
    acc[...] = third

    def backward(z, carry):
        inner = nt(third_low, wout[z]) * slope[z]
        sums[pl.ds(8 + z, 1)] = row_sum(inner)
        inner_low = inner.astype(BF16)
        acc[...] += nt(inner_low, win[z])
        dw[...] = tn(second_low, inner_low)
        put_slots(beside, mine, place, z, 0, 96, dw)
        dw[...] = tn(act[z], third_low)
        put_slots(beside, mine, place, z, 96, 96, dw)
        return carry

    lax.fori_loop(0, mp, backward, 0)
    unit, inverse = normed(z2[...])
    grad_rows = acc[...]
    values = norm_back(unit, inverse, gain[1:2], grad_rows)
    dz2[...] = values
    sums[3:4] = row_sum(values)
    sums[4:5] = row_sum(grad_rows * unit)
    sums[5:6] = row_sum(grad_rows)


def cross_back(dims, meta, dz2, cq, total, z1, gain, *refs):
    mp, local, heads, scaling, nseg = dims
    kv_ref, pieces, owns = refs[0], refs[1:11], refs[11:14]
    mem_out, kv_low, dcq, dz1, sums, sums_local = refs[14:20]
    wc, kv, dmem, acc, dout, sems = refs[20:]
    fetch_cross(pieces, owns, meta[0], wc, sems.at[0])
    pltpu.make_async_copy(kv_ref, kv, sems.at[1]).start()
    allowed = cross_mask(meta, nseg, dz2.shape[0], kv.shape[2])
    dz2_low = dz2[...].astype(BF16)
    acc[...] = dz2[...]
    dmem[...] = jnp.zeros_like(dmem)
    arrive(wc, sems.at[0])
    arrive(kv, sems.at[1])

    def step(z, carry):
        dout[...] = nt(dz2_low, wc[z, local : 2 * local]).astype(BF16)
        for i in range(heads):
            at = HD * i
            query = cq[z, :, at : at + HD]
            key = kv[z, at : at + HD]
            value = kv[z, local + at : local + at + HD]
            grad = dout[:, at : at + HD]
            scores = jnp.where(allowed, nn(query, key), NEG_FILL)
            probs = jnp.exp(scores - total[z * heads + i])
            probs_low = probs.astype(BF16)
            prob_grad = nn(grad, value)
            offset = jnp.sum(probs * prob_grad, -1, keepdims=True)
            score_grad = (probs * (prob_grad - offset)).astype(BF16)
            kv_low[z, at : at + HD] = tn(query, score_grad).astype(BF16)
            kv_low[z, local + at : local + at + HD] = tn(grad, probs_low).astype(BF16)
            mass = jnp.sum(probs_low.astype(F32), -1, keepdims=True)
            query_grad = nt(score_grad, key) * scaling
            dcq[z, :, at : at + HD] = query_grad.astype(BF16)
            sums_local[z, 0:1, at : at + HD] = row_sum(query_grad)
            sums_local[z, 1:2, at : at + HD] = row_sum(mass * grad.astype(F32))
        acc[...] += nn(dcq[z], wc[z, :local])
        dmem[...] += tn(wc[z, 2 * local :], kv_low[z])
        return carry

    lax.fori_loop(0, mp, step, 0)
    for block in range(mp):
        row = pl.multiple_of(lax.rem(meta[1] + block, mp) * local, 16)
        mem_out[block] = dmem[pl.ds(row, local)].astype(BF16)
    unit, inverse = normed(z1[...])
    grad_rows = acc[...]
    values = norm_back(unit, inverse, gain[0:1], grad_rows)
    dz1[...] = values
    sums[...] = jnp.zeros_like(sums)
    sums[0:1] = row_sum(values)
    sums[1:2] = row_sum(grad_rows * unit)
    sums[2:3] = row_sum(grad_rows)


def head_back(dims, meta, dz1, x_ref, qkv, self_low, dz2, first, dcq, cross_low, *refs):
    mp, local, heads, scaling, nseg = dims
    cross_sums, cross_local, ffn_sums = refs[:3]
    refs = refs[3:]
    kv_ref, blocks, pieces = refs[0], refs[1 : 1 + mp], refs[1 + mp : 11 + mp]
    own_self, own_sp = refs[11 + mp : 13 + mp]
    dx, small, beside, mine = refs[13 + mp : 17 + mp]
    ws, kv, mem, acc, dout, dqkv, dw, sums_local, sems = refs[17 + mp :]
    place = meta[0]
    fetch(pieces, place, ws, 0, 96, sems.at[0])
    fetch_own(own_self, ws, 0, sems.at[0])
    fetch_own(own_sp, ws, 3 * local, sems.at[0])
    pltpu.make_async_copy(kv_ref, kv, sems.at[1]).start()
    fetch_memory(blocks, meta[1], mem, sems.at[2])
    allowed = self_mask(meta, nseg, x_ref.shape[0])
    dz1_low = dz1[...].astype(BF16)
    dz2_low = dz2[...].astype(BF16)
    first_low = first[...].astype(BF16)
    acc[...] = dz1[...]
    arrive(ws, sems.at[0])
    arrive(kv, sems.at[1])
    arrive(mem, sems.at[2])

    def step(z, carry):
        dout[...] = nt(dz1_low, ws[z, 3 * local :]).astype(BF16)
        for i in range(heads):
            at = HD * i
            query = qkv[z, :, at : at + HD]
            key = qkv[z, :, local + at : local + at + HD]
            value = qkv[z, :, 2 * local + at : 2 * local + at + HD]
            grad = dout[:, at : at + HD]
            scores = jnp.where(allowed, nt(query, key), NEG_FILL)
            weights = jnp.exp(scores - jnp.max(scores, -1, keepdims=True))
            probs = weights / jnp.sum(weights, -1, keepdims=True)
            prob_grad = nt(grad, value)
            offset = jnp.sum(probs * prob_grad, -1, keepdims=True)
            score_grad = (probs * (prob_grad - offset)).astype(BF16)
            value_grad = tn(probs.astype(BF16), grad)
            query_grad = nn(score_grad, key) * scaling
            dqkv[:, at : at + HD] = query_grad.astype(BF16)
            dqkv[:, local + at : local + at + HD] = tn(score_grad, query).astype(BF16)
            dqkv[:, 2 * local + at : 2 * local + at + HD] = value_grad.astype(BF16)
            sums_local[z, 0:1, at : at + HD] = row_sum(query_grad)
            sums_local[z, 1:2, at : at + HD] = row_sum(value_grad)
        acc[...] += nn(dqkv[...], ws[z, : 3 * local])
        dw[: 3 * local] = tn(dqkv[...], x_ref[...])
        dw[3 * local :] = tn(self_low[z], dz1_low)
        put_slots(beside, mine, place, z, 0, 96, dw)
        dw[:local] = tn(dcq[z], first_low)
        dw[local : 2 * local] = tn(cross_low[z], dz2_low)
        dw[2 * local :] = nt(kv[z], mem[...])
        put_slots(beside, mine, place, z, 96, 96, dw)
        return carry

    lax.fori_loop(0, mp, step, 0)
    dx[...] = acc[...]
    small[...] = jnp.zeros_like(small)
    small[0:3] = cross_sums[0:3]
    small[3:9] = ffn_sums[0:6]

    def collect(z, carry):
        row = 9 + 2 * lax.rem(meta[1] + mp - z, mp)
        for i, part in enumerate((sums_local, cross_local)):
            for j in (0, 1):
                at = (2 * i + j) * local
                small[pl.ds(row, 1), at : at + local] = part[z, j : j + 1]
        small[pl.ds(row + 1, 1)] = ffn_sums[pl.ds(8 + z, 1)]
        return carry

    lax.fori_loop(0, mp, collect, 0)


def place_rows(place, ranges, low, over_two, over_four, near, far, across):
    half = near.shape[0]
    rows = low.shape[0]

    def taken(offset, start, size):
        if offset >= 4:
            return across[pl.ds((offset - 4) * rows + start, size)]
        if offset < 3:
            return (low, over_two, over_four)[offset][pl.ds(start, size)]
        if start < half:
            return near[pl.ds(start, size)]
        return far[pl.ds(start - half, size)]

    for offset in range(8):
        position = place ^ offset
        for start, size, targets in ranges:
            if offset == 3 and start < half < start + size:
                parts = ((start, half - start), (half, start + size - half))
            else:
                parts = ((start, size),)
            for begin, length in parts:
                source = taken(offset, begin, length).astype(F32)
                first = 0
                for target in targets:
                    count = target.shape[0] // size

                    @pl.when((position >= first) & (position < first + count))
                    def _():
                        row = (position - first) * size + (begin - start)
                        target[pl.ds(pl.multiple_of(row, 8), length)] = source

                    first += count


def finish_heads(meta, *refs):
    place_rows(meta[0], ((0, 96, refs[6:8]), (96, 96, refs[8:])), *refs[:6])


def finish_ffn(meta, *refs):
    gi, go = refs[6:]
    place_rows(meta[0], ((0, 96, (gi,)), (96, 96, (go,))), *refs[:6])


def join_columns(meta, *refs):
    blocks, target = refs[:-1], refs[-1]
    count = len(blocks)
    for step, block in enumerate(blocks):
        size = block.shape[1]
        at = pl.multiple_of(lax.rem(meta[1] + count - step, count) * size, 128)
        target[:, pl.ds(at, size)] = block[...].astype(target.dtype)


def join_rows(meta, *refs):
    blocks, target = refs[:-1], refs[-1]
    count = len(blocks)
    for step, block in enumerate(blocks):
        size = block.shape[0]
        at = pl.multiple_of(lax.rem(meta[1] + count - step, count) * size, 16)
        target[pl.ds(at, size)] = block[...].astype(target.dtype)


def shaped(shape, dtype=F32):
    return jax.ShapeDtypeStruct(shape, dtype)


def in_vmem(count):
    return [pl.BlockSpec(memory_space=pltpu.VMEM)] * count


def in_place(count):
    return [pl.BlockSpec(memory_space=pl.ANY)] * count


META = pl.BlockSpec(memory_space=pltpu.SMEM)


def call(kernel, in_specs, outs, scratch, flops, moved, name):
    return pl.pallas_call(
        kernel,
        out_shape=outs,
        in_specs=in_specs,
        out_specs=in_vmem(len(outs)),
        scratch_shapes=scratch,
        name=name,
        compiler_params=pltpu.CompilerParams(vmem_limit_bytes=60 * 1024 * 1024),
        cost_estimate=pl.CostEstimate(
            flops=flops // 16, bytes_accessed=moved // 4, transcendentals=0
        ),
    )


def solution(mesh):
    dp = mesh.shape["dp"]
    mp = mesh.shape["mp"]

    def swap(value, bit):
        return lax.ppermute(value, "dp", [(i, i ^ bit) for i in range(dp)])

    def shift(value, step):
        return lax.ppermute(value, "mp", [(i, (i + step) % mp) for i in range(mp)])

    def flip(value, bit):
        return lax.ppermute(value, "mp", [(i, i ^ bit) for i in range(mp)])

    def after(value, *others):
        return lax.optimization_barrier((value,) + others)[0] if others else value

    def meet(*values):
        return lax.optimization_barrier(values)

    def near_chips(own):
        return swap(own, 2), swap(own, 4)

    def far_chips(over_two, over_four):
        def halves(piece):
            if piece.ndim == 3:
                piece = piece.reshape(-1, piece.shape[1] // 2, piece.shape[2])
            half = piece.shape[0] // 2
            return piece[:half], piece[half:]

        return swap(halves(over_four)[0], 2), swap(halves(over_two)[1], 4)

    def beside(pieces):
        found = []
        for piece in pieces:
            found.append(swap(after(piece, *found[-1:]), 1))
        return found

    class Group:
        def __init__(self, *pairs):
            self.pairs = pairs
            self.low = self.summed(slice(0, 6)).astype(BF16)

        def summed(self, slots):
            parts = [
                mine[slots].astype(F32) + other[slots].astype(F32) for other, mine in self.pairs
            ]
            return parts[0] if len(parts) == 1 else jnp.concatenate(parts, axis=-2)

        def first(self):
            return swap(self.low[0:2], 2), swap(self.low[2:4], 4)

        def second(self, from_two, from_four):
            late_four = (self.low[5].astype(F32) + from_two[0].astype(F32)).astype(BF16)
            late_two = (self.low[4].astype(F32) + from_four[0].astype(F32)).astype(BF16)
            return late_two, late_four

        def third(self, from_two, from_four, late_two, late_four):
            top = self.summed(6) + from_two[1].astype(F32) + late_four.astype(F32)
            end = self.summed(7) + from_four[1].astype(F32) + late_two.astype(F32)
            bit = SUB
            while bit < dp:
                top = top + swap(top, bit)
                end = end + swap(end, bit)
                bit *= 2
            blocks = [top[0], top[1], end[0], end[1]]
            return blocks[0], [block.astype(BF16) for block in blocks[1:]]

    def line_sum(total, sent):
        for piece in sent:
            total = total + piece.astype(F32)
        return total.astype(BF16)

    def body(
        hidden,
        memory,
        out_grad,
        dec_starts,
        dec_length,
        mem_starts,
        mem_length,
        self_qkv,
        self_qv_bias,
        self_proj,
        cross_query,
        cross_kv,
        cross_qv_bias,
        cross_proj,
        ffn_in,
        ffn_in_bias,
        ffn_out,
        out_biases,
        norm_gains,
        norm_biases,
    ):
        row_count = dec_starts.shape[0]
        assert row_count == mp == 4 and dp % SUB == 0
        slots = hidden.shape[0] // row_count
        mem_slots = memory.shape[0] // row_count
        width = hidden.shape[1]
        local = self_proj.shape[0]
        heads = local // HD
        inner = ffn_out.shape[0]
        nseg = dec_starts.shape[1]
        dims = (mp, local, heads, HD ** (-0.5), nseg)
        line = lax.axis_index("mp")
        device = lax.axis_index("dp") % SUB
        place = (device & 1) * 4 + device // 2

        def row_of(array, size):
            return lax.dynamic_slice_in_dim(array, line * size, size, 0)

        def slice_of(array):
            size = array.shape[0] // SUB
            return lax.dynamic_slice_in_dim(array, place * size, size, 0)

        meta = jnp.concatenate(
            [
                jnp.stack([place, line]).astype(jnp.int32),
                row_of(dec_length, 1),
                row_of(mem_length, 1),
                row_of(dec_starts, 1)[0],
                row_of(mem_starts, 1)[0],
            ]
        )
        own_self = jnp.swapaxes(self_qkv, 1, 2).reshape(3 * local, width)
        own_cq = cross_query.T
        own_kv = jnp.swapaxes(cross_kv, 1, 2).reshape(2 * local, width)

        bias = jnp.concatenate(
            [self_qv_bias.reshape(-1), cross_qv_bias.reshape(-1), ffn_in_bias]
        ).reshape(-1, width)
        terms = []
        rest = bias
        for _ in range(3):
            term = lax.reduce_precision(rest, 8, 7)
            terms.append(term.astype(BF16))
            rest = rest - term
        bias_rows = 3 * bias.shape[0]
        terms = jnp.concatenate(terms + [jnp.zeros((16 - bias_rows, width), BF16)])
        head_piece = jnp.concatenate(
            [
                slice_of(jnp.concatenate([own_self, self_proj])),
                slice_of(jnp.concatenate([own_cq, cross_proj, own_kv])),
                terms,
            ]
        )
        ffn_piece = jnp.concatenate([slice_of(ffn_in), slice_of(ffn_out)])
        memory_t = memory.T
        memory_blocks = [
            lax.dynamic_slice_in_dim(memory_t, ((line + step) % mp) * mem_slots, mem_slots, 1)
            for step in range(mp)
        ]
        head_line = [shift(head_piece, step) for step in range(1, mp)]
        rows = head_piece.shape[0] - 16
        head_own = jnp.stack([piece[:rows] for piece in head_line])
        head_near = near_chips(head_own)
        ffn_piece = after(ffn_piece, *head_line)
        ffn_line = [shift(ffn_piece, step) for step in range(1, mp)]
        head_own, head_near, ffn_line, memory_blocks = meet(
            head_own, head_near, ffn_line, memory_blocks
        )
        head_far = far_chips(*head_near)
        head_beside = [swap(head_own, 1), swap(head_near[0], 1)]
        memory_blocks[1] = shift(memory_blocks[1], 1)
        ffn_own = jnp.stack(ffn_line)
        head_own, head_near, head_far, head_beside, ffn_own, memory_blocks = meet(
            head_own, head_near, head_far, head_beside, ffn_own, memory_blocks
        )
        head_beside += beside((head_near[1], *head_far))
        head_pieces = (head_own, *head_near, *head_far, *head_beside)
        ffn_near = near_chips(ffn_own)
        memory_blocks[2] = shift(memory_blocks[2], 2)
        biases = [bias]
        for piece in head_line:
            term = piece[rows : rows + bias_rows].reshape(3, -1, width).astype(F32)
            biases.append((term[0] + term[1]) + term[2])
        biases = jnp.stack(biases).reshape(mp, -1)

        self_bias = biases[:, : 2 * local].reshape(mp, 2, local)
        cross_bias = biases[:, 2 * local : 4 * local].reshape(mp, 2, local)
        inner_bias = biases[:, None, 4 * local :]
        hidden_row = row_of(hidden, slots)
        grad_row = row_of(out_grad, slots)
        params = (out_biases, norm_gains, norm_biases)
        dma = pltpu.SemaphoreType.DMA((2,))
        square = VMEM((width, width), F32)
        weights_shape = VMEM((mp, 4 * local, width), BF16)
        flat_shape = VMEM((slots, width), F32)
        kv_shape = VMEM((mp, 2 * local, mem_slots), BF16)
        row_shape = shaped((slots, width))
        low_shape = shaped((mp, slots, local), BF16)
        head_slots = shaped((8, 2, 4 * local // SUB, width), BF16)
        ffn_slots = shaped((8, 2, 2 * width // SUB, width), BF16)
        matmul = 2 * slots * width * width
        plain = width * width * 2

        def spread_line(rows):
            return [rows] + [shift(rows, step) for step in range(1, mp)]

        def bound(kernel):
            return lambda *refs: kernel(dims, *refs)

        qkv, self_low, z1, first = call(
            bound(self_forward),
            [META] + in_vmem(5) + in_place(12),
            (shaped((mp, slots, 3 * local), BF16), low_shape, row_shape, row_shape),
            [weights_shape, flat_shape, dma],
            20 * matmul,
            8 * plain,
            "self_forward",
        )(meta, hidden_row, self_bias, *params, *head_pieces, own_self, self_proj)
        ffn_own, ffn_near, memory_blocks, qkv, self_low, z1, first = meet(
            ffn_own, ffn_near, memory_blocks, qkv, self_low, z1, first
        )
        ffn_far = far_chips(*ffn_near)
        memory_blocks[3] = shift(memory_blocks[3], 3)
        ffn_far, ffn_beside, memory_blocks, first = meet(
            ffn_far, [swap(ffn_own, 1)], memory_blocks, first
        )
        ffn_beside += [swap(piece, 1) for piece in (*ffn_near, *ffn_far)]
        ffn_pieces = (ffn_own, *ffn_near, *ffn_far, *ffn_beside)
        cross_q, kv, cross_low, cross_total, z2, second = call(
            bound(cross_forward),
            [META] + in_vmem(5) + in_place(mp + 13),
            (
                low_shape,
                shaped((mp, 2 * local, mem_slots), BF16),
                low_shape,
                shaped((mp * heads, slots, 1)),
                row_shape,
                row_shape,
            ),
            [weights_shape, VMEM((width, mem_slots), BF16), flat_shape, dma],
            40 * matmul,
            8 * plain,
            "cross_forward",
        )(
            meta,
            cross_bias,
            *params,
            first,
            *memory_blocks,
            *head_pieces,
            own_cq,
            cross_proj,
            own_kv,
        )
        result, dz2, ffn_sums, ffn_beside, ffn_mine = call(
            bound(ffn_both),
            [META] + in_vmem(7) + in_place(12),
            (
                shaped((slots, width), BF16),
                row_shape,
                shaped((16, width)),
                ffn_slots,
                ffn_slots,
            ),
            [
                VMEM((mp, width, inner), BF16),
                VMEM((mp, inner, width), BF16),
                flat_shape,
                VMEM((mp, slots, inner), BF16),
                VMEM((mp, slots, inner), F32),
                square,
                dma,
            ],
            50 * matmul,
            16 * plain,
            "ffn_both",
        )(meta, second, z2, grad_row, inner_bias, *params, *ffn_pieces, ffn_in, ffn_out)
        ffn_other = swap(ffn_beside, 1)
        result_blocks = spread_line(result)

        memory_grads, kv_low, cross_dq, dz1, cross_sums, cross_local = call(
            bound(cross_back),
            [META] + in_vmem(5) + in_place(14),
            (
                shaped((mp, local, mem_slots), BF16),
                shaped((mp, 2 * local, mem_slots), BF16),
                low_shape,
                row_shape,
                shaped((8, width)),
                shaped((mp, 2, local)),
            ),
            [
                weights_shape,
                kv_shape,
                VMEM((width, mem_slots), F32),
                flat_shape,
                VMEM((slots, local), BF16),
                dma,
            ],
            50 * matmul,
            12 * plain,
            "cross_back",
        )(
            meta,
            dz2,
            cross_q,
            cross_total,
            z1,
            norm_gains,
            kv,
            *head_pieces,
            own_cq,
            cross_proj,
            own_kv,
        )
        ffn_other, result_blocks, memory_grads, kv_low, dz1 = meet(
            ffn_other, result_blocks, memory_grads, kv_low, dz1
        )
        ffn_group = Group((ffn_other, ffn_mine))
        ffn_group.low, dz1, memory_grads = meet(ffn_group.low, dz1, memory_grads)
        ffn_from = ffn_group.first()
        memory_out = [memory_grads[0]] + [shift(memory_grads[step], step) for step in (1, 2)]
        hidden_grad, small, head_beside, head_mine = call(
            bound(head_back),
            [META] + in_vmem(11) + in_place(mp + 13),
            (row_shape, shaped((24, width)), ffn_slots, ffn_slots),
            [
                weights_shape,
                kv_shape,
                VMEM((width, mem_slots), BF16),
                flat_shape,
                VMEM((slots, local), BF16),
                VMEM((slots, 3 * local), BF16),
                square,
                VMEM((mp, 2, local), F32),
                pltpu.SemaphoreType.DMA((3,)),
            ],
            60 * matmul,
            24 * plain,
            "head_back",
        )(
            meta,
            dz1,
            hidden_row,
            qkv,
            self_low,
            dz2,
            first,
            cross_dq,
            cross_low,
            cross_sums,
            cross_local,
            ffn_sums,
            kv_low,
            *memory_blocks,
            *head_pieces,
            own_self,
            self_proj,
        )
        ffn_from, memory_out, memory_grads, hidden_grad, small, head_beside, head_mine = meet(
            ffn_from, memory_out, memory_grads, hidden_grad, small, head_beside, head_mine
        )
        late_two, late_four = ffn_group.second(*ffn_from)
        head_other = swap(head_beside, 1)
        small = small + flip(small, 1)
        memory_out.append(shift(after(memory_grads[3], small), 3))
        ffn_late = swap(late_two, 2), swap(late_four, 4)
        ffn_late, head_other, memory_out = meet(ffn_late, head_other, memory_out)
        head_group = Group((head_other, head_mine))
        head_from = head_group.first()
        bit = 2
        while bit < mp:
            small = small + flip(small, bit)
            bit *= 2
        ffn_late = after(ffn_late[0], small), ffn_late[1]
        ffn_total, ffn_blocks = ffn_group.third(*ffn_from, *ffn_late)
        ffn_sent = [shift(ffn_blocks[step - 1], -step) for step in range(1, mp)]

        def joined(kernel, blocks, shape, dtype, name):
            return call(
                kernel, [META] + in_vmem(mp), (shaped(shape, dtype),), [], 0, 2 * plain, name
            )(meta, *blocks)[0]

        rows_shape = (mp * slots, width)
        memory_grad = joined(
            join_columns, memory_out, (local, mp * mem_slots), F32, "join_memory"
        )
        result = joined(join_rows, result_blocks, rows_shape, BF16, "join_result")
        head_from, ffn_sent, memory_grad, result, hidden_grad = meet(
            head_from, ffn_sent, memory_grad, result, hidden_grad
        )
        late_two, late_four = head_group.second(*head_from)
        head_late = swap(late_two, 2), swap(late_four, 4)
        hidden_blocks = spread_line(hidden_grad.astype(BF16))
        ffn_low = line_sum(ffn_total, ffn_sent)
        head_late, hidden_blocks, ffn_low, small = meet(head_late, hidden_blocks, ffn_low, small)
        head_total, head_blocks = head_group.third(*head_from, *head_late)
        ffn_near = near_chips(ffn_low)
        head_sent = [shift(head_blocks[0], -1), shift(head_blocks[2], -3)]
        ffn_near, head_sent, head_blocks = meet(ffn_near, head_sent, head_blocks)
        ffn_far = far_chips(*ffn_near)
        head_sent.append(shift(head_blocks[1], -2))
        hidden_grad = joined(join_rows, hidden_blocks, rows_shape, F32, "join_hidden")
        head_sent, ffn_near, ffn_far, small, hidden_grad = meet(
            head_sent, ffn_near, ffn_far, small, hidden_grad
        )
        head_low = line_sum(head_total, head_sent)
        head_near = near_chips(head_low)
        ffn_reduced = (ffn_low, *ffn_near, *ffn_far)
        ffn_reduced += (swap(jnp.concatenate(ffn_reduced), 1),)
        small = small + swap(small, 1)
        head_near, ffn_reduced, small = meet(head_near, ffn_reduced, small)
        grad_in, grad_out = call(
            finish_ffn,
            [META] + in_vmem(6),
            (shaped((width, inner)), shaped((inner, width))),
            [],
            0,
            plain,
            "finish_ffn",
        )(meta, *ffn_reduced)
        head_far = far_chips(*head_near)
        small = small + swap(small, 2)
        head_far, small, grad_in, grad_out = meet(head_far, small, grad_in, grad_out)
        head_reduced = (head_low, *head_near, *head_far)
        head_reduced += (swap(jnp.concatenate(head_reduced), 1),)
        small = small + swap(small, 4)
        bit = SUB
        while bit < dp:
            small = small + swap(small, bit)
            bit *= 2
        sharded = lax.dynamic_index_in_dim(
            small[9 : 9 + 2 * mp].reshape(mp, -1), line, 0, keepdims=False
        )
        grad_self, grad_sp, grad_cq, grad_cp, grad_kv = call(
            finish_heads,
            [META] + in_vmem(6),
            (
                shaped((3 * local, width)),
                shaped((local, width)),
                shaped((local, width)),
                shaped((local, width)),
                shaped((2 * local, width)),
            ),
            [],
            0,
            plain,
            "finish_heads",
        )(meta, *head_reduced)
        return (
            result,
            hidden_grad,
            memory_grad.T,
            jnp.swapaxes(grad_self.reshape(3, local, width), 1, 2),
            sharded[: 2 * local].reshape(2, local),
            grad_sp,
            grad_cq.T,
            jnp.swapaxes(grad_kv.reshape(2, local, width), 1, 2),
            sharded[2 * local : 4 * local].reshape(2, local),
            grad_cp,
            grad_in,
            sharded[4 * local :],
            grad_out,
            jnp.stack([small[0], small[6], small[3]]),
            jnp.stack([small[1], small[7], small[4]]),
            jnp.stack([small[2], small[8], small[5]]),
        )

    return jax.shard_map(
        body,
        mesh=mesh,
        in_specs=(
            P("dp", None),
            P("dp", "mp"),
            P("dp", None),
            P("dp", None),
            P("dp"),
            P("dp", None),
            P("dp"),
            P(None, None, "mp"),
            P(None, "mp"),
            P("mp", None),
            P(None, "mp"),
            P(None, None, "mp"),
            P(None, "mp"),
            P("mp", None),
            P(None, "mp"),
            P("mp"),
            P("mp", None),
            P(),
            P(),
            P(),
        ),
        out_specs=(
            P("dp", None),
            P("dp", None),
            P("dp", "mp"),
            P(None, None, "mp"),
            P(None, "mp"),
            P("mp", None),
            P(None, "mp"),
            P(None, None, "mp"),
            P(None, "mp"),
            P("mp", None),
            P(None, "mp"),
            P("mp"),
            P("mp", None),
            P(),
            P(),
            P(),
        ),
        check_vma=False,
    )
```

```python
import jax
import jax.numpy as jnp
from jax import lax
from jax.experimental import pallas as pl
from jax.experimental.pallas import tpu as pltpu
from jax.sharding import PartitionSpec as P

HD = 64
SUB = 8
NEG_FILL = -1000000000.0
EPSILON = 1e-05
F32 = jnp.float32
BF16 = jnp.bfloat16
VMEM = pltpu.VMEM
ROOT_HALF = 0.7071067811865476
ROOT_TWO_PI = 0.3989422804014327
SLOTS = ((3, 0), (1, 0), (3, 1), (2, 1), (1, 1), (2, 0), (0, 0), (0, 1))


def nn(left, right):
    return lax.dot_general(left, right, (((1,), (0,)), ((), ())), preferred_element_type=F32)


def nt(left, right):
    return lax.dot_general(left, right, (((1,), (1,)), ((), ())), preferred_element_type=F32)


def tn(left, right):
    return lax.dot_general(left, right, (((0,), (0,)), ((), ())), preferred_element_type=F32)


def normed(values):
    average = jnp.mean(values, -1, keepdims=True)
    centered = values - average
    variance = jnp.mean(centered * centered, -1, keepdims=True)
    inverse = lax.rsqrt(variance + EPSILON)
    return centered * inverse, inverse


def norm_back(unit, inverse, gain, grad):
    scaled = grad * gain
    return (
        scaled
        - jnp.mean(scaled, -1, keepdims=True)
        - unit * jnp.mean(scaled * unit, -1, keepdims=True)
    ) * inverse


def row_sum(values):
    return jnp.sum(values, 0, keepdims=True)


def segments(meta, start, count, shape, axis):
    places = lax.broadcasted_iota(jnp.int32, shape, axis)
    found = jnp.zeros(shape, jnp.int32) - 1
    for j in range(count):
        found = found + (meta[start + j] <= places).astype(jnp.int32)
    return found, places


def fetch(pieces, place, target, low, high, sems):
    size = high - low
    blocks, rows = pieces[0].shape[:2]
    half = rows // 2
    for block in range(blocks):
        sem = sems.at[block + 1]
        for beside in (0, 1):
            whole = pieces[5 * beside : 5 * beside + 3]
            split = pieces[5 * beside + 3 : 5 * beside + 5]
            for offset in range(4):
                row = (place ^ (offset + 4 * beside)) * size
                if offset < 3:
                    source = whole[offset].at[block, pl.ds(low, size)]
                    to = target.at[block + 1, pl.ds(pl.multiple_of(row, 16), size)]
                    pltpu.make_async_copy(source, to, sem).start()
                    continue
                for part in range(low // half, high // half):
                    at = 2 * block + part
                    source = split[at // blocks].at[at % blocks]
                    start = pl.multiple_of(row + part * half - low, 16)
                    to = target.at[block + 1, pl.ds(start, half)]
                    pltpu.make_async_copy(source, to, sem).start()


def fetch_own(sources, target, sems):
    row = 0
    for source in sources:
        size = source.shape[0]
        pltpu.make_async_copy(source, target.at[0, pl.ds(row, size)], sems.at[0]).start()
        row += size


def arrive(target, sem):
    pltpu.make_async_copy(target, target, sem).wait()


def fetch_memory(blocks, line, target, sem):
    count = len(blocks)
    for step, block in enumerate(blocks):
        size = block.shape[0]
        row = pl.multiple_of(lax.rem(line + count - step, count) * size, 16)
        pltpu.make_async_copy(block, target.at[pl.ds(row, size)], sem).start()


def slot_of(offset, half):
    first = SLOTS.index((offset, 0))
    second = SLOTS.index((offset, 1))
    return jnp.where(half == 0, first, second)


def self_mask(meta, nseg, slots):
    shape = (slots, slots)
    query_segment, query_place = segments(meta, 4, nseg, shape, 0)
    key_segment, key_place = segments(meta, 4, nseg, shape, 1)
    return (query_segment == key_segment) & (key_place <= query_place) & (key_place < meta[2])


def self_forward(dims, meta, x_ref, sb, ob, gain, bias, *refs):
    mp, local, heads, scaling, nseg = dims
    pieces, (own_self, own_sp) = refs[:10], refs[10:12]
    qkv, low, z1, first = refs[12:16]
    ws, acc, sems = refs[16:]
    fetch_own((own_self, own_sp), ws, sems.at[0])
    fetch(pieces, meta[0], ws, 0, 96, sems.at[0])
    allowed = self_mask(meta, nseg, x_ref.shape[0])
    acc[...] = x_ref[...].astype(F32) + ob[0:1]

    def step(z, carry):
        arrive(ws.at[z], sems.at[0, z])
        flat = nt(x_ref[...], ws[z, : 3 * local])
        rows = sb[z]
        qkv[z, :, :local] = ((flat[:, :local] + rows[0:1]) * scaling).astype(BF16)
        qkv[z, :, local : 2 * local] = flat[:, local : 2 * local].astype(BF16)
        qkv[z, :, 2 * local :] = (flat[:, 2 * local :] + rows[1:2]).astype(BF16)
        for i in range(heads):
            at = HD * i
            scores = nt(qkv[z, :, at : at + HD], qkv[z, :, local + at : local + at + HD])
            scores = jnp.where(allowed, scores, NEG_FILL)
            weights = jnp.exp(scores - jnp.max(scores, -1, keepdims=True))
            probs = (weights * (1.0 / jnp.sum(weights, -1, keepdims=True))).astype(BF16)
            out = nn(probs, qkv[z, :, 2 * local + at : 2 * local + at + HD])
            low[z, :, at : at + HD] = out.astype(BF16)
        acc[...] += nn(low[z], ws[z, 3 * local :])
        return carry

    lax.fori_loop(0, mp, step, 0)
    z1[...] = acc[...]
    unit, _ = normed(acc[...])
    first[...] = unit * gain[0:1] + bias[0:1]


def cross_mask(meta, nseg, slots, mem_slots):
    query_segment, _ = segments(meta, 4, nseg, (slots, 1), 0)
    key_segment, key_place = segments(meta, 4 + nseg, nseg, (1, mem_slots), 1)
    key_segment = jnp.where(key_place < meta[3], key_segment, -1)
    return query_segment == key_segment


def fetch_cross(pieces, owns, place, target, sem):
    fetch_own(owns, target, sem)
    fetch(pieces, place, target, 96, 192, sem)


def cross_forward(dims, meta, cb, ob, gain, bias, first, *refs):
    mp, local, heads, scaling, nseg = dims
    blocks, pieces, owns = refs[:mp], refs[mp : mp + 10], refs[mp + 10 : mp + 13]
    cq, kv, low, total, z2, second = refs[mp + 13 : mp + 19]
    wc, mem, acc, sems = refs[mp + 19 :]
    fetch_memory(blocks, meta[1], mem, sems.at[1, 0])
    fetch_cross(pieces, owns, meta[0], wc, sems.at[0])
    allowed = cross_mask(meta, nseg, first.shape[0], mem.shape[1])
    acc[...] = first[...] + ob[1:2]
    first_low = first[...].astype(BF16)
    arrive(mem, sems.at[1, 0])

    def step(z, carry):
        arrive(wc.at[z], sems.at[0, z])
        rows = cb[z]
        cq[z] = ((nt(first_low, wc[z, :local]) + rows[0:1]) * scaling).astype(BF16)
        flat = nn(wc[z, 2 * local :], mem[...])
        column = jnp.swapaxes(jnp.broadcast_to(rows[1:2], (8, local)), 0, 1)[:, :1]
        keys = flat[:local].astype(BF16)
        values = (flat[local:] + column).astype(BF16)
        kv[z, :local] = keys
        kv[z, local:] = values
        for i in range(heads):
            at = HD * i
            scores = nn(cq[z, :, at : at + HD], keys[at : at + HD])
            scores = jnp.where(allowed, scores, NEG_FILL)
            peak = jnp.max(scores, -1, keepdims=True)
            weights = jnp.exp(scores - peak)
            mass = jnp.sum(weights, -1, keepdims=True)
            probs = (weights * (1.0 / mass)).astype(BF16)
            low[z, :, at : at + HD] = nt(probs, values[at : at + HD]).astype(BF16)
            total[z * heads + i] = peak + jnp.log(mass)
        acc[...] += nn(low[z], wc[z, local : 2 * local])
        return carry

    lax.fori_loop(0, mp, step, 0)
    z2[...] = acc[...]
    unit, _ = normed(acc[...])
    second[...] = unit * gain[1:2] + bias[1:2]


def put_slots(beside, mine, place, z, base, source, sem):
    half = lax.div(z, 2)
    at = lax.rem(z, 2)
    size = source.shape[0] // SUB
    for offset in range(4):
        slot = slot_of(offset, half)
        for target, flip in ((mine, 0), (beside, 4)):
            row = pl.multiple_of((place ^ (offset + flip)) * size, 16)
            to = target.at[slot, at, pl.ds(base, size)]
            pltpu.make_async_copy(source.at[pl.ds(row, size)], to, sem).start()


def ffn_both(dims, meta, second, z2, grad, ib, ob, gain, bias, *refs):
    mp, local, heads, scaling, nseg = dims
    pieces, (own_in, own_out) = refs[:10], refs[10:12]
    result, dz2, sums, shared, own_half = refs[12:17]
    win, wout, acc, act, slope, low, sems = refs[17:]
    place = meta[0]
    width = second.shape[1]
    half = width // 2
    mine = pl.multiple_of(lax.div(place, 4) * half, 128)
    other = pl.multiple_of((1 - lax.div(place, 4)) * half, 128)
    fetch_own((own_in,), win, sems.at[0])
    fetch_own((own_out,), wout, sems.at[1])
    fetch(pieces, place, win, 0, 96, sems.at[0])
    fetch(pieces, place, wout, 96, 192, sems.at[1])
    acc[...] = second[...] + ob[2:3]
    low[...] = second[...].astype(BF16)
    own_half[0] = low[:, pl.ds(mine, half)]
    shared[0, :, width:] = low[:, pl.ds(other, half)]

    def forward(z, carry):
        arrive(win.at[z], sems.at[0, z])
        arrive(wout.at[z], sems.at[1, z])
        inner = nn(low[...], win[z]) + ib[z]
        share = 0.5 * (1.0 + lax.erf(inner * ROOT_HALF))
        act[z] = (inner * share).astype(BF16)
        own_half[z + 1] = act[z, :, pl.ds(mine, half)]
        shared[z + 1, :, width:] = act[z, :, pl.ds(other, half)]
        slope[z] = share + inner * (ROOT_TWO_PI * jnp.exp(-0.5 * inner * inner))
        acc[...] += nn(act[z], wout[z])
        return carry

    lax.fori_loop(0, mp, forward, 0, unroll=True)
    unit, inverse = normed(acc[...])
    result[...] = (unit * gain[2:3] + bias[2:3]).astype(BF16)
    out_grad = grad[...].astype(F32)
    third = norm_back(unit, inverse, gain[2:3], out_grad)
    sums[...] = jnp.zeros_like(sums)
    sums[0:1] = row_sum(third)
    sums[1:2] = row_sum(out_grad * unit)
    sums[2:3] = row_sum(out_grad)
    third_low = third.astype(BF16)
    shared[0, :, :width] = third_low
    acc[...] = third

    def backward(z, carry):
        inner = nt(third_low, wout[z]) * slope[z]
        sums[pl.ds(8 + z, 1)] = row_sum(inner)
        inner_low = inner.astype(BF16)
        acc[...] += nt(inner_low, win[z])
        shared[z + 1, :, :width] = inner_low
        return carry

    lax.fori_loop(0, mp, backward, 0, unroll=True)
    unit, inverse = normed(z2[...])
    grad_rows = acc[...]
    values = norm_back(unit, inverse, gain[1:2], grad_rows)
    dz2[...] = values
    sums[3:4] = row_sum(values)
    sums[4:5] = row_sum(grad_rows * unit)
    sums[5:6] = row_sum(grad_rows)


def ffn_weights(dims, meta, shared, own_half, theirs, to_two, to_four, rest, rows, dw, sems):
    mp = dims[0]
    slots = shared.shape[1]
    width = rows.shape[2] - own_half.shape[2]
    for i in range(mp + 1):
        sem = sems.at[i % mp, i // mp]
        part = rows.at[i, pl.ds(0, slots)]
        pltpu.make_async_copy(shared.at[i, :, pl.ds(0, width)], part.at[:, pl.ds(0, width)], sem).start()
        pltpu.make_async_copy(own_half.at[i], part.at[:, pl.ds(width, width // 2)], sem).start()
        pltpu.make_async_copy(theirs.at[i], rows.at[i, pl.ds(slots, slots)], sem).start()
    arrive(rows.at[0], sems.at[0, 0])
    for z in range(mp):
        i = z + 1
        arrive(rows.at[i], sems.at[i % mp, i // mp])
        dw[z, 0] = tn(rows[0, :, width:], rows[i, :, :width]).astype(BF16)
        dw[z, 1] = tn(rows[i, :, width:], rows[0, :, :width]).astype(BF16)
        size = dw.shape[2] // 4
        for offset in range(4):
            slot = SLOTS.index((offset, z // 2))
            if slot < 4:
                target = (to_two, to_four)[slot // 2].at[slot % 2, z % 2]
            else:
                target = rest.at[slot - 4, z % 2]
            row = pl.multiple_of(((meta[0] ^ offset) & 3) * size, 16)
            for j in (0, 1):
                source = dw.at[z, j, pl.ds(row, size)]
                pltpu.make_async_copy(source, target.at[pl.ds(j * size, size)], sems.at[0, 2]).start()
    arrive(dw, sems.at[0, 2])


def cross_back(dims, meta, dz2, cq, total, z1, gain, *refs):
    mp, local, heads, scaling, nseg = dims
    kv_ref, pieces, owns = refs[0], refs[1:11], refs[11:14]
    mem_out, (kv_low, dcq, dz1, sums, sums_local) = refs[14 : 14 + mp], refs[14 + mp : 19 + mp]
    wc, kv, dmem, acc, dout, sems = refs[19 + mp :]
    for z in range(mp):
        pltpu.make_async_copy(kv_ref.at[z], kv.at[z], sems.at[1, z]).start()
    fetch_cross(pieces, owns, meta[0], wc, sems.at[0])
    allowed = cross_mask(meta, nseg, dz2.shape[0], kv.shape[2])
    dz2_low = dz2[...].astype(BF16)
    acc[...] = dz2[...]
    dmem[...] = jnp.zeros_like(dmem)

    def step(z, carry):
        arrive(wc.at[z], sems.at[0, z])
        arrive(kv.at[z], sems.at[1, z])
        dout[...] = nt(dz2_low, wc[z, local : 2 * local]).astype(BF16)
        for i in range(heads):
            at = HD * i
            query = cq[z, :, at : at + HD]
            key = kv[z, at : at + HD]
            value = kv[z, local + at : local + at + HD]
            grad = dout[:, at : at + HD]
            scores = jnp.where(allowed, nn(query, key), NEG_FILL)
            probs = jnp.exp(scores - total[z * heads + i])
            probs_low = probs.astype(BF16)
            prob_grad = nn(grad, value)
            offset = jnp.sum(probs * prob_grad, -1, keepdims=True)
            score_grad = (probs * (prob_grad - offset)).astype(BF16)
            kv_low[z, at : at + HD] = tn(query, score_grad).astype(BF16)
            kv_low[z, local + at : local + at + HD] = tn(grad, probs_low).astype(BF16)
            mass = jnp.sum(probs_low.astype(F32), -1, keepdims=True)
            query_grad = nt(score_grad, key) * scaling
            dcq[z, :, at : at + HD] = query_grad.astype(BF16)
            sums_local[z, 0:1, at : at + HD] = row_sum(query_grad)
            sums_local[z, 1:2, at : at + HD] = row_sum(mass * grad.astype(F32))
        acc[...] += nn(dcq[z], wc[z, :local])
        dmem[...] += tn(wc[z, 2 * local :], kv_low[z])
        return carry

    lax.fori_loop(0, mp, step, 0)
    for block in range(mp):
        row = pl.multiple_of(lax.rem(meta[1] + block, mp) * local, 16)
        mem_out[block][...] = dmem[pl.ds(row, local)].astype(BF16)
    unit, inverse = normed(z1[...])
    grad_rows = acc[...]
    values = norm_back(unit, inverse, gain[0:1], grad_rows)
    dz1[...] = values
    sums[...] = jnp.zeros_like(sums)
    sums[0:1] = row_sum(values)
    sums[1:2] = row_sum(grad_rows * unit)
    sums[2:3] = row_sum(grad_rows)


def head_back(dims, meta, dz1, x_ref, qkv, self_low, dz2, first, dcq, cross_low, *refs):
    mp, local, heads, scaling, nseg = dims
    cross_sums, cross_local, ffn_sums = refs[:3]
    refs = refs[3:]
    kv_ref, blocks, pieces = refs[0], refs[1 : 1 + mp], refs[1 + mp : 11 + mp]
    own_self, own_sp = refs[11 + mp : 13 + mp]
    dx, small, beside, mine = refs[13 + mp : 17 + mp]
    ws, kv, mem, acc, dout, dqkv, dw, sums_local, sems = refs[17 + mp :]
    place = meta[0]
    fetch_own((own_self, own_sp), ws, sems.at[0])
    fetch(pieces, place, ws, 0, 96, sems.at[0])
    fetch_memory(blocks, meta[1], mem, sems.at[2, 0])
    for z in range(mp):
        pltpu.make_async_copy(kv_ref.at[z], kv.at[z], sems.at[1, z]).start()
    allowed = self_mask(meta, nseg, x_ref.shape[0])
    dz1_low = dz1[...].astype(BF16)
    dz2_low = dz2[...].astype(BF16)
    first_low = first[...].astype(BF16)
    acc[...] = dz1[...]
    arrive(mem, sems.at[2, 0])

    def step(z, carry):
        arrive(ws.at[z], sems.at[0, z])
        arrive(kv.at[z], sems.at[1, z])
        dout[...] = nt(dz1_low, ws[z, 3 * local :]).astype(BF16)
        for i in range(heads):
            at = HD * i
            query = qkv[z, :, at : at + HD]
            key = qkv[z, :, local + at : local + at + HD]
            value = qkv[z, :, 2 * local + at : 2 * local + at + HD]
            grad = dout[:, at : at + HD]
            scores = jnp.where(allowed, nt(query, key), NEG_FILL)
            weights = jnp.exp(scores - jnp.max(scores, -1, keepdims=True))
            probs = weights * (1.0 / jnp.sum(weights, -1, keepdims=True))
            prob_grad = nt(grad, value)
            offset = jnp.sum(probs * prob_grad, -1, keepdims=True)
            score_grad = (probs * (prob_grad - offset)).astype(BF16)
            value_grad = tn(probs.astype(BF16), grad)
            query_grad = nn(score_grad, key) * scaling
            dqkv[:, at : at + HD] = query_grad.astype(BF16)
            dqkv[:, local + at : local + at + HD] = tn(score_grad, query).astype(BF16)
            dqkv[:, 2 * local + at : 2 * local + at + HD] = value_grad.astype(BF16)
            sums_local[z, 0:1, at : at + HD] = row_sum(query_grad)
            sums_local[z, 1:2, at : at + HD] = row_sum(value_grad)
        acc[...] += nn(dqkv[...], ws[z, : 3 * local])
        dw[z, 0, : 3 * local] = tn(dqkv[...], x_ref[...]).astype(BF16)
        dw[z, 0, 3 * local :] = tn(self_low[z], dz1_low).astype(BF16)
        put_slots(beside, mine, place, z, 0, dw.at[z, 0], sems.at[3, 0])
        dw[z, 1, :local] = tn(dcq[z], first_low).astype(BF16)
        dw[z, 1, local : 2 * local] = tn(cross_low[z], dz2_low).astype(BF16)
        dw[z, 1, 2 * local :] = nt(kv[z], mem[...]).astype(BF16)
        put_slots(beside, mine, place, z, 96, dw.at[z, 1], sems.at[3, 0])
        return carry

    lax.fori_loop(0, mp, step, 0)
    dx[...] = acc[...]
    small[...] = jnp.zeros_like(small)
    small[0:3] = cross_sums[0:3]
    small[3:9] = ffn_sums[0:6]

    def collect(z, carry):
        row = 9 + 2 * lax.rem(meta[1] + mp - z, mp)
        for i, part in enumerate((sums_local, cross_local)):
            for j in (0, 1):
                at = (2 * i + j) * local
                small[pl.ds(row, 1), at : at + local] = part[z, j : j + 1]
        small[pl.ds(row + 1, 1)] = ffn_sums[pl.ds(8 + z, 1)]
        return carry

    lax.fori_loop(0, mp, collect, 0)
    arrive(dw, sems.at[3, 0])


def place_rows(place, ranges, pieces):
    half = pieces[3].shape[0]

    def taken(offset, start, size):
        mine = pieces[5 * (offset // 4) :]
        offset = offset % 4
        if offset < 3:
            return mine[offset][pl.ds(start, size)]
        if start < half:
            return mine[3][pl.ds(start, size)]
        return mine[4][pl.ds(start - half, size)]

    for offset in range(8):
        position = place ^ offset
        for start, size, targets in ranges:
            if offset % 4 == 3 and start < half < start + size:
                parts = ((start, half - start), (half, start + size - half))
            else:
                parts = ((start, size),)
            for begin, length in parts:
                source = taken(offset, begin, length).astype(F32)
                first = 0
                for target in targets:
                    count = target.shape[0] // size

                    @pl.when((position >= first) & (position < first + count))
                    def _():
                        row = (position - first) * size + (begin - start)
                        target[pl.ds(pl.multiple_of(row, 8), length)] = source

                    first += count


def finish_heads(meta, small, *refs):
    place_rows(meta[0], ((0, 96, refs[10:12]), (96, 96, refs[12:15])), refs[:10])
    shared, sharded = refs[15:18], refs[18:]
    for i, target in enumerate(shared):
        for j, row in enumerate((0, 6, 3)):
            target[j : j + 1] = small[row + i : row + i + 1]
    row = 9 + 2 * meta[1]
    local = sharded[0].shape[1]
    for i in (0, 1):
        for j in (0, 1):
            at = (2 * i + j) * local
            sharded[i][j : j + 1] = small[pl.ds(row, 1), at : at + local]
    sharded[2][...] = small[pl.ds(row + 1, 1)].reshape(sharded[2].shape)


def finish_ffn(meta, *refs):
    gi, go = refs[6:]
    pieces, joined = list(refs[:5]), refs[5]
    row = 0
    for piece in refs[:5]:
        pieces.append(joined.at[pl.ds(row, piece.shape[0])])
        row += piece.shape[0]
    place_rows(meta[0], ((0, 96, (gi,)), (96, 96, (go,))), pieces)


def join_columns(meta, *refs):
    blocks, target = refs[:-1], refs[-1]
    count = len(blocks)
    for step, block in enumerate(blocks):
        size = block.shape[1]
        at = pl.multiple_of(lax.rem(meta[1] + count - step, count) * size, 128)
        target[:, pl.ds(at, size)] = block[...].astype(target.dtype)


def join_rows(meta, *refs):
    blocks, target = refs[:-1], refs[-1]
    count = len(blocks)
    for step, block in enumerate(blocks):
        size = block.shape[0]
        at = pl.multiple_of(lax.rem(meta[1] + count - step, count) * size, 16)
        target[pl.ds(at, size)] = block[...].astype(target.dtype)


def shaped(shape, dtype=F32):
    return jax.ShapeDtypeStruct(shape, dtype)


def in_vmem(count):
    return [pl.BlockSpec(memory_space=pltpu.VMEM)] * count


def in_place(count):
    return [pl.BlockSpec(memory_space=pl.ANY)] * count


META = pl.BlockSpec(memory_space=pltpu.SMEM)


def call(kernel, in_specs, outs, scratch, flops, moved, name, written=0):
    return pl.pallas_call(
        kernel,
        out_shape=outs,
        in_specs=in_specs,
        out_specs=in_vmem(len(outs) - written) + in_place(written),
        scratch_shapes=scratch,
        name=name,
        compiler_params=pltpu.CompilerParams(vmem_limit_bytes=60 * 1024 * 1024),
        cost_estimate=pl.CostEstimate(
            flops=flops // 16, bytes_accessed=moved // 4, transcendentals=0
        ),
    )


def solution(mesh):
    dp = mesh.shape["dp"]
    mp = mesh.shape["mp"]

    def swap(value, bit):
        return lax.ppermute(value, "dp", [(i, i ^ bit) for i in range(dp)])

    def shift(value, step):
        return lax.ppermute(value, "mp", [(i, (i + step) % mp) for i in range(mp)])

    def flip(value, bit):
        return lax.ppermute(value, "mp", [(i, i ^ bit) for i in range(mp)])

    def after(value, *others):
        return lax.optimization_barrier((value,) + others)[0] if others else value

    def meet(*values):
        return lax.optimization_barrier(values)

    def near_chips(own):
        return swap(own, 2), swap(own, 4)

    def far_chips(over_two, over_four):
        def halves(piece):
            if piece.ndim == 3:
                piece = piece.reshape(-1, piece.shape[1] // 2, piece.shape[2])
            half = piece.shape[0] // 2
            return piece[:half], piece[half:]

        return swap(halves(over_four)[0], 2), swap(halves(over_two)[1], 4)

    def beside(pieces):
        found = []
        for piece in pieces:
            found.append(swap(after(piece, *found[-1:]), 1))
        return found

    class Group:
        def __init__(self, summed):
            self.summed = summed

        def second(self, from_two, from_four):
            late_two = (self.summed(4) + from_four[0].astype(F32)).astype(BF16)
            late_four = (self.summed(5) + from_two[0].astype(F32)).astype(BF16)
            return late_two, late_four

        def third(self, from_two, from_four, late_two, late_four):
            blocks = []
            for slot, near, late in ((6, from_two, late_four), (7, from_four, late_two)):
                for i in (0, 1):
                    total = self.summed(slot, i) + near[1, i].astype(F32) + late[i].astype(F32)
                    bit = SUB
                    while bit < dp:
                        total = total + swap(total, bit)
                        bit *= 2
                    blocks.append(total)
            return blocks[0], [block.astype(BF16) for block in blocks[1:]]

    def line_sum(total, sent):
        for piece in sent:
            total = total + piece.astype(F32)
        return total.astype(BF16)

    def body(
        hidden,
        memory,
        out_grad,
        dec_starts,
        dec_length,
        mem_starts,
        mem_length,
        self_qkv,
        self_qv_bias,
        self_proj,
        cross_query,
        cross_kv,
        cross_qv_bias,
        cross_proj,
        ffn_in,
        ffn_in_bias,
        ffn_out,
        out_biases,
        norm_gains,
        norm_biases,
    ):
        row_count = dec_starts.shape[0]
        assert row_count == mp == 4 and dp % SUB == 0
        slots = hidden.shape[0] // row_count
        mem_slots = memory.shape[0] // row_count
        width = hidden.shape[1]
        local = self_proj.shape[0]
        heads = local // HD
        inner = ffn_out.shape[0]
        nseg = dec_starts.shape[1]
        dims = (mp, local, heads, HD ** (-0.5), nseg)
        line = lax.axis_index("mp")
        device = lax.axis_index("dp") % SUB
        place = (device & 1) * 4 + device // 2

        def row_of(array, size):
            return lax.dynamic_slice_in_dim(array, line * size, size, 0)

        def slice_of(array):
            size = array.shape[0] // SUB
            return lax.dynamic_slice_in_dim(array, place * size, size, 0)

        meta = jnp.concatenate(
            [
                jnp.stack([place, line]).astype(jnp.int32),
                row_of(dec_length, 1),
                row_of(mem_length, 1),
                row_of(dec_starts, 1)[0],
                row_of(mem_starts, 1)[0],
            ]
        )
        own_self = jnp.swapaxes(self_qkv, 1, 2).reshape(3 * local, width)
        own_cq = cross_query.T
        own_kv = jnp.swapaxes(cross_kv, 1, 2).reshape(2 * local, width)

        bias = jnp.concatenate(
            [self_qv_bias.reshape(-1), cross_qv_bias.reshape(-1), ffn_in_bias]
        ).reshape(-1, width)
        terms = []
        rest = bias
        for _ in range(3):
            term = lax.reduce_precision(rest, 8, 7)
            terms.append(term.astype(BF16))
            rest = rest - term
        bias_rows = 3 * bias.shape[0]
        terms = jnp.concatenate(terms + [jnp.zeros((16 - bias_rows, width), BF16)])
        head_piece = jnp.concatenate(
            [
                slice_of(jnp.concatenate([own_self, self_proj])),
                slice_of(jnp.concatenate([own_cq, cross_proj, own_kv])),
                terms,
            ]
        )
        ffn_piece = jnp.concatenate([slice_of(ffn_in), slice_of(ffn_out)])
        memory_t = memory.T
        memory_blocks = [
            lax.dynamic_slice_in_dim(memory_t, ((line + step) % mp) * mem_slots, mem_slots, 1)
            for step in range(mp)
        ]
        head_line = [shift(head_piece, step) for step in range(1, mp)]
        rows = head_piece.shape[0] - 16
        head_own = jnp.stack([piece[:rows] for piece in head_line])
        head_near = near_chips(head_own)
        ffn_piece = after(ffn_piece, *head_line)
        ffn_line = [shift(ffn_piece, step) for step in range(1, mp)]
        biases = [bias]
        for piece in head_line:
            term = piece[rows : rows + bias_rows].reshape(3, -1, width).astype(F32)
            biases.append((term[0] + term[1]) + term[2])
        biases = jnp.stack(biases).reshape(mp, -1)
        self_bias = biases[:, : 2 * local].reshape(mp, 2, local)
        cross_bias = biases[:, 2 * local : 4 * local].reshape(mp, 2, local)
        inner_bias = biases[:, None, 4 * local :]
        hidden_row = row_of(hidden, slots)
        grad_row = row_of(out_grad, slots)
        early = (meta, self_bias, cross_bias, inner_bias, hidden_row, grad_row)
        head_own, head_near, ffn_line, memory_blocks, early = meet(
            head_own, head_near, ffn_line, memory_blocks, early
        )
        meta, self_bias, cross_bias, inner_bias, hidden_row, grad_row = early
        head_far = far_chips(*head_near)
        head_beside = [swap(head_own, 1), swap(head_near[0], 1)]
        memory_blocks[1] = shift(memory_blocks[1], 1)
        ffn_own = jnp.stack(ffn_line)
        head_own, head_near, head_far, head_beside, ffn_own, memory_blocks = meet(
            head_own, head_near, head_far, head_beside, ffn_own, memory_blocks
        )
        head_beside += beside((head_near[1], *head_far))
        head_pieces = (head_own, *head_near, *head_far, *head_beside)
        ffn_near = near_chips(ffn_own)
        memory_blocks[2] = shift(memory_blocks[2], 2)
        params = (out_biases, norm_gains, norm_biases)
        dma = pltpu.SemaphoreType.DMA((4, mp))
        squares = VMEM((mp, 2, width, width), BF16)
        weights_shape = VMEM((mp, 4 * local, width), BF16)
        flat_shape = VMEM((slots, width), F32)
        kv_shape = VMEM((mp, 2 * local, mem_slots), BF16)
        row_shape = shaped((slots, width))
        low_shape = shaped((mp, slots, local), BF16)
        head_slots = shaped((8, 2, 4 * local // SUB, width), BF16)
        ffn_slots = shaped((8, 2, 2 * width // SUB, width), BF16)
        matmul = 2 * slots * width * width
        plain = width * width * 2

        def spread_line(rows):
            return [rows] + [shift(rows, step) for step in range(1, mp)]

        def bound(kernel):
            return lambda *refs: kernel(dims, *refs)

        qkv, self_low, z1, first = call(
            bound(self_forward),
            [META] + in_vmem(5) + in_place(12),
            (shaped((mp, slots, 3 * local), BF16), low_shape, row_shape, row_shape),
            [weights_shape, flat_shape, dma],
            20 * matmul,
            8 * plain,
            "self_forward",
        )(meta, hidden_row, self_bias, *params, *head_pieces, own_self, self_proj)
        ffn_own, ffn_near, memory_blocks, qkv, self_low, z1, first = meet(
            ffn_own, ffn_near, memory_blocks, qkv, self_low, z1, first
        )
        ffn_far = far_chips(*ffn_near)
        memory_blocks[3] = shift(memory_blocks[3], 3)
        ffn_far, ffn_beside, memory_blocks, first = meet(
            ffn_far, [swap(ffn_own, 1)], memory_blocks, first
        )
        ffn_beside += [swap(piece, 1) for piece in (*ffn_near, *ffn_far)]
        ffn_pieces = (ffn_own, *ffn_near, *ffn_far, *ffn_beside)
        cross_q, kv, cross_low, cross_total, z2, second = call(
            bound(cross_forward),
            [META] + in_vmem(5) + in_place(mp + 13),
            (
                low_shape,
                shaped((mp, 2 * local, mem_slots), BF16),
                low_shape,
                shaped((mp * heads, slots, 1)),
                row_shape,
                row_shape,
            ),
            [weights_shape, VMEM((width, mem_slots), BF16), flat_shape, dma],
            40 * matmul,
            8 * plain,
            "cross_forward",
        )(
            meta,
            cross_bias,
            *params,
            first,
            *memory_blocks,
            *head_pieces,
            own_cq,
            cross_proj,
            own_kv,
        )
        shared_shape = (mp + 1, slots, width + width // 2)
        result, dz2, ffn_sums, ffn_shared, ffn_half = call(
            bound(ffn_both),
            [META] + in_vmem(7) + in_place(12),
            (
                shaped((slots, width), BF16),
                row_shape,
                shaped((16, width)),
                shaped(shared_shape, BF16),
                shaped((mp + 1, slots, width // 2), BF16),
            ),
            [
                VMEM((mp, width, inner), BF16),
                VMEM((mp, inner, width), BF16),
                flat_shape,
                VMEM((mp, slots, inner), BF16),
                VMEM((mp, slots, inner), F32),
                VMEM((slots, width), BF16),
                dma,
            ],
            40 * matmul,
            10 * plain,
            "ffn_both",
        )(meta, second, z2, grad_row, inner_bias, *params, *ffn_pieces, ffn_in, ffn_out)
        ffn_theirs = swap(ffn_shared, 1)
        result_blocks = spread_line(result)
        *memory_grads, kv_low, cross_dq, dz1, cross_sums, cross_local = call(
            bound(cross_back),
            [META] + in_vmem(5) + in_place(14),
            (
                *[shaped((local, mem_slots), BF16)] * mp,
                shaped((mp, 2 * local, mem_slots), BF16),
                low_shape,
                row_shape,
                shaped((8, width)),
                shaped((mp, 2, local)),
            ),
            [
                weights_shape,
                kv_shape,
                VMEM((width, mem_slots), F32),
                flat_shape,
                VMEM((slots, local), BF16),
                dma,
            ],
            50 * matmul,
            12 * plain,
            "cross_back",
        )(
            meta,
            dz2,
            cross_q,
            cross_total,
            z1,
            norm_gains,
            kv,
            *head_pieces,
            own_cq,
            cross_proj,
            own_kv,
        )
        result_blocks, memory_grads, kv_low, dz1, ffn_theirs = meet(
            result_blocks, memory_grads, kv_low, dz1, ffn_theirs
        )
        memory_out = [memory_grads[0]]
        memory_out += [shift(memory_grads[step], step) for step in (1, 2)]
        pair_slots = shaped((2, 2, 2 * width // SUB, width), BF16)
        to_two, to_four, ffn_rest = call(
            bound(ffn_weights),
            [META] + in_place(3),
            (pair_slots, pair_slots, shaped((4, 2, 2 * width // SUB, width), BF16)),
            [
                VMEM((mp + 1, 2 * slots, width + width // 2), BF16),
                VMEM((mp, 2, width // 2, width), BF16),
                dma,
            ],
            16 * matmul,
            8 * plain,
            "ffn_weights",
            3,
        )(meta, ffn_shared, ffn_half, ffn_theirs)
        ffn_from = swap(to_two, 2), swap(to_four, 4)
        dz1 = after(dz1, to_two)
        hidden_grad, small, head_beside, head_mine = call(
            bound(head_back),
            [META] + in_vmem(11) + in_place(mp + 13),
            (row_shape, shaped((24, width)), ffn_slots, ffn_slots),
            [
                weights_shape,
                kv_shape,
                VMEM((width, mem_slots), BF16),
                flat_shape,
                VMEM((slots, local), BF16),
                VMEM((slots, 3 * local), BF16),
                squares,
                VMEM((mp, 2, local), F32),
                dma,
            ],
            60 * matmul,
            24 * plain,
            "head_back",
            2,
        )(
            meta,
            dz1,
            hidden_row,
            qkv,
            self_low,
            dz2,
            first,
            cross_dq,
            cross_low,
            cross_sums,
            cross_local,
            ffn_sums,
            kv_low,
            *memory_blocks,
            *head_pieces,
            own_self,
            self_proj,
        )
        ffn_from, memory_out, memory_last, hidden_grad, small, head_beside, head_mine = meet(
            ffn_from, memory_out, memory_grads[3], hidden_grad, small, head_beside, head_mine
        )
        head_other = swap(head_beside, 1)
        ffn_group = Group(lambda slot, *at: ffn_rest[(slot - 4, *at)].astype(F32))
        late_two, late_four = ffn_group.second(*ffn_from)
        ffn_late = swap(late_two, 2), swap(late_four, 4)
        memory_out.append(shift(memory_last, 3))
        small = small + flip(small, 1)
        head_other, ffn_late, memory_out, small = meet(head_other, ffn_late, memory_out, small)
        ffn_total, ffn_blocks = ffn_group.third(*ffn_from, *ffn_late)

        def head_summed(*slots):
            return head_mine[slots].astype(F32) + head_other[slots].astype(F32)

        head_group = Group(head_summed)
        head_from = (
            swap(head_summed(slice(0, 2)).astype(BF16), 2),
            swap(head_summed(slice(2, 4)).astype(BF16), 4),
        )
        ffn_sent = [shift(ffn_blocks[step - 1], -step) for step in range(1, mp)]

        def joined(kernel, blocks, shape, dtype, name):
            return call(
                kernel, [META] + in_vmem(mp), (shaped(shape, dtype),), [], 0, 2 * plain, name
            )(meta, *blocks)[0]

        rows_shape = (mp * slots, width)
        memory_grad = joined(
            join_columns, memory_out, (local, mp * mem_slots), F32, "join_memory"
        )
        result = joined(join_rows, result_blocks, rows_shape, BF16, "join_result")
        head_from, ffn_sent, memory_grad, result, hidden_grad = meet(
            head_from, ffn_sent, memory_grad, result, hidden_grad
        )
        late_two, late_four = head_group.second(*head_from)
        head_late = swap(late_two, 2), swap(late_four, 4)
        bit = 2
        while bit < mp:
            small = small + flip(small, bit)
            bit *= 2
        ffn_low = line_sum(ffn_total, ffn_sent)
        small = small + swap(small, 1)
        bit = SUB
        while bit < dp:
            small = small + swap(small, bit)
            bit *= 2
        head_late, ffn_low, small = meet(head_late, ffn_low, small)
        head_total, head_blocks = head_group.third(*head_from, *head_late)
        head_sent = [shift(head_blocks[step - 1], -step) for step in range(1, mp)]
        ffn_near = near_chips(ffn_low)
        small, *ffn_near = meet(small, *ffn_near)
        small = small + swap(small, 2)
        small = small + swap(small, 4)
        ffn_near[0], _ = meet(ffn_near[0], head_sent[0])
        ffn_far = far_chips(*ffn_near)
        hidden_low = hidden_grad.astype(BF16)
        ffn_reduced = (ffn_low, *ffn_near, *ffn_far)
        ffn_joined = jnp.concatenate(ffn_reduced)
        head_sent, ffn_reduced, ffn_joined, small, hidden_low = meet(
            head_sent, ffn_reduced, ffn_joined, small, hidden_low
        )
        head_low = line_sum(head_total, head_sent)
        head_near = near_chips(head_low)
        hidden_blocks = [hidden_low, shift(hidden_low, 1), None, shift(hidden_low, 3)]
        ffn_joined = swap(ffn_joined, 1)
        head_near, ffn_joined, hidden_blocks = meet(head_near, ffn_joined, hidden_blocks)
        grad_in, grad_out = call(
            finish_ffn,
            [META] + in_vmem(6),
            (shaped((width, inner)), shaped((inner, width))),
            [],
            0,
            plain,
            "finish_ffn",
        )(meta, *ffn_reduced, ffn_joined)
        hidden_blocks[2] = shift(hidden_blocks[0], 2)
        head_far = far_chips(*head_near)
        head_beside = [swap(piece, 1) for piece in (head_low, *head_near)]
        head_far, head_beside, grad_in, grad_out, hidden_blocks = meet(
            head_far, head_beside, grad_in, grad_out, hidden_blocks
        )
        hidden_grad = joined(join_rows, hidden_blocks, rows_shape, F32, "join_hidden")
        head_beside += [swap(piece, 1) for piece in head_far]
        finished = call(
            finish_heads,
            [META] + in_vmem(11),
            (
                shaped((3 * local, width)),
                shaped((local, width)),
                shaped((local, width)),
                shaped((local, width)),
                shaped((2 * local, width)),
                shaped((3, width)),
                shaped((3, width)),
                shaped((3, width)),
                shaped((2, local)),
                shaped((2, local)),
                shaped((inner,)),
            ),
            [],
            0,
            plain,
            "finish_heads",
        )(meta, small, head_low, *head_near, *head_far, *head_beside)
        grad_self, grad_sp, grad_cq, grad_cp, grad_kv = finished[:5]
        return (
            result,
            hidden_grad,
            memory_grad.T,
            jnp.swapaxes(grad_self.reshape(3, local, width), 1, 2),
            finished[8],
            grad_sp,
            grad_cq.T,
            jnp.swapaxes(grad_kv.reshape(2, local, width), 1, 2),
            finished[9],
            grad_cp,
            grad_in,
            finished[10],
            grad_out,
            *finished[5:8],
        )

    return jax.shard_map(
        body,
        mesh=mesh,
        in_specs=(
            P("dp", None),
            P("dp", "mp"),
            P("dp", None),
            P("dp", None),
            P("dp"),
            P("dp", None),
            P("dp"),
            P(None, None, "mp"),
            P(None, "mp"),
            P("mp", None),
            P(None, "mp"),
            P(None, None, "mp"),
            P(None, "mp"),
            P("mp", None),
            P(None, "mp"),
            P("mp"),
            P("mp", None),
            P(),
            P(),
            P(),
        ),
        out_specs=(
            P("dp", None),
            P("dp", None),
            P("dp", "mp"),
            P(None, None, "mp"),
            P(None, "mp"),
            P("mp", None),
            P(None, "mp"),
            P(None, None, "mp"),
            P(None, "mp"),
            P("mp", None),
            P(None, "mp"),
            P("mp"),
            P("mp", None),
            P(),
            P(),
            P(),
        ),
        check_vma=False,
    )
```

```python
import jax
import jax.numpy as jnp
from jax import lax
from jax.experimental import pallas as pl
from jax.experimental.pallas import tpu as pltpu
from jax.sharding import PartitionSpec as P

HD = 64
SUB = 8
NEG_FILL = -1000000000.0
EPSILON = 1e-05
F32 = jnp.float32
BF16 = jnp.bfloat16
VMEM = pltpu.VMEM
ROOT_HALF = 0.7071067811865476
ROOT_TWO_PI = 0.3989422804014327
SLOTS = ((3, 0), (1, 0), (3, 1), (2, 1), (1, 1), (2, 0), (0, 0), (0, 1))


def nn(left, right):
    return lax.dot_general(left, right, (((1,), (0,)), ((), ())), preferred_element_type=F32)


def nt(left, right):
    return lax.dot_general(left, right, (((1,), (1,)), ((), ())), preferred_element_type=F32)


def tn(left, right):
    return lax.dot_general(left, right, (((0,), (0,)), ((), ())), preferred_element_type=F32)


def normed(values):
    average = jnp.mean(values, -1, keepdims=True)
    centered = values - average
    variance = jnp.mean(centered * centered, -1, keepdims=True)
    inverse = lax.rsqrt(variance + EPSILON)
    return centered * inverse, inverse


def norm_back(unit, inverse, gain, grad):
    scaled = grad * gain
    return (
        scaled
        - jnp.mean(scaled, -1, keepdims=True)
        - unit * jnp.mean(scaled * unit, -1, keepdims=True)
    ) * inverse


def row_sum(values):
    return jnp.sum(values, 0, keepdims=True)


def segments(meta, start, count, shape, axis):
    places = lax.broadcasted_iota(jnp.int32, shape, axis)
    found = jnp.zeros(shape, jnp.int32) - 1
    for j in range(count):
        found = found + (meta[start + j] <= places).astype(jnp.int32)
    return found, places


def fetch(pieces, place, target, low, high, sems):
    size = high - low
    blocks, rows = pieces[0].shape[:2]
    half = rows // 2
    for block in range(blocks):
        sem = sems.at[block + 1]
        for beside in (0, 1):
            whole = pieces[5 * beside : 5 * beside + 3]
            split = pieces[5 * beside + 3 : 5 * beside + 5]
            for offset in range(4):
                row = (place ^ (offset + 4 * beside)) * size
                if offset < 3:
                    source = whole[offset].at[block, pl.ds(low, size)]
                    to = target.at[block + 1, pl.ds(pl.multiple_of(row, 16), size)]
                    pltpu.make_async_copy(source, to, sem).start()
                    continue
                for part in range(low // half, high // half):
                    at = 2 * block + part
                    source = split[at // blocks].at[at % blocks]
                    start = pl.multiple_of(row + part * half - low, 16)
                    to = target.at[block + 1, pl.ds(start, half)]
                    pltpu.make_async_copy(source, to, sem).start()


def fetch_own(sources, target, sems):
    row = 0
    for source in sources:
        size = source.shape[0]
        pltpu.make_async_copy(source, target.at[0, pl.ds(row, size)], sems.at[0]).start()
        row += size


def arrive(target, sem):
    pltpu.make_async_copy(target, target, sem).wait()


def fetch_halves(pieces, owns, place, target, sems):
    own_cq, own_cp, own_kv = owns
    size = own_cq.shape[0]
    pltpu.make_async_copy(own_cq, target.at[0, 0, pl.ds(0, size)], sems.at[0, 0]).start()
    pltpu.make_async_copy(own_cp, target.at[0, 0, pl.ds(size, size)], sems.at[0, 0]).start()
    pltpu.make_async_copy(own_kv, target.at[1, 0], sems.at[1, 0]).start()
    blocks, rows = pieces[0].shape[:2]
    size = rows // 2
    for block in range(blocks):
        for index in range(8):
            offset = index % 4
            mine = pieces[5 * (index // 4) :]
            position = place ^ index
            plane = lax.div(position, 4)
            row = pl.multiple_of(lax.rem(position, 4) * size, 16)
            if offset < 3:
                source = mine[offset].at[block, pl.ds(size, size)]
            else:
                at = 2 * block + 1
                source = mine[3 + at // blocks].at[at % blocks]
            to = target.at[plane, block + 1, pl.ds(row, size)]
            pltpu.make_async_copy(source, to, sems.at[plane, block + 1]).start()


def fetch_memory(blocks, line, target, sem):
    count = len(blocks)
    for step, block in enumerate(blocks):
        size = block.shape[0]
        row = pl.multiple_of(lax.rem(line + count - step, count) * size, 16)
        pltpu.make_async_copy(block, target.at[pl.ds(row, size)], sem).start()


def slot_of(offset, half):
    first = SLOTS.index((offset, 0))
    second = SLOTS.index((offset, 1))
    return jnp.where(half == 0, first, second)


def self_mask(meta, nseg, slots):
    shape = (slots, slots)
    query_segment, query_place = segments(meta, 4, nseg, shape, 0)
    key_segment, key_place = segments(meta, 4, nseg, shape, 1)
    return (query_segment == key_segment) & (key_place <= query_place) & (key_place < meta[2])


def self_forward(dims, meta, x_ref, sb, ob, gain, bias, *refs):
    mp, local, heads, scaling, nseg = dims
    pieces, (own_self, own_sp) = refs[:10], refs[10:12]
    qkv, low, z1, first = refs[12:16]
    ws, acc, sems = refs[16:]
    fetch_own((own_self, own_sp), ws, sems.at[0])
    fetch(pieces, meta[0], ws, 0, 96, sems.at[0])
    allowed = self_mask(meta, nseg, x_ref.shape[0])
    acc[...] = x_ref[...].astype(F32) + ob[0:1]

    def step(z, carry):
        arrive(ws.at[z], sems.at[0, z])
        flat = nt(x_ref[...], ws[z, : 3 * local])
        rows = sb[z]
        qkv[z, :, :local] = ((flat[:, :local] + rows[0:1]) * scaling).astype(BF16)
        qkv[z, :, local : 2 * local] = flat[:, local : 2 * local].astype(BF16)
        qkv[z, :, 2 * local :] = (flat[:, 2 * local :] + rows[1:2]).astype(BF16)
        for i in range(heads):
            at = HD * i
            scores = nt(qkv[z, :, at : at + HD], qkv[z, :, local + at : local + at + HD])
            scores = jnp.where(allowed, scores, NEG_FILL)
            weights = jnp.exp(scores - jnp.max(scores, -1, keepdims=True))
            probs = (weights * (1.0 / jnp.sum(weights, -1, keepdims=True))).astype(BF16)
            out = nn(probs, qkv[z, :, 2 * local + at : 2 * local + at + HD])
            low[z, :, at : at + HD] = out.astype(BF16)
        acc[...] += nn(low[z], ws[z, 3 * local :])
        return carry

    lax.fori_loop(0, mp, step, 0)
    z1[...] = acc[...]
    unit, _ = normed(acc[...])
    first[...] = unit * gain[0:1] + bias[0:1]


def put_heads(target, source, heads):
    rows = source.shape[0]
    for i in range(heads):
        columns = slice(HD * i, HD * (i + 1))
        target[rows * i : rows * (i + 1), columns] = source[:, columns]


def masked(scores, allowed):
    shape = scores.shape
    scores = scores.reshape((-1,) + allowed.shape)
    return jnp.where(allowed[None], scores, NEG_FILL).reshape(shape)


def cross_mask(meta, nseg, slots, mem_slots):
    query_segment, _ = segments(meta, 4, nseg, (slots, 1), 0)
    key_segment, key_place = segments(meta, 4 + nseg, nseg, (1, mem_slots), 1)
    key_segment = jnp.where(key_place < meta[3], key_segment, -1)
    return query_segment == key_segment


def fetch_cross(pieces, owns, place, target, sem):
    fetch_own(owns, target, sem)
    fetch(pieces, place, target, 96, 192, sem)


def cross_forward(dims, meta, cb, ob, gain, bias, first, *refs):
    mp, local, heads, scaling, nseg = dims
    blocks, pieces, owns = refs[:mp], refs[mp : mp + 10], refs[mp + 10 : mp + 13]
    cq, low, total, z2, second, kv = refs[mp + 13 : mp + 19]
    wc, mem, acc, stacked, both, sems = refs[mp + 19 :]
    fetch_memory(blocks, meta[1], mem, sems.at[1, 0])
    fetch_cross(pieces, owns, meta[0], wc, sems.at[0])
    slots = first.shape[0]
    allowed = cross_mask(meta, nseg, slots, mem.shape[1])
    acc[...] = first[...] + ob[1:2]
    stacked[...] = jnp.zeros_like(stacked)
    first_low = first[...].astype(BF16)
    arrive(mem, sems.at[1, 0])

    def step(z, carry):
        arrive(wc.at[z], sems.at[0, z])
        rows = cb[z]
        query = ((nt(first_low, wc[z, :local]) + rows[0:1]) * scaling).astype(BF16)
        cq[z] = query
        put_heads(stacked, query, heads)
        flat = nn(wc[z, 2 * local :], mem[...])
        column = jnp.swapaxes(jnp.broadcast_to(rows[1:2], (8, local)), 0, 1)[:, :1]
        keys = flat[:local].astype(BF16)
        values = (flat[local:] + column).astype(BF16)
        both[z, :local] = keys
        both[z, local:] = values
        pltpu.make_async_copy(both.at[z], kv.at[z], sems.at[2, 0]).start()
        scores = masked(nn(stacked[...], keys), allowed)
        peak = jnp.max(scores, -1, keepdims=True)
        weights = jnp.exp(scores - peak)
        mass = jnp.sum(weights, -1, keepdims=True)
        probs = (weights * (1.0 / mass)).astype(BF16)
        total[z] = peak + jnp.log(mass)
        out = nt(probs, values)
        for i in range(heads):
            columns = slice(HD * i, HD * (i + 1))
            low[z, :, columns] = out[slots * i : slots * (i + 1), columns].astype(BF16)
        acc[...] += nn(low[z], wc[z, local : 2 * local])
        return carry

    lax.fori_loop(0, mp, step, 0)
    z2[...] = acc[...]
    unit, _ = normed(acc[...])
    second[...] = unit * gain[1:2] + bias[1:2]
    arrive(both, sems.at[2, 0])


def put_slots(beside, mine, place, z, base, source, sem):
    half = lax.div(z, 2)
    at = lax.rem(z, 2)
    size = source.shape[0] // SUB
    for offset in range(4):
        slot = slot_of(offset, half)
        for target, flip in ((mine, 0), (beside, 4)):
            row = pl.multiple_of((place ^ (offset + flip)) * size, 16)
            to = target.at[slot, at, pl.ds(base, size)]
            pltpu.make_async_copy(source.at[pl.ds(row, size)], to, sem).start()


def ffn_both(dims, meta, second, z2, grad, ib, ob, gain, bias, *refs):
    mp, local, heads, scaling, nseg = dims
    pieces, (own_in, own_out) = refs[:10], refs[10:12]
    result, dz2, sums, shared, own_half = refs[12:17]
    win, wout, acc, act, slope, low, sems = refs[17:]
    place = meta[0]
    width = second.shape[1]
    half = width // 2
    mine = pl.multiple_of(lax.div(place, 4) * half, 128)
    other = pl.multiple_of((1 - lax.div(place, 4)) * half, 128)
    fetch_own((own_in,), win, sems.at[0])
    fetch_own((own_out,), wout, sems.at[1])
    fetch(pieces, place, win, 0, 96, sems.at[0])
    fetch(pieces, place, wout, 96, 192, sems.at[1])
    acc[...] = second[...] + ob[2:3]
    low[...] = second[...].astype(BF16)
    own_half[0] = low[:, pl.ds(mine, half)]
    shared[0, :, width:] = low[:, pl.ds(other, half)]

    def forward(z, carry):
        arrive(win.at[z], sems.at[0, z])
        arrive(wout.at[z], sems.at[1, z])
        inner = nn(low[...], win[z]) + ib[z]
        share = 0.5 * (1.0 + lax.erf(inner * ROOT_HALF))
        act[z] = (inner * share).astype(BF16)
        own_half[z + 1] = act[z, :, pl.ds(mine, half)]
        shared[z + 1, :, width:] = act[z, :, pl.ds(other, half)]
        slope[z] = share + inner * (ROOT_TWO_PI * jnp.exp(-0.5 * inner * inner))
        acc[...] += nn(act[z], wout[z])
        return carry

    lax.fori_loop(0, mp, forward, 0, unroll=True)
    unit, inverse = normed(acc[...])
    result[...] = (unit * gain[2:3] + bias[2:3]).astype(BF16)
    out_grad = grad[...].astype(F32)
    third = norm_back(unit, inverse, gain[2:3], out_grad)
    sums[...] = jnp.zeros_like(sums)
    sums[0:1] = row_sum(third)
    sums[1:2] = row_sum(out_grad * unit)
    sums[2:3] = row_sum(out_grad)
    third_low = third.astype(BF16)
    shared[0, :, :width] = third_low
    acc[...] = third

    def backward(z, carry):
        inner = nt(third_low, wout[z]) * slope[z]
        sums[pl.ds(8 + z, 1)] = row_sum(inner)
        inner_low = inner.astype(BF16)
        acc[...] += nt(inner_low, win[z])
        shared[z + 1, :, :width] = inner_low
        return carry

    lax.fori_loop(0, mp, backward, 0, unroll=True)
    unit, inverse = normed(z2[...])
    grad_rows = acc[...]
    values = norm_back(unit, inverse, gain[1:2], grad_rows)
    dz2[...] = values
    sums[3:4] = row_sum(values)
    sums[4:5] = row_sum(grad_rows * unit)
    sums[5:6] = row_sum(grad_rows)


def ffn_weights(dims, meta, shared, own_half, theirs, to_two, to_four, rest, rows, dw, sems):
    mp = dims[0]
    slots = shared.shape[1]
    width = rows.shape[2] - own_half.shape[2]
    for i in range(mp + 1):
        sem = sems.at[i % mp, i // mp]
        part = rows.at[i, pl.ds(0, slots)]
        pltpu.make_async_copy(shared.at[i, :, pl.ds(0, width)], part.at[:, pl.ds(0, width)], sem).start()
        pltpu.make_async_copy(own_half.at[i], part.at[:, pl.ds(width, width // 2)], sem).start()
        pltpu.make_async_copy(theirs.at[i], rows.at[i, pl.ds(slots, slots)], sem).start()
    arrive(rows.at[0], sems.at[0, 0])
    for z in range(mp):
        i = z + 1
        arrive(rows.at[i], sems.at[i % mp, i // mp])
        dw[z, 0] = tn(rows[0, :, width:], rows[i, :, :width]).astype(BF16)
        dw[z, 1] = tn(rows[i, :, width:], rows[0, :, :width]).astype(BF16)
        size = dw.shape[2] // 4
        for offset in range(4):
            slot = SLOTS.index((offset, z // 2))
            if slot < 4:
                target = (to_two, to_four)[slot // 2].at[slot % 2, z % 2]
            else:
                target = rest.at[slot - 4, z % 2]
            row = pl.multiple_of(((meta[0] ^ offset) & 3) * size, 16)
            for j in (0, 1):
                source = dw.at[z, j, pl.ds(row, size)]
                pltpu.make_async_copy(source, target.at[pl.ds(j * size, size)], sems.at[0, 2]).start()
    arrive(dw, sems.at[0, 2])


def cross_back(dims, meta, dz2, cq, total, z1, gain, *refs):
    mp, local, heads, scaling, nseg = dims
    kv_ref, pieces, owns = refs[0], refs[1:11], refs[11:14]
    dcq, dz1, sums, sums_local, kv_low = refs[14:19]
    mem_out = refs[19 : 19 + mp]
    wc, kv, kv_grad, dmem, acc, queries, grads, sems = refs[19 + mp :]
    for z in range(mp):
        pltpu.make_async_copy(kv_ref.at[z], kv.at[z], sems.at[2, z]).start()
    fetch_halves(pieces, owns, meta[0], wc, sems)
    slots = dz2.shape[0]
    allowed = cross_mask(meta, nseg, slots, kv.shape[2])
    queries[...] = jnp.zeros_like(queries)
    grads[...] = jnp.zeros_like(grads)
    dz2_low = dz2[...].astype(BF16)
    acc[...] = dz2[...]

    def step(z, carry):
        arrive(wc.at[0, z], sems.at[0, z])
        arrive(wc.at[1, z], sems.at[1, z])
        arrive(kv.at[z], sems.at[2, z])
        put_heads(queries, cq[z], heads)
        grad = nt(dz2_low, wc[0, z, local:]).astype(BF16)
        put_heads(grads, grad, heads)
        keys, values = kv[z, :local], kv[z, local:]
        probs = jnp.exp(masked(nn(queries[...], keys), allowed) - total[z])
        probs_low = probs.astype(BF16)
        prob_grad = nn(grads[...], values)
        offset = jnp.sum(probs * prob_grad, -1, keepdims=True)
        score_grad = (probs * (prob_grad - offset)).astype(BF16)
        kv_grad[z, :local] = tn(queries[...], score_grad).astype(BF16)
        kv_grad[z, local:] = tn(grads[...], probs_low).astype(BF16)
        pltpu.make_async_copy(kv_grad.at[z], kv_low.at[z], sems.at[3, 0]).start()
        mass = jnp.sum(probs_low.astype(F32), -1, keepdims=True)
        query_grad = nt(score_grad, keys) * scaling
        for i in range(heads):
            columns = slice(HD * i, HD * (i + 1))
            rows = slice(slots * i, slots * (i + 1))
            part = query_grad[rows, columns]
            dcq[z, :, columns] = part.astype(BF16)
            sums_local[z, 0:1, columns] = row_sum(part)
            sums_local[z, 1:2, columns] = row_sum(mass[rows] * grad[:, columns].astype(F32))
        acc[...] += nn(dcq[z], wc[0, z, :local])
        return carry

    lax.fori_loop(0, mp, step, 0)
    depth = mp * kv_grad.shape[1]
    product = tn(wc[1].reshape(depth, wc.shape[3]), kv_grad[...].reshape(depth, kv.shape[2]))
    dmem[...] = product.astype(BF16)
    for block in range(mp):
        row = pl.multiple_of(lax.rem(meta[1] + block, mp) * local, 16)
        source = dmem.at[pl.ds(row, local)]
        pltpu.make_async_copy(source, mem_out[block], sems.at[3, 1]).start()
    unit, inverse = normed(z1[...])
    grad_rows = acc[...]
    values = norm_back(unit, inverse, gain[0:1], grad_rows)
    dz1[...] = values
    sums[...] = jnp.zeros_like(sums)
    sums[0:1] = row_sum(values)
    sums[1:2] = row_sum(grad_rows * unit)
    sums[2:3] = row_sum(grad_rows)
    arrive(kv_grad, sems.at[3, 0])
    arrive(dmem, sems.at[3, 1])


def head_back(dims, meta, dz1, x_ref, qkv, self_low, dz2, first, dcq, cross_low, *refs):
    mp, local, heads, scaling, nseg = dims
    cross_sums, cross_local, ffn_sums = refs[:3]
    refs = refs[3:]
    kv_ref, blocks, pieces = refs[0], refs[1 : 1 + mp], refs[1 + mp : 11 + mp]
    own_self, own_sp = refs[11 + mp : 13 + mp]
    dx, small, beside, mine = refs[13 + mp : 17 + mp]
    ws, kv, mem, acc, dout, dqkv, dw, sums_local, sems = refs[17 + mp :]
    place = meta[0]
    fetch_own((own_self, own_sp), ws, sems.at[0])
    fetch(pieces, place, ws, 0, 96, sems.at[0])
    fetch_memory(blocks, meta[1], mem, sems.at[2, 0])
    for z in range(mp):
        pltpu.make_async_copy(kv_ref.at[z], kv.at[z], sems.at[1, z]).start()
    allowed = self_mask(meta, nseg, x_ref.shape[0])
    dz1_low = dz1[...].astype(BF16)
    dz2_low = dz2[...].astype(BF16)
    first_low = first[...].astype(BF16)
    acc[...] = dz1[...]
    arrive(mem, sems.at[2, 0])

    def step(z, carry):
        arrive(ws.at[z], sems.at[0, z])
        arrive(kv.at[z], sems.at[1, z])
        dout[...] = nt(dz1_low, ws[z, 3 * local :]).astype(BF16)
        for i in range(heads):
            at = HD * i
            query = qkv[z, :, at : at + HD]
            key = qkv[z, :, local + at : local + at + HD]
            value = qkv[z, :, 2 * local + at : 2 * local + at + HD]
            grad = dout[:, at : at + HD]
            scores = jnp.where(allowed, nt(query, key), NEG_FILL)
            weights = jnp.exp(scores - jnp.max(scores, -1, keepdims=True))
            probs = weights * (1.0 / jnp.sum(weights, -1, keepdims=True))
            prob_grad = nt(grad, value)
            offset = jnp.sum(probs * prob_grad, -1, keepdims=True)
            score_grad = (probs * (prob_grad - offset)).astype(BF16)
            value_grad = tn(probs.astype(BF16), grad)
            query_grad = nn(score_grad, key) * scaling
            dqkv[:, at : at + HD] = query_grad.astype(BF16)
            dqkv[:, local + at : local + at + HD] = tn(score_grad, query).astype(BF16)
            dqkv[:, 2 * local + at : 2 * local + at + HD] = value_grad.astype(BF16)
            sums_local[z, 0:1, at : at + HD] = row_sum(query_grad)
            sums_local[z, 1:2, at : at + HD] = row_sum(value_grad)
        acc[...] += nn(dqkv[...], ws[z, : 3 * local])
        dw[z, 0, : 3 * local] = tn(dqkv[...], x_ref[...]).astype(BF16)
        dw[z, 0, 3 * local :] = tn(self_low[z], dz1_low).astype(BF16)
        put_slots(beside, mine, place, z, 0, dw.at[z, 0], sems.at[3, 0])
        dw[z, 1, :local] = tn(dcq[z], first_low).astype(BF16)
        dw[z, 1, local : 2 * local] = tn(cross_low[z], dz2_low).astype(BF16)
        dw[z, 1, 2 * local :] = nt(kv[z], mem[...]).astype(BF16)
        put_slots(beside, mine, place, z, 96, dw.at[z, 1], sems.at[3, 0])
        return carry

    lax.fori_loop(0, mp, step, 0)
    dx[...] = acc[...]
    small[...] = jnp.zeros_like(small)
    small[0:3] = cross_sums[0:3]
    small[3:9] = ffn_sums[0:6]

    def collect(z, carry):
        row = 9 + 2 * lax.rem(meta[1] + mp - z, mp)
        for i, part in enumerate((sums_local, cross_local)):
            for j in (0, 1):
                at = (2 * i + j) * local
                small[pl.ds(row, 1), at : at + local] = part[z, j : j + 1]
        small[pl.ds(row + 1, 1)] = ffn_sums[pl.ds(8 + z, 1)]
        return carry

    lax.fori_loop(0, mp, collect, 0)
    arrive(dw, sems.at[3, 0])


def place_rows(place, ranges, pieces):
    half = pieces[3].shape[0]

    def taken(offset, start, size):
        mine = pieces[5 * (offset // 4) :]
        offset = offset % 4
        if offset < 3:
            return mine[offset][pl.ds(start, size)]
        if start < half:
            return mine[3][pl.ds(start, size)]
        return mine[4][pl.ds(start - half, size)]

    for offset in range(8):
        position = place ^ offset
        for start, size, targets in ranges:
            if offset % 4 == 3 and start < half < start + size:
                parts = ((start, half - start), (half, start + size - half))
            else:
                parts = ((start, size),)
            for begin, length in parts:
                source = taken(offset, begin, length).astype(F32)
                first = 0
                for target in targets:
                    count = target.shape[0] // size

                    @pl.when((position >= first) & (position < first + count))
                    def _():
                        row = (position - first) * size + (begin - start)
                        target[pl.ds(pl.multiple_of(row, 8), length)] = source

                    first += count


def finish_heads(meta, small, *refs):
    place_rows(meta[0], ((0, 96, refs[10:12]), (96, 96, refs[12:15])), refs[:10])
    shared, sharded = refs[15:18], refs[18:]
    for i, target in enumerate(shared):
        for j, row in enumerate((0, 6, 3)):
            target[j : j + 1] = small[row + i : row + i + 1]
    row = 9 + 2 * meta[1]
    local = sharded[0].shape[1]
    for i in (0, 1):
        for j in (0, 1):
            at = (2 * i + j) * local
            sharded[i][j : j + 1] = small[pl.ds(row, 1), at : at + local]
    sharded[2][...] = small[pl.ds(row + 1, 1)].reshape(sharded[2].shape)


def finish_ffn(meta, *refs):
    gi, go = refs[6:]
    pieces, joined = list(refs[:5]), refs[5]
    row = 0
    for piece in refs[:5]:
        pieces.append(joined.at[pl.ds(row, piece.shape[0])])
        row += piece.shape[0]
    place_rows(meta[0], ((0, 96, (gi,)), (96, 96, (go,))), pieces)


def add_slots(mine, other, to_two, to_four, left, right, out, sems):
    count = out.shape[0]
    for i in range(count):
        pltpu.make_async_copy(mine.at[i], left.at[i], sems.at[0, i]).start()
        pltpu.make_async_copy(other.at[i], right.at[i], sems.at[1, i]).start()
    for i in range(count):
        arrive(left.at[i], sems.at[0, i])
        arrive(right.at[i], sems.at[1, i])
        out[i] = (left[i].astype(F32) + right[i].astype(F32)).astype(BF16)
        target = (to_two, to_four)[i // 2].at[i % 2]
        pltpu.make_async_copy(out.at[i], target, sems.at[2, 0]).start()
    arrive(out, sems.at[2, 0])


def join_columns(meta, *refs):
    blocks, target = refs[:-1], refs[-1]
    count = len(blocks)
    for step, block in enumerate(blocks):
        size = block.shape[1]
        at = pl.multiple_of(lax.rem(meta[1] + count - step, count) * size, 128)
        target[:, pl.ds(at, size)] = block[...].astype(target.dtype)


def join_rows(meta, *refs):
    blocks, target = refs[:-1], refs[-1]
    count = len(blocks)
    for step, block in enumerate(blocks):
        size = block.shape[0]
        at = pl.multiple_of(lax.rem(meta[1] + count - step, count) * size, 16)
        target[pl.ds(at, size)] = block[...].astype(target.dtype)


def shaped(shape, dtype=F32):
    return jax.ShapeDtypeStruct(shape, dtype)


def in_vmem(count):
    return [pl.BlockSpec(memory_space=pltpu.VMEM)] * count


def in_place(count):
    return [pl.BlockSpec(memory_space=pl.ANY)] * count


META = pl.BlockSpec(memory_space=pltpu.SMEM)


def call(kernel, in_specs, outs, scratch, flops, moved, name, written=0):
    return pl.pallas_call(
        kernel,
        out_shape=outs,
        in_specs=in_specs,
        out_specs=in_vmem(len(outs) - written) + in_place(written),
        scratch_shapes=scratch,
        name=name,
        compiler_params=pltpu.CompilerParams(vmem_limit_bytes=60 * 1024 * 1024),
        cost_estimate=pl.CostEstimate(
            flops=flops // 16, bytes_accessed=moved // 4, transcendentals=0
        ),
    )


def solution(mesh):
    dp = mesh.shape["dp"]
    mp = mesh.shape["mp"]

    def swap(value, bit):
        return lax.ppermute(value, "dp", [(i, i ^ bit) for i in range(dp)])

    def shift(value, step):
        return lax.ppermute(value, "mp", [(i, (i + step) % mp) for i in range(mp)])

    def flip(value, bit):
        return lax.ppermute(value, "mp", [(i, i ^ bit) for i in range(mp)])

    def after(value, *others):
        return lax.optimization_barrier((value,) + others)[0] if others else value

    def meet(*values):
        return lax.optimization_barrier(values)

    def near_chips(own):
        return swap(own, 2), swap(own, 4)

    def far_chips(over_two, over_four):
        def halves(piece):
            if piece.ndim == 3:
                piece = piece.reshape(-1, piece.shape[1] // 2, piece.shape[2])
            half = piece.shape[0] // 2
            return piece[:half], piece[half:]

        return swap(halves(over_four)[0], 2), swap(halves(over_two)[1], 4)

    def beside(pieces):
        found = []
        for piece in pieces:
            found.append(swap(after(piece, *found[-1:]), 1))
        return found

    class Group:
        def __init__(self, summed):
            self.summed = summed

        def second(self, from_two, from_four):
            late_two = (self.summed(4) + from_four[0].astype(F32)).astype(BF16)
            late_four = (self.summed(5) + from_two[0].astype(F32)).astype(BF16)
            return late_two, late_four

        def third(self, from_two, from_four, late_two, late_four):
            blocks = []
            for slot, near, late in ((6, from_two, late_four), (7, from_four, late_two)):
                for i in (0, 1):
                    total = self.summed(slot, i) + near[1, i].astype(F32) + late[i].astype(F32)
                    bit = SUB
                    while bit < dp:
                        total = total + swap(total, bit)
                        bit *= 2
                    blocks.append(total)
            return blocks[0], [block.astype(BF16) for block in blocks[1:]]

    def line_sum(total, sent):
        for piece in sent:
            total = total + piece.astype(F32)
        return total.astype(BF16)

    def body(
        hidden,
        memory,
        out_grad,
        dec_starts,
        dec_length,
        mem_starts,
        mem_length,
        self_qkv,
        self_qv_bias,
        self_proj,
        cross_query,
        cross_kv,
        cross_qv_bias,
        cross_proj,
        ffn_in,
        ffn_in_bias,
        ffn_out,
        out_biases,
        norm_gains,
        norm_biases,
    ):
        row_count = dec_starts.shape[0]
        assert row_count == mp == 4 and dp % SUB == 0
        slots = hidden.shape[0] // row_count
        mem_slots = memory.shape[0] // row_count
        width = hidden.shape[1]
        local = self_proj.shape[0]
        heads = local // HD
        inner = ffn_out.shape[0]
        nseg = dec_starts.shape[1]
        dims = (mp, local, heads, HD ** (-0.5), nseg)
        line = lax.axis_index("mp")
        device = lax.axis_index("dp") % SUB
        place = (device & 1) * 4 + device // 2

        def row_of(array, size):
            return lax.dynamic_slice_in_dim(array, line * size, size, 0)

        def slice_of(array):
            size = array.shape[0] // SUB
            return lax.dynamic_slice_in_dim(array, place * size, size, 0)

        meta = jnp.concatenate(
            [
                jnp.stack([place, line]).astype(jnp.int32),
                row_of(dec_length, 1),
                row_of(mem_length, 1),
                row_of(dec_starts, 1)[0],
                row_of(mem_starts, 1)[0],
            ]
        )
        own_self = jnp.swapaxes(self_qkv, 1, 2).reshape(3 * local, width)
        own_cq = cross_query.T
        own_kv = jnp.swapaxes(cross_kv, 1, 2).reshape(2 * local, width)

        bias = jnp.concatenate(
            [self_qv_bias.reshape(-1), cross_qv_bias.reshape(-1), ffn_in_bias]
        ).reshape(-1, width)
        terms = []
        rest = bias
        for _ in range(3):
            term = lax.reduce_precision(rest, 8, 7)
            terms.append(term.astype(BF16))
            rest = rest - term
        bias_rows = 3 * bias.shape[0]
        terms = jnp.concatenate(terms + [jnp.zeros((16 - bias_rows, width), BF16)])
        head_piece = jnp.concatenate(
            [
                slice_of(jnp.concatenate([own_self, self_proj])),
                slice_of(jnp.concatenate([own_cq, cross_proj, own_kv])),
                terms,
            ]
        )
        ffn_piece = jnp.concatenate([slice_of(ffn_in), slice_of(ffn_out)])
        memory_t = memory.T
        memory_blocks = [
            lax.dynamic_slice_in_dim(memory_t, ((line + step) % mp) * mem_slots, mem_slots, 1)
            for step in range(mp)
        ]
        head_line = [shift(head_piece, step) for step in range(1, mp)]
        rows = head_piece.shape[0] - 16
        head_own = jnp.stack([piece[:rows] for piece in head_line])
        head_near = near_chips(head_own)
        ffn_piece = after(ffn_piece, *head_line)
        ffn_line = [shift(ffn_piece, step) for step in range(1, mp)]
        biases = [bias]
        for piece in head_line:
            term = piece[rows : rows + bias_rows].reshape(3, -1, width).astype(F32)
            biases.append((term[0] + term[1]) + term[2])
        biases = jnp.stack(biases).reshape(mp, -1)
        self_bias = biases[:, : 2 * local].reshape(mp, 2, local)
        cross_bias = biases[:, 2 * local : 4 * local].reshape(mp, 2, local)
        inner_bias = biases[:, None, 4 * local :]
        hidden_row = row_of(hidden, slots)
        grad_row = row_of(out_grad, slots)
        early = (meta, self_bias, cross_bias, inner_bias, hidden_row, grad_row)
        head_own, head_near, ffn_line, memory_blocks, early = meet(
            head_own, head_near, ffn_line, memory_blocks, early
        )
        meta, self_bias, cross_bias, inner_bias, hidden_row, grad_row = early
        head_far = far_chips(*head_near)
        head_beside = [swap(head_own, 1), swap(head_near[0], 1)]
        memory_blocks[1] = shift(memory_blocks[1], 1)
        ffn_own = jnp.stack(ffn_line)
        head_own, head_near, head_far, head_beside, ffn_own, memory_blocks = meet(
            head_own, head_near, head_far, head_beside, ffn_own, memory_blocks
        )
        head_beside += beside((head_near[1], *head_far))
        head_pieces = (head_own, *head_near, *head_far, *head_beside)
        ffn_near = near_chips(ffn_own)
        memory_blocks[2] = shift(memory_blocks[2], 2)
        params = (out_biases, norm_gains, norm_biases)
        dma = pltpu.SemaphoreType.DMA((4, mp))
        squares = VMEM((mp, 2, width, width), BF16)
        weights_shape = VMEM((mp, 4 * local, width), BF16)
        flat_shape = VMEM((slots, width), F32)
        kv_shape = VMEM((mp, 2 * local, mem_slots), BF16)
        stack_shape = VMEM((heads * slots, local), BF16)
        row_shape = shaped((slots, width))
        low_shape = shaped((mp, slots, local), BF16)
        head_slots = shaped((8, 2, 4 * local // SUB, width), BF16)
        ffn_slots = shaped((8, 2, 2 * width // SUB, width), BF16)
        matmul = 2 * slots * width * width
        plain = width * width * 2

        def spread_line(rows):
            return [rows] + [shift(rows, step) for step in range(1, mp)]

        def bound(kernel):
            return lambda *refs: kernel(dims, *refs)

        qkv, self_low, z1, first = call(
            bound(self_forward),
            [META] + in_vmem(5) + in_place(12),
            (shaped((mp, slots, 3 * local), BF16), low_shape, row_shape, row_shape),
            [weights_shape, flat_shape, dma],
            20 * matmul,
            8 * plain,
            "self_forward",
        )(meta, hidden_row, self_bias, *params, *head_pieces, own_self, self_proj)
        ffn_own, ffn_near, memory_blocks, qkv, self_low, z1, first = meet(
            ffn_own, ffn_near, memory_blocks, qkv, self_low, z1, first
        )
        ffn_far = far_chips(*ffn_near)
        memory_blocks[3] = shift(memory_blocks[3], 3)
        ffn_far, ffn_beside, memory_blocks, first = meet(
            ffn_far, [swap(ffn_own, 1)], memory_blocks, first
        )
        ffn_beside += [swap(piece, 1) for piece in (*ffn_near, *ffn_far)]
        ffn_pieces = (ffn_own, *ffn_near, *ffn_far, *ffn_beside)
        cross_q, cross_low, cross_total, z2, second, kv = call(
            bound(cross_forward),
            [META] + in_vmem(5) + in_place(mp + 13),
            (
                low_shape,
                low_shape,
                shaped((mp, heads * slots, 1)),
                row_shape,
                row_shape,
                shaped((mp, 2 * local, mem_slots), BF16),
            ),
            [
                weights_shape,
                VMEM((width, mem_slots), BF16),
                flat_shape,
                stack_shape,
                kv_shape,
                dma,
            ],
            40 * matmul,
            8 * plain,
            "cross_forward",
            1,
        )(
            meta,
            cross_bias,
            *params,
            first,
            *memory_blocks,
            *head_pieces,
            own_cq,
            cross_proj,
            own_kv,
        )
        shared_shape = (mp + 1, slots, width + width // 2)
        result, dz2, ffn_sums, ffn_shared, ffn_half = call(
            bound(ffn_both),
            [META] + in_vmem(7) + in_place(12),
            (
                shaped((slots, width), BF16),
                row_shape,
                shaped((16, width)),
                shaped(shared_shape, BF16),
                shaped((mp + 1, slots, width // 2), BF16),
            ),
            [
                VMEM((mp, width, inner), BF16),
                VMEM((mp, inner, width), BF16),
                flat_shape,
                VMEM((mp, slots, inner), BF16),
                VMEM((mp, slots, inner), F32),
                VMEM((slots, width), BF16),
                dma,
            ],
            40 * matmul,
            10 * plain,
            "ffn_both",
        )(meta, second, z2, grad_row, inner_bias, *params, *ffn_pieces, ffn_in, ffn_out)
        ffn_theirs = swap(ffn_shared, 1)
        result_blocks = spread_line(result)
        cross_dq, dz1, cross_sums, cross_local, kv_low, *memory_grads = call(
            bound(cross_back),
            [META] + in_vmem(5) + in_place(14),
            (
                low_shape,
                row_shape,
                shaped((8, width)),
                shaped((mp, 2, local)),
                shaped((mp, 2 * local, mem_slots), BF16),
                *[shaped((local, mem_slots), BF16)] * mp,
            ),
            [
                VMEM((2, mp, 2 * local, width), BF16),
                kv_shape,
                kv_shape,
                VMEM((width, mem_slots), BF16),
                flat_shape,
                stack_shape,
                stack_shape,
                dma,
            ],
            50 * matmul,
            12 * plain,
            "cross_back",
            1 + mp,
        )(
            meta,
            dz2,
            cross_q,
            cross_total,
            z1,
            norm_gains,
            kv,
            *head_pieces,
            own_cq,
            cross_proj,
            own_kv,
        )
        result_blocks, memory_grads, kv_low, dz1, ffn_theirs = meet(
            result_blocks, memory_grads, kv_low, dz1, ffn_theirs
        )
        memory_out = [memory_grads[0]]
        memory_out += [shift(memory_grads[step], step) for step in (1, 2)]
        pair_slots = shaped((2, 2, 2 * width // SUB, width), BF16)
        to_two, to_four, ffn_rest = call(
            bound(ffn_weights),
            [META] + in_place(3),
            (pair_slots, pair_slots, shaped((4, 2, 2 * width // SUB, width), BF16)),
            [
                VMEM((mp + 1, 2 * slots, width + width // 2), BF16),
                VMEM((mp, 2, width // 2, width), BF16),
                dma,
            ],
            16 * matmul,
            8 * plain,
            "ffn_weights",
            3,
        )(meta, ffn_shared, ffn_half, ffn_theirs)
        ffn_from = swap(to_two, 2), swap(to_four, 4)
        dz1 = after(dz1, to_two)
        hidden_grad, small, head_beside, head_mine = call(
            bound(head_back),
            [META] + in_vmem(11) + in_place(mp + 13),
            (row_shape, shaped((24, width)), ffn_slots, ffn_slots),
            [
                weights_shape,
                kv_shape,
                VMEM((width, mem_slots), BF16),
                flat_shape,
                VMEM((slots, local), BF16),
                VMEM((slots, 3 * local), BF16),
                squares,
                VMEM((mp, 2, local), F32),
                dma,
            ],
            60 * matmul,
            24 * plain,
            "head_back",
            2,
        )(
            meta,
            dz1,
            hidden_row,
            qkv,
            self_low,
            dz2,
            first,
            cross_dq,
            cross_low,
            cross_sums,
            cross_local,
            ffn_sums,
            kv_low,
            *memory_blocks,
            *head_pieces,
            own_self,
            self_proj,
        )
        ffn_from, memory_out, memory_last, hidden_grad, small, head_beside, head_mine = meet(
            ffn_from, memory_out, memory_grads[3], hidden_grad, small, head_beside, head_mine
        )
        head_other = swap(head_beside, 1)
        ffn_group = Group(lambda slot, *at: ffn_rest[(slot - 4, *at)].astype(F32))
        late_two, late_four = ffn_group.second(*ffn_from)
        ffn_late = swap(late_two, 2), swap(late_four, 4)
        memory_out.append(shift(memory_last, 3))
        small = small + flip(small, 1)
        head_other, ffn_late, memory_out, small = meet(head_other, ffn_late, memory_out, small)
        ffn_total, ffn_blocks = ffn_group.third(*ffn_from, *ffn_late)

        def head_summed(*slots):
            return head_mine[slots].astype(F32) + head_other[slots].astype(F32)

        head_group = Group(head_summed)
        four_slots = VMEM((4, 2, 2 * width // SUB, width), BF16)
        to_two, to_four = call(
            add_slots,
            in_place(2),
            (pair_slots, pair_slots),
            [four_slots, four_slots, four_slots, dma],
            0,
            4 * plain,
            "add_slots",
            2,
        )(head_mine, head_other)
        head_from = swap(to_two, 2), swap(to_four, 4)
        ffn_sent = [shift(ffn_blocks[step - 1], -step) for step in range(1, mp)]

        def joined(kernel, blocks, shape, dtype, name):
            return call(
                kernel, [META] + in_vmem(mp), (shaped(shape, dtype),), [], 0, 2 * plain, name
            )(meta, *blocks)[0]

        rows_shape = (mp * slots, width)
        memory_grad = joined(
            join_columns, memory_out, (local, mp * mem_slots), F32, "join_memory"
        )
        result = joined(join_rows, result_blocks, rows_shape, BF16, "join_result")
        head_from, ffn_sent, memory_grad, result, hidden_grad = meet(
            head_from, ffn_sent, memory_grad, result, hidden_grad
        )
        late_two, late_four = head_group.second(*head_from)
        head_late = swap(late_two, 2), swap(late_four, 4)
        hidden_low = hidden_grad.astype(BF16)
        hidden_blocks = [hidden_low, shift(hidden_low, 1), None, shift(hidden_low, 3)]
        small = after(small, hidden_blocks[1])
        bit = 2
        while bit < mp:
            small = small + flip(small, bit)
            bit *= 2
        ffn_low = line_sum(ffn_total, ffn_sent)
        small = small + swap(small, 1)
        bit = SUB
        while bit < dp:
            small = small + swap(small, bit)
            bit *= 2
        head_late, ffn_low, small, hidden_blocks = meet(
            head_late, ffn_low, small, hidden_blocks
        )
        head_total, head_blocks = head_group.third(*head_from, *head_late)
        head_sent = [shift(head_blocks[step - 1], -step) for step in range(1, mp)]
        ffn_near = near_chips(ffn_low)
        small, *ffn_near = meet(small, *ffn_near)
        small = small + swap(small, 2)
        small = small + swap(small, 4)
        ffn_near[0], _ = meet(ffn_near[0], head_sent[0])
        ffn_far = far_chips(*ffn_near)
        ffn_reduced = (ffn_low, *ffn_near, *ffn_far)
        ffn_joined = jnp.concatenate(ffn_reduced)
        head_sent, ffn_reduced, ffn_joined, small, hidden_blocks = meet(
            head_sent, ffn_reduced, ffn_joined, small, hidden_blocks
        )
        head_low = line_sum(head_total, head_sent)
        head_near = near_chips(head_low)
        hidden_blocks[2] = shift(hidden_blocks[0], 2)
        ffn_joined = swap(ffn_joined, 1)
        head_near, ffn_joined, hidden_blocks = meet(head_near, ffn_joined, hidden_blocks)
        grad_in, grad_out = call(
            finish_ffn,
            [META] + in_vmem(6),
            (shaped((width, inner)), shaped((inner, width))),
            [],
            0,
            plain,
            "finish_ffn",
        )(meta, *ffn_reduced, ffn_joined)
        hidden_grad = joined(join_rows, hidden_blocks, rows_shape, F32, "join_hidden")
        head_far = far_chips(*head_near)
        head_beside = [swap(piece, 1) for piece in (head_low, *head_near)]
        head_far, head_beside, grad_in, grad_out, hidden_grad = meet(
            head_far, head_beside, grad_in, grad_out, hidden_grad
        )
        head_beside += [swap(piece, 1) for piece in head_far]
        finished = call(
            finish_heads,
            [META] + in_vmem(11),
            (
                shaped((3 * local, width)),
                shaped((local, width)),
                shaped((local, width)),
                shaped((local, width)),
                shaped((2 * local, width)),
                shaped((3, width)),
                shaped((3, width)),
                shaped((3, width)),
                shaped((2, local)),
                shaped((2, local)),
                shaped((inner,)),
            ),
            [],
            0,
            plain,
            "finish_heads",
        )(meta, small, head_low, *head_near, *head_far, *head_beside)
        grad_self, grad_sp, grad_cq, grad_cp, grad_kv = finished[:5]
        return (
            result,
            hidden_grad,
            memory_grad.T,
            jnp.swapaxes(grad_self.reshape(3, local, width), 1, 2),
            finished[8],
            grad_sp,
            grad_cq.T,
            jnp.swapaxes(grad_kv.reshape(2, local, width), 1, 2),
            finished[9],
            grad_cp,
            grad_in,
            finished[10],
            grad_out,
            *finished[5:8],
        )

    return jax.shard_map(
        body,
        mesh=mesh,
        in_specs=(
            P("dp", None),
            P("dp", "mp"),
            P("dp", None),
            P("dp", None),
            P("dp"),
            P("dp", None),
            P("dp"),
            P(None, None, "mp"),
            P(None, "mp"),
            P("mp", None),
            P(None, "mp"),
            P(None, None, "mp"),
            P(None, "mp"),
            P("mp", None),
            P(None, "mp"),
            P("mp"),
            P("mp", None),
            P(),
            P(),
            P(),
        ),
        out_specs=(
            P("dp", None),
            P("dp", None),
            P("dp", "mp"),
            P(None, None, "mp"),
            P(None, "mp"),
            P("mp", None),
            P(None, "mp"),
            P(None, None, "mp"),
            P(None, "mp"),
            P("mp", None),
            P(None, "mp"),
            P("mp"),
            P("mp", None),
            P(),
            P(),
            P(),
        ),
        check_vma=False,
    )
```

```python
import jax
import jax.numpy as jnp
from jax import lax
from jax.experimental import pallas as pl
from jax.experimental.pallas import tpu as pltpu
from jax.sharding import PartitionSpec as P

HD = 64
SUB = 8
NEG_FILL = -1000000000.0
EPSILON = 1e-05
F32 = jnp.float32
BF16 = jnp.bfloat16
VMEM = pltpu.VMEM
ROOT_HALF = 0.7071067811865476
ROOT_TWO_PI = 0.3989422804014327
SLOTS = ((3, 0), (1, 0), (3, 1), (2, 1), (1, 1), (2, 0), (0, 0), (0, 1))


def nn(left, right):
    return lax.dot_general(left, right, (((1,), (0,)), ((), ())), preferred_element_type=F32)


def nt(left, right):
    return lax.dot_general(left, right, (((1,), (1,)), ((), ())), preferred_element_type=F32)


def tn(left, right):
    return lax.dot_general(left, right, (((0,), (0,)), ((), ())), preferred_element_type=F32)


def normed(values):
    average = jnp.mean(values, -1, keepdims=True)
    centered = values - average
    variance = jnp.mean(centered * centered, -1, keepdims=True)
    inverse = lax.rsqrt(variance + EPSILON)
    return centered * inverse, inverse


def norm_back(unit, inverse, gain, grad):
    scaled = grad * gain
    return (
        scaled
        - jnp.mean(scaled, -1, keepdims=True)
        - unit * jnp.mean(scaled * unit, -1, keepdims=True)
    ) * inverse


def row_sum(values):
    return jnp.sum(values, 0, keepdims=True)


def segments(meta, start, count, shape, axis):
    places = lax.broadcasted_iota(jnp.int32, shape, axis)
    found = jnp.zeros(shape, jnp.int32) - 1
    for j in range(count):
        found = found + (meta[start + j] <= places).astype(jnp.int32)
    return found, places


def fetch(pieces, place, target, low, high, sems):
    size = high - low
    blocks, rows = pieces[0].shape[:2]
    half = rows // 2
    for block in range(blocks):
        sem = sems.at[block + 1]
        for beside in (0, 1):
            whole = pieces[5 * beside : 5 * beside + 3]
            split = pieces[5 * beside + 3 : 5 * beside + 5]
            for offset in range(4):
                row = (place ^ (offset + 4 * beside)) * size
                if offset < 3:
                    source = whole[offset].at[block, pl.ds(low, size)]
                    to = target.at[block + 1, pl.ds(pl.multiple_of(row, 16), size)]
                    pltpu.make_async_copy(source, to, sem).start()
                    continue
                for part in range(low // half, high // half):
                    at = 2 * block + part
                    source = split[at // blocks].at[at % blocks]
                    start = pl.multiple_of(row + part * half - low, 16)
                    to = target.at[block + 1, pl.ds(start, half)]
                    pltpu.make_async_copy(source, to, sem).start()


def fetch_own(sources, target, sems):
    row = 0
    for source in sources:
        size = source.shape[0]
        pltpu.make_async_copy(source, target.at[0, pl.ds(row, size)], sems.at[0]).start()
        row += size


def arrive(target, sem):
    pltpu.make_async_copy(target, target, sem).wait()


def fetch_halves(pieces, owns, place, target, sems):
    own_cq, own_cp, own_kv = owns
    size = own_cq.shape[0]
    pltpu.make_async_copy(own_cq, target.at[0, 0, pl.ds(0, size)], sems.at[0, 0]).start()
    pltpu.make_async_copy(own_cp, target.at[0, 0, pl.ds(size, size)], sems.at[0, 0]).start()
    pltpu.make_async_copy(own_kv, target.at[1, 0], sems.at[1, 0]).start()
    blocks, rows = pieces[0].shape[:2]
    size = rows // 2
    for block in range(blocks):
        for index in range(8):
            offset = index % 4
            mine = pieces[5 * (index // 4) :]
            position = place ^ index
            plane = lax.div(position, 4)
            row = pl.multiple_of(lax.rem(position, 4) * size, 16)
            if offset < 3:
                source = mine[offset].at[block, pl.ds(size, size)]
            else:
                at = 2 * block + 1
                source = mine[3 + at // blocks].at[at % blocks]
            to = target.at[plane, block + 1, pl.ds(row, size)]
            pltpu.make_async_copy(source, to, sems.at[plane, block + 1]).start()


def fetch_memory(blocks, line, target, sem):
    count = len(blocks)
    for step, block in enumerate(blocks):
        size = block.shape[0]
        row = pl.multiple_of(lax.rem(line + count - step, count) * size, 16)
        pltpu.make_async_copy(block, target.at[pl.ds(row, size)], sem).start()


def slot_of(offset, half):
    first = SLOTS.index((offset, 0))
    second = SLOTS.index((offset, 1))
    return jnp.where(half == 0, first, second)


def self_mask(meta, nseg, slots):
    shape = (slots, slots)
    query_segment, query_place = segments(meta, 4, nseg, shape, 0)
    key_segment, key_place = segments(meta, 4, nseg, shape, 1)
    return (query_segment == key_segment) & (key_place <= query_place) & (key_place < meta[2])


def self_forward(dims, meta, x_ref, sb, ob, gain, bias, *refs):
    mp, local, heads, scaling, nseg = dims
    pieces, (own_self, own_sp) = refs[:10], refs[10:12]
    qkv, low, z1, first = refs[12:16]
    ws, acc, sems = refs[16:]
    fetch_own((own_self, own_sp), ws, sems.at[0])
    fetch(pieces, meta[0], ws, 0, 96, sems.at[0])
    allowed = self_mask(meta, nseg, x_ref.shape[0])
    acc[...] = x_ref[...].astype(F32) + ob[0:1]

    def step(z, carry):
        arrive(ws.at[z], sems.at[0, z])
        flat = nt(x_ref[...], ws[z, : 3 * local])
        rows = sb[z]
        qkv[z, :, :local] = ((flat[:, :local] + rows[0:1]) * scaling).astype(BF16)
        qkv[z, :, local : 2 * local] = flat[:, local : 2 * local].astype(BF16)
        qkv[z, :, 2 * local :] = (flat[:, 2 * local :] + rows[1:2]).astype(BF16)
        for i in range(heads):
            at = HD * i
            scores = nt(qkv[z, :, at : at + HD], qkv[z, :, local + at : local + at + HD])
            scores = jnp.where(allowed, scores, NEG_FILL)
            weights = jnp.exp(scores - jnp.max(scores, -1, keepdims=True))
            probs = (weights * (1.0 / jnp.sum(weights, -1, keepdims=True))).astype(BF16)
            out = nn(probs, qkv[z, :, 2 * local + at : 2 * local + at + HD])
            low[z, :, at : at + HD] = out.astype(BF16)
        acc[...] += nn(low[z], ws[z, 3 * local :])
        return carry

    lax.fori_loop(0, mp, step, 0)
    z1[...] = acc[...]
    unit, _ = normed(acc[...])
    first[...] = unit * gain[0:1] + bias[0:1]


def put_heads(target, source, heads):
    rows = source.shape[0]
    for i in range(heads):
        columns = slice(HD * i, HD * (i + 1))
        target[rows * i : rows * (i + 1), columns] = source[:, columns]


def masked(scores, allowed):
    shape = scores.shape
    scores = scores.reshape((-1,) + allowed.shape)
    return jnp.where(allowed[None], scores, NEG_FILL).reshape(shape)


def cross_mask(meta, nseg, slots, mem_slots):
    query_segment, _ = segments(meta, 4, nseg, (slots, 1), 0)
    key_segment, key_place = segments(meta, 4 + nseg, nseg, (1, mem_slots), 1)
    key_segment = jnp.where(key_place < meta[3], key_segment, -1)
    return query_segment == key_segment


def fetch_cross(pieces, owns, place, target, sem):
    fetch_own(owns, target, sem)
    fetch(pieces, place, target, 96, 192, sem)


def cross_forward(dims, meta, cb, ob, gain, bias, first, *refs):
    mp, local, heads, scaling, nseg = dims
    blocks, pieces, owns = refs[:mp], refs[mp : mp + 10], refs[mp + 10 : mp + 13]
    cq, low, total, z2, second, kv = refs[mp + 13 : mp + 19]
    wc, mem, acc, stacked, both, sems = refs[mp + 19 :]
    fetch_memory(blocks, meta[1], mem, sems.at[1, 0])
    fetch_cross(pieces, owns, meta[0], wc, sems.at[0])
    slots = first.shape[0]
    allowed = cross_mask(meta, nseg, slots, mem.shape[1])
    acc[...] = first[...] + ob[1:2]
    stacked[...] = jnp.zeros_like(stacked)
    first_low = first[...].astype(BF16)
    arrive(mem, sems.at[1, 0])

    def step(z, carry):
        arrive(wc.at[z], sems.at[0, z])
        rows = cb[z]
        query = ((nt(first_low, wc[z, :local]) + rows[0:1]) * scaling).astype(BF16)
        cq[z] = query
        put_heads(stacked, query, heads)
        flat = nn(wc[z, 2 * local :], mem[...])
        column = jnp.swapaxes(jnp.broadcast_to(rows[1:2], (8, local)), 0, 1)[:, :1]
        keys = flat[:local].astype(BF16)
        values = (flat[local:] + column).astype(BF16)
        both[z, :local] = keys
        both[z, local:] = values
        pltpu.make_async_copy(both.at[z], kv.at[z], sems.at[2, 0]).start()
        scores = masked(nn(stacked[...], keys), allowed)
        peak = jnp.max(scores, -1, keepdims=True)
        weights = jnp.exp(scores - peak)
        mass = jnp.sum(weights, -1, keepdims=True)
        probs = (weights * (1.0 / mass)).astype(BF16)
        total[z] = peak + jnp.log(mass)
        out = nt(probs, values)
        for i in range(heads):
            columns = slice(HD * i, HD * (i + 1))
            low[z, :, columns] = out[slots * i : slots * (i + 1), columns].astype(BF16)
        acc[...] += nn(low[z], wc[z, local : 2 * local])
        return carry

    lax.fori_loop(0, mp, step, 0)
    z2[...] = acc[...]
    unit, _ = normed(acc[...])
    second[...] = unit * gain[1:2] + bias[1:2]
    arrive(both, sems.at[2, 0])


def put_slots(beside, mine, place, z, base, source, sem):
    half = lax.div(z, 2)
    at = lax.rem(z, 2)
    size = source.shape[0] // SUB
    for offset in range(4):
        slot = slot_of(offset, half)
        for target, flip in ((mine, 0), (beside, 4)):
            row = pl.multiple_of((place ^ (offset + flip)) * size, 16)
            to = target.at[slot, at, pl.ds(base, size)]
            pltpu.make_async_copy(source.at[pl.ds(row, size)], to, sem).start()


def ffn_both(dims, meta, second, z2, grad, ib, ob, gain, bias, *refs):
    mp, local, heads, scaling, nseg = dims
    pieces, (own_in, own_out) = refs[:10], refs[10:12]
    result, dz2, sums, shared, own_half = refs[12:17]
    win, wout, acc, act, slope, low, sems = refs[17:]
    place = meta[0]
    width = second.shape[1]
    half = width // 2
    mine = pl.multiple_of(lax.div(place, 4) * half, 128)
    other = pl.multiple_of((1 - lax.div(place, 4)) * half, 128)
    fetch_own((own_in,), win, sems.at[0])
    fetch_own((own_out,), wout, sems.at[1])
    fetch(pieces, place, win, 0, 96, sems.at[0])
    fetch(pieces, place, wout, 96, 192, sems.at[1])
    acc[...] = second[...] + ob[2:3]
    low[...] = second[...].astype(BF16)
    own_half[0] = low[:, pl.ds(mine, half)]
    shared[0, :, width:] = low[:, pl.ds(other, half)]

    def forward(z, carry):
        arrive(win.at[z], sems.at[0, z])
        arrive(wout.at[z], sems.at[1, z])
        inner = nn(low[...], win[z]) + ib[z]
        share = 0.5 * (1.0 + lax.erf(inner * ROOT_HALF))
        act[z] = (inner * share).astype(BF16)
        own_half[z + 1] = act[z, :, pl.ds(mine, half)]
        shared[z + 1, :, width:] = act[z, :, pl.ds(other, half)]
        slope[z] = share + inner * (ROOT_TWO_PI * jnp.exp(-0.5 * inner * inner))
        acc[...] += nn(act[z], wout[z])
        return carry

    lax.fori_loop(0, mp, forward, 0, unroll=True)
    unit, inverse = normed(acc[...])
    result[...] = (unit * gain[2:3] + bias[2:3]).astype(BF16)
    out_grad = grad[...].astype(F32)
    third = norm_back(unit, inverse, gain[2:3], out_grad)
    sums[...] = jnp.zeros_like(sums)
    sums[0:1] = row_sum(third)
    sums[1:2] = row_sum(out_grad * unit)
    sums[2:3] = row_sum(out_grad)
    third_low = third.astype(BF16)
    shared[0, :, :width] = third_low
    acc[...] = third

    def backward(z, carry):
        inner = nt(third_low, wout[z]) * slope[z]
        sums[pl.ds(8 + z, 1)] = row_sum(inner)
        inner_low = inner.astype(BF16)
        acc[...] += nt(inner_low, win[z])
        shared[z + 1, :, :width] = inner_low
        return carry

    lax.fori_loop(0, mp, backward, 0, unroll=True)
    unit, inverse = normed(z2[...])
    grad_rows = acc[...]
    values = norm_back(unit, inverse, gain[1:2], grad_rows)
    dz2[...] = values
    sums[3:4] = row_sum(values)
    sums[4:5] = row_sum(grad_rows * unit)
    sums[5:6] = row_sum(grad_rows)


def ffn_weights(dims, meta, shared, own_half, theirs, to_two, to_four, rest, rows, dw, sems):
    mp = dims[0]
    slots = shared.shape[1]
    width = rows.shape[2] - own_half.shape[2]
    for i in range(mp + 1):
        sem = sems.at[i % mp, i // mp]
        part = rows.at[i, pl.ds(0, slots)]
        pltpu.make_async_copy(shared.at[i, :, pl.ds(0, width)], part.at[:, pl.ds(0, width)], sem).start()
        pltpu.make_async_copy(own_half.at[i], part.at[:, pl.ds(width, width // 2)], sem).start()
        pltpu.make_async_copy(theirs.at[i], rows.at[i, pl.ds(slots, slots)], sem).start()
    arrive(rows.at[0], sems.at[0, 0])
    for z in range(mp):
        i = z + 1
        arrive(rows.at[i], sems.at[i % mp, i // mp])
        dw[z, 0] = tn(rows[0, :, width:], rows[i, :, :width]).astype(BF16)
        dw[z, 1] = tn(rows[i, :, width:], rows[0, :, :width]).astype(BF16)
        size = dw.shape[2] // 4
        for offset in range(4):
            slot = SLOTS.index((offset, z // 2))
            if slot < 4:
                target = (to_two, to_four)[slot // 2].at[slot % 2, z % 2]
            else:
                target = rest.at[slot - 4, z % 2]
            row = pl.multiple_of(((meta[0] ^ offset) & 3) * size, 16)
            for j in (0, 1):
                source = dw.at[z, j, pl.ds(row, size)]
                pltpu.make_async_copy(source, target.at[pl.ds(j * size, size)], sems.at[0, 2]).start()
    arrive(dw, sems.at[0, 2])


def cross_back(dims, meta, dz2, cq, total, z1, gain, *refs):
    mp, local, heads, scaling, nseg = dims
    kv_ref, pieces, owns = refs[0], refs[1:11], refs[11:14]
    dcq, dz1, sums, sums_local, kv_low = refs[14:19]
    mem_out = refs[19 : 19 + mp]
    wc, kv, kv_grad, dmem, acc, queries, grads, sems = refs[19 + mp :]
    for z in range(mp):
        pltpu.make_async_copy(kv_ref.at[z], kv.at[z], sems.at[2, z]).start()
    fetch_halves(pieces, owns, meta[0], wc, sems)
    slots = dz2.shape[0]
    allowed = cross_mask(meta, nseg, slots, kv.shape[2])
    queries[...] = jnp.zeros_like(queries)
    grads[...] = jnp.zeros_like(grads)
    dz2_low = dz2[...].astype(BF16)
    acc[...] = dz2[...]

    def step(z, carry):
        arrive(wc.at[0, z], sems.at[0, z])
        arrive(wc.at[1, z], sems.at[1, z])
        arrive(kv.at[z], sems.at[2, z])
        put_heads(queries, cq[z], heads)
        grad = nt(dz2_low, wc[0, z, local:]).astype(BF16)
        put_heads(grads, grad, heads)
        keys, values = kv[z, :local], kv[z, local:]
        probs = jnp.exp(masked(nn(queries[...], keys), allowed) - total[z])
        probs_low = probs.astype(BF16)
        prob_grad = nn(grads[...], values)
        offset = jnp.sum(probs * prob_grad, -1, keepdims=True)
        score_grad = (probs * (prob_grad - offset)).astype(BF16)
        kv_grad[z, :local] = tn(queries[...], score_grad).astype(BF16)
        kv_grad[z, local:] = tn(grads[...], probs_low).astype(BF16)
        pltpu.make_async_copy(kv_grad.at[z], kv_low.at[z], sems.at[3, 0]).start()
        mass = jnp.sum(probs_low.astype(F32), -1, keepdims=True)
        query_grad = nt(score_grad, keys) * scaling
        for i in range(heads):
            columns = slice(HD * i, HD * (i + 1))
            rows = slice(slots * i, slots * (i + 1))
            part = query_grad[rows, columns]
            dcq[z, :, columns] = part.astype(BF16)
            sums_local[z, 0:1, columns] = row_sum(part)
            sums_local[z, 1:2, columns] = row_sum(mass[rows] * grad[:, columns].astype(F32))
        acc[...] += nn(dcq[z], wc[0, z, :local])
        return carry

    lax.fori_loop(0, mp, step, 0)
    depth = mp * kv_grad.shape[1]
    product = tn(wc[1].reshape(depth, wc.shape[3]), kv_grad[...].reshape(depth, kv.shape[2]))
    dmem[...] = product.astype(BF16)
    for block in range(mp):
        row = pl.multiple_of(lax.rem(meta[1] + block, mp) * local, 16)
        source = dmem.at[pl.ds(row, local)]
        pltpu.make_async_copy(source, mem_out[block], sems.at[3, 1]).start()
    unit, inverse = normed(z1[...])
    grad_rows = acc[...]
    values = norm_back(unit, inverse, gain[0:1], grad_rows)
    dz1[...] = values
    sums[...] = jnp.zeros_like(sums)
    sums[0:1] = row_sum(values)
    sums[1:2] = row_sum(grad_rows * unit)
    sums[2:3] = row_sum(grad_rows)
    arrive(kv_grad, sems.at[3, 0])
    arrive(dmem, sems.at[3, 1])


def head_back(dims, meta, dz1, x_ref, qkv, self_low, dz2, first, dcq, cross_low, *refs):
    mp, local, heads, scaling, nseg = dims
    cross_sums, cross_local, ffn_sums = refs[:3]
    refs = refs[3:]
    kv_ref, blocks, pieces = refs[0], refs[1 : 1 + mp], refs[1 + mp : 11 + mp]
    own_self, own_sp = refs[11 + mp : 13 + mp]
    dx, small, beside, mine = refs[13 + mp : 17 + mp]
    ws, kv, mem, acc, dout, dqkv, dw, sums_local, sems = refs[17 + mp :]
    place = meta[0]
    fetch_own((own_self, own_sp), ws, sems.at[0])
    fetch(pieces, place, ws, 0, 96, sems.at[0])
    fetch_memory(blocks, meta[1], mem, sems.at[2, 0])
    for z in range(mp):
        pltpu.make_async_copy(kv_ref.at[z], kv.at[z], sems.at[1, z]).start()
    allowed = self_mask(meta, nseg, x_ref.shape[0])
    dz1_low = dz1[...].astype(BF16)
    dz2_low = dz2[...].astype(BF16)
    first_low = first[...].astype(BF16)
    acc[...] = dz1[...]
    arrive(mem, sems.at[2, 0])

    def step(z, carry):
        arrive(ws.at[z], sems.at[0, z])
        arrive(kv.at[z], sems.at[1, z])
        dout[...] = nt(dz1_low, ws[z, 3 * local :]).astype(BF16)
        for i in range(heads):
            at = HD * i
            query = qkv[z, :, at : at + HD]
            key = qkv[z, :, local + at : local + at + HD]
            value = qkv[z, :, 2 * local + at : 2 * local + at + HD]
            grad = dout[:, at : at + HD]
            scores = jnp.where(allowed, nt(query, key), NEG_FILL)
            weights = jnp.exp(scores - jnp.max(scores, -1, keepdims=True))
            probs = weights * (1.0 / jnp.sum(weights, -1, keepdims=True))
            prob_grad = nt(grad, value)
            offset = jnp.sum(probs * prob_grad, -1, keepdims=True)
            score_grad = (probs * (prob_grad - offset)).astype(BF16)
            value_grad = tn(probs.astype(BF16), grad)
            query_grad = nn(score_grad, key) * scaling
            dqkv[:, at : at + HD] = query_grad.astype(BF16)
            dqkv[:, local + at : local + at + HD] = tn(score_grad, query).astype(BF16)
            dqkv[:, 2 * local + at : 2 * local + at + HD] = value_grad.astype(BF16)
            sums_local[z, 0:1, at : at + HD] = row_sum(query_grad)
            sums_local[z, 1:2, at : at + HD] = row_sum(value_grad)
        acc[...] += nn(dqkv[...], ws[z, : 3 * local])
        dw[z, 0, : 3 * local] = tn(dqkv[...], x_ref[...]).astype(BF16)
        dw[z, 0, 3 * local :] = tn(self_low[z], dz1_low).astype(BF16)
        put_slots(beside, mine, place, z, 0, dw.at[z, 0], sems.at[3, 0])
        dw[z, 1, :local] = tn(dcq[z], first_low).astype(BF16)
        dw[z, 1, local : 2 * local] = tn(cross_low[z], dz2_low).astype(BF16)
        dw[z, 1, 2 * local :] = nt(kv[z], mem[...]).astype(BF16)
        put_slots(beside, mine, place, z, 96, dw.at[z, 1], sems.at[3, 0])
        return carry

    lax.fori_loop(0, mp, step, 0)
    dx[...] = acc[...]
    small[...] = jnp.zeros_like(small)
    small[0:3] = cross_sums[0:3]
    small[3:9] = ffn_sums[0:6]

    def collect(z, carry):
        row = 9 + 2 * (meta[1] ^ z)
        for i, part in enumerate((sums_local, cross_local)):
            for j in (0, 1):
                at = (2 * i + j) * local
                small[pl.ds(row, 1), at : at + local] = part[z, j : j + 1]
        small[pl.ds(row + 1, 1)] = ffn_sums[pl.ds(8 + z, 1)]
        return carry

    lax.fori_loop(0, mp, collect, 0)
    arrive(dw, sems.at[3, 0])


def place_rows(place, ranges, pieces):
    half = pieces[3].shape[0]

    def taken(offset, start, size):
        mine = pieces[5 * (offset // 4) :]
        offset = offset % 4
        if offset < 3:
            return mine[offset][pl.ds(start, size)]
        if start < half:
            return mine[3][pl.ds(start, size)]
        return mine[4][pl.ds(start - half, size)]

    for offset in range(8):
        position = place ^ offset
        for start, size, targets in ranges:
            if offset % 4 == 3 and start < half < start + size:
                parts = ((start, half - start), (half, start + size - half))
            else:
                parts = ((start, size),)
            for begin, length in parts:
                source = taken(offset, begin, length).astype(F32)
                first = 0
                for target in targets:
                    count = target.shape[0] // size

                    @pl.when((position >= first) & (position < first + count))
                    def _():
                        row = (position - first) * size + (begin - start)
                        target[pl.ds(pl.multiple_of(row, 8), length)] = source

                    first += count


def finish_heads(meta, small, *refs):
    place_rows(meta[0], ((0, 96, refs[10:12]), (96, 96, refs[12:15])), refs[:10])
    shared, sharded = refs[15:18], refs[18:]
    for i, target in enumerate(shared):
        for j, row in enumerate((0, 6, 3)):
            target[j : j + 1] = small[row + i : row + i + 1]
    row = 9 + 2 * meta[1]
    local = sharded[0].shape[1]
    for i in (0, 1):
        for j in (0, 1):
            at = (2 * i + j) * local
            sharded[i][j : j + 1] = small[pl.ds(row, 1), at : at + local]
    sharded[2][...] = small[pl.ds(row + 1, 1)].reshape(sharded[2].shape)


def finish_ffn(meta, *refs):
    gi, go = refs[6:]
    pieces, joined = list(refs[:5]), refs[5]
    row = 0
    for piece in refs[:5]:
        pieces.append(joined.at[pl.ds(row, piece.shape[0])])
        row += piece.shape[0]
    place_rows(meta[0], ((0, 96, (gi,)), (96, 96, (go,))), pieces)


def add_slots(mine, other, to_two, to_four, left, right, out, sems):
    count = out.shape[0]
    for i in range(count):
        pltpu.make_async_copy(mine.at[i], left.at[i], sems.at[0, i]).start()
        pltpu.make_async_copy(other.at[i], right.at[i], sems.at[1, i]).start()
    for i in range(count):
        arrive(left.at[i], sems.at[0, i])
        arrive(right.at[i], sems.at[1, i])
        out[i] = (left[i].astype(F32) + right[i].astype(F32)).astype(BF16)
        target = (to_two, to_four)[i // 2].at[i % 2]
        pltpu.make_async_copy(out.at[i], target, sems.at[2, 0]).start()
    arrive(out, sems.at[2, 0])


def join_columns(meta, *refs):
    blocks, target = refs[:-1], refs[-1]
    count = len(blocks)
    for step, block in enumerate(blocks):
        size = block.shape[1]
        at = pl.multiple_of(lax.rem(meta[1] + count - step, count) * size, 128)
        target[:, pl.ds(at, size)] = block[...].astype(target.dtype)


def join_rows(meta, *refs):
    blocks, target = refs[:-1], refs[-1]
    count = len(blocks)
    for step, block in enumerate(blocks):
        size = block.shape[0]
        at = pl.multiple_of(lax.rem(meta[1] + count - step, count) * size, 16)
        target[pl.ds(at, size)] = block[...].astype(target.dtype)


def shaped(shape, dtype=F32):
    return jax.ShapeDtypeStruct(shape, dtype)


def in_vmem(count):
    return [pl.BlockSpec(memory_space=pltpu.VMEM)] * count


def in_place(count):
    return [pl.BlockSpec(memory_space=pl.ANY)] * count


META = pl.BlockSpec(memory_space=pltpu.SMEM)


def call(kernel, in_specs, outs, scratch, flops, moved, name, written=0):
    return pl.pallas_call(
        kernel,
        out_shape=outs,
        in_specs=in_specs,
        out_specs=in_vmem(len(outs) - written) + in_place(written),
        scratch_shapes=scratch,
        name=name,
        compiler_params=pltpu.CompilerParams(vmem_limit_bytes=60 * 1024 * 1024),
        cost_estimate=pl.CostEstimate(
            flops=flops // 16, bytes_accessed=moved // 4, transcendentals=0
        ),
    )


def solution(mesh):
    dp = mesh.shape["dp"]
    mp = mesh.shape["mp"]

    def swap(value, bit):
        return lax.ppermute(value, "dp", [(i, i ^ bit) for i in range(dp)])

    def shift(value, step):
        return lax.ppermute(value, "mp", [(i, (i + step) % mp) for i in range(mp)])

    def flip(value, bit):
        return lax.ppermute(value, "mp", [(i, i ^ bit) for i in range(mp)])

    def after(value, *others):
        return lax.optimization_barrier((value,) + others)[0] if others else value

    def meet(*values):
        return lax.optimization_barrier(values)

    def near_chips(own):
        return swap(own, 2), swap(own, 4)

    def far_chips(over_two, over_four):
        def halves(piece):
            if piece.ndim == 3:
                piece = piece.reshape(-1, piece.shape[1] // 2, piece.shape[2])
            half = piece.shape[0] // 2
            return piece[:half], piece[half:]

        return swap(halves(over_four)[0], 2), swap(halves(over_two)[1], 4)

    def beside(pieces):
        found = []
        for piece in pieces:
            found.append(swap(after(piece, *found[-1:]), 1))
        return found

    class Group:
        def __init__(self, summed):
            self.summed = summed

        def second(self, from_two, from_four):
            late_two = (self.summed(4) + from_four[0].astype(F32)).astype(BF16)
            late_four = (self.summed(5) + from_two[0].astype(F32)).astype(BF16)
            return late_two, late_four

        def third(self, from_two, from_four, late_two, late_four):
            blocks = []
            for slot, near, late in ((6, from_two, late_four), (7, from_four, late_two)):
                for i in (0, 1):
                    total = self.summed(slot, i) + near[1, i].astype(F32) + late[i].astype(F32)
                    bit = SUB
                    while bit < dp:
                        total = total + swap(total, bit)
                        bit *= 2
                    blocks.append(total)
            return blocks[0], [block.astype(BF16) for block in blocks[1:]]

    def line_sum(total, sent):
        for piece in sent:
            total = total + piece.astype(F32)
        return total.astype(BF16)

    def body(
        hidden,
        memory,
        out_grad,
        dec_starts,
        dec_length,
        mem_starts,
        mem_length,
        self_qkv,
        self_qv_bias,
        self_proj,
        cross_query,
        cross_kv,
        cross_qv_bias,
        cross_proj,
        ffn_in,
        ffn_in_bias,
        ffn_out,
        out_biases,
        norm_gains,
        norm_biases,
    ):
        row_count = dec_starts.shape[0]
        assert row_count == mp == 4 and dp % SUB == 0
        slots = hidden.shape[0] // row_count
        mem_slots = memory.shape[0] // row_count
        width = hidden.shape[1]
        local = self_proj.shape[0]
        heads = local // HD
        inner = ffn_out.shape[0]
        nseg = dec_starts.shape[1]
        dims = (mp, local, heads, HD ** (-0.5), nseg)
        line = lax.axis_index("mp")
        device = lax.axis_index("dp") % SUB
        place = (device & 1) * 4 + device // 2

        def row_of(array, size):
            return lax.dynamic_slice_in_dim(array, line * size, size, 0)

        def slice_of(array):
            size = array.shape[0] // SUB
            return lax.dynamic_slice_in_dim(array, place * size, size, 0)

        meta = jnp.concatenate(
            [
                jnp.stack([place, line]).astype(jnp.int32),
                row_of(dec_length, 1),
                row_of(mem_length, 1),
                row_of(dec_starts, 1)[0],
                row_of(mem_starts, 1)[0],
            ]
        )
        own_self = jnp.swapaxes(self_qkv, 1, 2).reshape(3 * local, width)
        own_cq = cross_query.T
        own_kv = jnp.swapaxes(cross_kv, 1, 2).reshape(2 * local, width)

        bias = jnp.concatenate(
            [self_qv_bias.reshape(-1), cross_qv_bias.reshape(-1), ffn_in_bias]
        ).reshape(-1, width)
        terms = []
        rest = bias
        for _ in range(3):
            term = lax.reduce_precision(rest, 8, 7)
            terms.append(term.astype(BF16))
            rest = rest - term
        bias_rows = 3 * bias.shape[0]
        terms = jnp.concatenate(terms + [jnp.zeros((16 - bias_rows, width), BF16)])
        head_piece = jnp.concatenate(
            [
                slice_of(jnp.concatenate([own_self, self_proj])),
                slice_of(jnp.concatenate([own_cq, cross_proj, own_kv])),
                terms,
            ]
        )
        ffn_piece = jnp.concatenate([slice_of(ffn_in), slice_of(ffn_out)])
        memory_t = memory.T
        memory_blocks = [
            lax.dynamic_slice_in_dim(memory_t, ((line + step) % mp) * mem_slots, mem_slots, 1)
            for step in range(mp)
        ]
        head_line = [flip(head_piece, step) for step in range(1, mp)]
        rows = head_piece.shape[0] - 16
        head_own = jnp.stack([piece[:rows] for piece in head_line])
        head_near = near_chips(head_own)
        ffn_piece = after(ffn_piece, *head_line)
        ffn_line = [flip(ffn_piece, step) for step in range(1, mp)]
        biases = [bias]
        for piece in head_line:
            term = piece[rows : rows + bias_rows].reshape(3, -1, width).astype(F32)
            biases.append((term[0] + term[1]) + term[2])
        biases = jnp.stack(biases).reshape(mp, -1)
        self_bias = biases[:, : 2 * local].reshape(mp, 2, local)
        cross_bias = biases[:, 2 * local : 4 * local].reshape(mp, 2, local)
        inner_bias = biases[:, None, 4 * local :]
        hidden_row = row_of(hidden, slots)
        grad_row = row_of(out_grad, slots)
        early = (meta, self_bias, cross_bias, inner_bias, hidden_row, grad_row)
        head_own, head_near, ffn_line, memory_blocks, early = meet(
            head_own, head_near, ffn_line, memory_blocks, early
        )
        meta, self_bias, cross_bias, inner_bias, hidden_row, grad_row = early
        head_far = far_chips(*head_near)
        head_beside = [swap(head_own, 1), swap(head_near[0], 1)]
        memory_blocks[1] = shift(memory_blocks[1], 1)
        ffn_own = jnp.stack(ffn_line)
        head_own, head_near, head_far, head_beside, ffn_own, memory_blocks = meet(
            head_own, head_near, head_far, head_beside, ffn_own, memory_blocks
        )
        head_beside += beside((head_near[1], *head_far))
        head_pieces = (head_own, *head_near, *head_far, *head_beside)
        ffn_near = near_chips(ffn_own)
        memory_blocks[2] = shift(memory_blocks[2], 2)
        params = (out_biases, norm_gains, norm_biases)
        dma = pltpu.SemaphoreType.DMA((4, mp))
        squares = VMEM((mp, 2, width, width), BF16)
        weights_shape = VMEM((mp, 4 * local, width), BF16)
        flat_shape = VMEM((slots, width), F32)
        kv_shape = VMEM((mp, 2 * local, mem_slots), BF16)
        stack_shape = VMEM((heads * slots, local), BF16)
        row_shape = shaped((slots, width))
        low_shape = shaped((mp, slots, local), BF16)
        head_slots = shaped((8, 2, 4 * local // SUB, width), BF16)
        ffn_slots = shaped((8, 2, 2 * width // SUB, width), BF16)
        matmul = 2 * slots * width * width
        plain = width * width * 2

        def spread_line(rows):
            return [rows] + [shift(rows, step) for step in range(1, mp)]

        def bound(kernel):
            return lambda *refs: kernel(dims, *refs)

        qkv, self_low, z1, first = call(
            bound(self_forward),
            [META] + in_vmem(5) + in_place(12),
            (shaped((mp, slots, 3 * local), BF16), low_shape, row_shape, row_shape),
            [weights_shape, flat_shape, dma],
            20 * matmul,
            8 * plain,
            "self_forward",
        )(meta, hidden_row, self_bias, *params, *head_pieces, own_self, self_proj)
        ffn_own, ffn_near, memory_blocks, qkv, self_low, z1, first = meet(
            ffn_own, ffn_near, memory_blocks, qkv, self_low, z1, first
        )
        ffn_far = far_chips(*ffn_near)
        memory_blocks[3] = shift(memory_blocks[3], 3)
        ffn_far, ffn_beside, memory_blocks, first = meet(
            ffn_far, [swap(ffn_own, 1)], memory_blocks, first
        )
        ffn_beside += [swap(piece, 1) for piece in (*ffn_near, *ffn_far)]
        ffn_pieces = (ffn_own, *ffn_near, *ffn_far, *ffn_beside)
        cross_q, cross_low, cross_total, z2, second, kv = call(
            bound(cross_forward),
            [META] + in_vmem(5) + in_place(mp + 13),
            (
                low_shape,
                low_shape,
                shaped((mp, heads * slots, 1)),
                row_shape,
                row_shape,
                shaped((mp, 2 * local, mem_slots), BF16),
            ),
            [
                weights_shape,
                VMEM((width, mem_slots), BF16),
                flat_shape,
                stack_shape,
                kv_shape,
                dma,
            ],
            40 * matmul,
            8 * plain,
            "cross_forward",
            1,
        )(
            meta,
            cross_bias,
            *params,
            first,
            *memory_blocks,
            *head_pieces,
            own_cq,
            cross_proj,
            own_kv,
        )
        shared_shape = (mp + 1, slots, width + width // 2)
        result, dz2, ffn_sums, ffn_shared, ffn_half = call(
            bound(ffn_both),
            [META] + in_vmem(7) + in_place(12),
            (
                shaped((slots, width), BF16),
                row_shape,
                shaped((16, width)),
                shaped(shared_shape, BF16),
                shaped((mp + 1, slots, width // 2), BF16),
            ),
            [
                VMEM((mp, width, inner), BF16),
                VMEM((mp, inner, width), BF16),
                flat_shape,
                VMEM((mp, slots, inner), BF16),
                VMEM((mp, slots, inner), F32),
                VMEM((slots, width), BF16),
                dma,
            ],
            40 * matmul,
            10 * plain,
            "ffn_both",
        )(meta, second, z2, grad_row, inner_bias, *params, *ffn_pieces, ffn_in, ffn_out)
        ffn_theirs = swap(ffn_shared, 1)
        result_blocks = spread_line(result)
        cross_dq, dz1, cross_sums, cross_local, kv_low, *memory_grads = call(
            bound(cross_back),
            [META] + in_vmem(5) + in_place(14),
            (
                low_shape,
                row_shape,
                shaped((8, width)),
                shaped((mp, 2, local)),
                shaped((mp, 2 * local, mem_slots), BF16),
                *[shaped((local, mem_slots), BF16)] * mp,
            ),
            [
                VMEM((2, mp, 2 * local, width), BF16),
                kv_shape,
                kv_shape,
                VMEM((width, mem_slots), BF16),
                flat_shape,
                stack_shape,
                stack_shape,
                dma,
            ],
            50 * matmul,
            12 * plain,
            "cross_back",
            1 + mp,
        )(
            meta,
            dz2,
            cross_q,
            cross_total,
            z1,
            norm_gains,
            kv,
            *head_pieces,
            own_cq,
            cross_proj,
            own_kv,
        )
        result_blocks, memory_grads, kv_low, dz1, ffn_theirs = meet(
            result_blocks, memory_grads, kv_low, dz1, ffn_theirs
        )
        memory_out = [memory_grads[0]]
        memory_out += [shift(memory_grads[step], step) for step in (1, 2)]
        pair_slots = shaped((2, 2, 2 * width // SUB, width), BF16)
        to_two, to_four, ffn_rest = call(
            bound(ffn_weights),
            [META] + in_place(3),
            (pair_slots, pair_slots, shaped((4, 2, 2 * width // SUB, width), BF16)),
            [
                VMEM((mp + 1, 2 * slots, width + width // 2), BF16),
                VMEM((mp, 2, width // 2, width), BF16),
                dma,
            ],
            16 * matmul,
            8 * plain,
            "ffn_weights",
            3,
        )(meta, ffn_shared, ffn_half, ffn_theirs)
        ffn_from = swap(to_two, 2), swap(to_four, 4)
        dz1 = after(dz1, to_two)
        hidden_grad, small, head_beside, head_mine = call(
            bound(head_back),
            [META] + in_vmem(11) + in_place(mp + 13),
            (row_shape, shaped((24, width)), ffn_slots, ffn_slots),
            [
                weights_shape,
                kv_shape,
                VMEM((width, mem_slots), BF16),
                flat_shape,
                VMEM((slots, local), BF16),
                VMEM((slots, 3 * local), BF16),
                squares,
                VMEM((mp, 2, local), F32),
                dma,
            ],
            60 * matmul,
            24 * plain,
            "head_back",
            2,
        )(
            meta,
            dz1,
            hidden_row,
            qkv,
            self_low,
            dz2,
            first,
            cross_dq,
            cross_low,
            cross_sums,
            cross_local,
            ffn_sums,
            kv_low,
            *memory_blocks,
            *head_pieces,
            own_self,
            self_proj,
        )
        ffn_from, memory_out, memory_last, hidden_grad, small, head_beside, head_mine = meet(
            ffn_from, memory_out, memory_grads[3], hidden_grad, small, head_beside, head_mine
        )
        head_other = swap(head_beside, 1)
        ffn_group = Group(lambda slot, *at: ffn_rest[(slot - 4, *at)].astype(F32))
        late_two, late_four = ffn_group.second(*ffn_from)
        ffn_late = swap(late_two, 2), swap(late_four, 4)
        small = small + flip(small, 1)
        memory_out.append(shift(after(memory_last, small), 3))
        four_slots = VMEM((4, 2, 2 * width // SUB, width), BF16)
        to_two, to_four = call(
            add_slots,
            in_place(2),
            (pair_slots, pair_slots),
            [four_slots, four_slots, four_slots, dma],
            0,
            4 * plain,
            "add_slots",
            2,
        )(head_mine, head_other)
        to_two, to_four, head_other, ffn_late, memory_out, small = meet(
            to_two, to_four, head_other, ffn_late, memory_out, small
        )
        ffn_total, ffn_blocks = ffn_group.third(*ffn_from, *ffn_late)

        def head_summed(*slots):
            return head_mine[slots].astype(F32) + head_other[slots].astype(F32)

        head_group = Group(head_summed)
        head_from = swap(to_two, 2), swap(to_four, 4)
        ffn_sent = [flip(ffn_blocks[step - 1], step) for step in range(1, mp)]

        def joined(kernel, blocks, shape, dtype, name):
            return call(
                kernel, [META] + in_vmem(mp), (shaped(shape, dtype),), [], 0, 2 * plain, name
            )(meta, *blocks)[0]

        rows_shape = (mp * slots, width)
        memory_grad = joined(
            join_columns, memory_out, (local, mp * mem_slots), F32, "join_memory"
        )
        result = joined(join_rows, result_blocks, rows_shape, BF16, "join_result")
        head_from, ffn_sent, memory_grad, result, hidden_grad = meet(
            head_from, ffn_sent, memory_grad, result, hidden_grad
        )
        late_two, late_four = head_group.second(*head_from)
        head_late = swap(late_two, 2), swap(late_four, 4)
        hidden_low = hidden_grad.astype(BF16)
        hidden_blocks = [hidden_low, shift(hidden_low, 1), None, shift(hidden_low, 3)]
        small = after(small, hidden_blocks[1])
        bit = 2
        while bit < mp:
            small = small + flip(small, bit)
            bit *= 2
        ffn_low = line_sum(ffn_total, ffn_sent)
        small = small + swap(small, 1)
        bit = SUB
        while bit < dp:
            small = small + swap(small, bit)
            bit *= 2
        head_late, ffn_low, small, hidden_blocks = meet(
            head_late, ffn_low, small, hidden_blocks
        )
        head_total, head_blocks = head_group.third(*head_from, *head_late)
        ffn_low, head_blocks = meet(ffn_low, head_blocks)
        head_sent = [flip(head_blocks[step - 1], step) for step in range(1, mp)]
        ffn_near = near_chips(ffn_low)
        small, *ffn_near = meet(small, *ffn_near)
        small = small + swap(small, 2)
        small = small + swap(small, 4)
        ffn_near[0], _ = meet(ffn_near[0], head_sent[0])
        ffn_far = far_chips(*ffn_near)
        ffn_reduced = (ffn_low, *ffn_near, *ffn_far)
        ffn_joined = jnp.concatenate(ffn_reduced)
        head_sent, ffn_reduced, ffn_joined, small, hidden_blocks = meet(
            head_sent, ffn_reduced, ffn_joined, small, hidden_blocks
        )
        head_low = line_sum(head_total, head_sent)
        head_near = near_chips(head_low)
        hidden_blocks[2] = shift(hidden_blocks[0], 2)
        ffn_joined = swap(ffn_joined, 1)
        grad_in, grad_out = call(
            finish_ffn,
            [META] + in_vmem(6),
            (shaped((width, inner)), shaped((inner, width))),
            [],
            0,
            plain,
            "finish_ffn",
        )(meta, *ffn_reduced, ffn_joined)
        head_near, grad_in, grad_out, hidden_blocks = meet(
            head_near, grad_in, grad_out, hidden_blocks
        )
        hidden_grad = joined(join_rows, hidden_blocks, rows_shape, F32, "join_hidden")
        head_far = far_chips(*head_near)
        head_beside = [swap(piece, 1) for piece in (head_low, *head_near)]
        head_far, head_beside, hidden_grad = meet(head_far, head_beside, hidden_grad)
        head_beside += [swap(piece, 1) for piece in head_far]
        finished = call(
            finish_heads,
            [META] + in_vmem(11),
            (
                shaped((3 * local, width)),
                shaped((local, width)),
                shaped((local, width)),
                shaped((local, width)),
                shaped((2 * local, width)),
                shaped((3, width)),
                shaped((3, width)),
                shaped((3, width)),
                shaped((2, local)),
                shaped((2, local)),
                shaped((inner,)),
            ),
            [],
            0,
            plain,
            "finish_heads",
        )(meta, small, head_low, *head_near, *head_far, *head_beside)
        grad_self, grad_sp, grad_cq, grad_cp, grad_kv = finished[:5]
        return (
            result,
            hidden_grad,
            memory_grad.T,
            jnp.swapaxes(grad_self.reshape(3, local, width), 1, 2),
            finished[8],
            grad_sp,
            grad_cq.T,
            jnp.swapaxes(grad_kv.reshape(2, local, width), 1, 2),
            finished[9],
            grad_cp,
            grad_in,
            finished[10],
            grad_out,
            *finished[5:8],
        )

    return jax.shard_map(
        body,
        mesh=mesh,
        in_specs=(
            P("dp", None),
            P("dp", "mp"),
            P("dp", None),
            P("dp", None),
            P("dp"),
            P("dp", None),
            P("dp"),
            P(None, None, "mp"),
            P(None, "mp"),
            P("mp", None),
            P(None, "mp"),
            P(None, None, "mp"),
            P(None, "mp"),
            P("mp", None),
            P(None, "mp"),
            P("mp"),
            P("mp", None),
            P(),
            P(),
            P(),
        ),
        out_specs=(
            P("dp", None),
            P("dp", None),
            P("dp", "mp"),
            P(None, None, "mp"),
            P(None, "mp"),
            P("mp", None),
            P(None, "mp"),
            P(None, None, "mp"),
            P(None, "mp"),
            P("mp", None),
            P(None, "mp"),
            P("mp"),
            P("mp", None),
            P(),
            P(),
            P(),
        ),
        check_vma=False,
    )
```

```python
import jax
import jax.numpy as jnp
from jax import lax
from jax.experimental import pallas as pl
from jax.experimental.pallas import tpu as pltpu
from jax.sharding import PartitionSpec as P

HD = 64
SUB = 8
NEG_FILL = -1000000000.0
EPSILON = 1e-05
F32 = jnp.float32
BF16 = jnp.bfloat16
VMEM = pltpu.VMEM
ROOT_HALF = 0.7071067811865476
ROOT_TWO_PI = 0.3989422804014327
SLOTS = ((3, 0), (1, 0), (3, 1), (2, 1), (1, 1), (2, 0), (0, 0), (0, 1))


def nn(left, right):
    return lax.dot_general(left, right, (((1,), (0,)), ((), ())), preferred_element_type=F32)


def nt(left, right):
    return lax.dot_general(left, right, (((1,), (1,)), ((), ())), preferred_element_type=F32)


def tn(left, right):
    return lax.dot_general(left, right, (((0,), (0,)), ((), ())), preferred_element_type=F32)


def normed(values):
    average = jnp.mean(values, -1, keepdims=True)
    centered = values - average
    variance = jnp.mean(centered * centered, -1, keepdims=True)
    inverse = lax.rsqrt(variance + EPSILON)
    return centered * inverse, inverse


def norm_back(unit, inverse, gain, grad):
    scaled = grad * gain
    return (
        scaled
        - jnp.mean(scaled, -1, keepdims=True)
        - unit * jnp.mean(scaled * unit, -1, keepdims=True)
    ) * inverse


def row_sum(values):
    return jnp.sum(values, 0, keepdims=True)


def segments(meta, start, count, shape, axis):
    places = lax.broadcasted_iota(jnp.int32, shape, axis)
    found = jnp.zeros(shape, jnp.int32) - 1
    for j in range(count):
        found = found + (meta[start + j] <= places).astype(jnp.int32)
    return found, places


def fetch(pieces, place, target, low, high, sems):
    size = high - low
    blocks, rows = pieces[0].shape[:2]
    half = rows // 2
    for block in range(blocks):
        sem = sems.at[block + 1]
        for beside in (0, 1):
            whole = pieces[5 * beside : 5 * beside + 3]
            split = pieces[5 * beside + 3 : 5 * beside + 5]
            for offset in range(4):
                row = (place ^ (offset + 4 * beside)) * size
                if offset < 3:
                    source = whole[offset].at[block, pl.ds(low, size)]
                    to = target.at[block + 1, pl.ds(pl.multiple_of(row, 16), size)]
                    pltpu.make_async_copy(source, to, sem).start()
                    continue
                for part in range(low // half, high // half):
                    at = 2 * block + part
                    source = split[at // blocks].at[at % blocks]
                    start = pl.multiple_of(row + part * half - low, 16)
                    to = target.at[block + 1, pl.ds(start, half)]
                    pltpu.make_async_copy(source, to, sem).start()


def fetch_own(sources, target, sems):
    row = 0
    for source in sources:
        size = source.shape[0]
        pltpu.make_async_copy(source, target.at[0, pl.ds(row, size)], sems.at[0]).start()
        row += size


def arrive(target, sem):
    pltpu.make_async_copy(target, target, sem).wait()


def fetch_halves(pieces, owns, place, target, sems):
    own_cq, own_cp, own_kv = owns
    size = own_cq.shape[0]
    pltpu.make_async_copy(own_cq, target.at[0, 0, pl.ds(0, size)], sems.at[0, 0]).start()
    pltpu.make_async_copy(own_cp, target.at[0, 0, pl.ds(size, size)], sems.at[0, 0]).start()
    pltpu.make_async_copy(own_kv, target.at[1, 0], sems.at[1, 0]).start()
    blocks, rows = pieces[0].shape[:2]
    size = rows // 2
    for block in range(blocks):
        for index in range(8):
            offset = index % 4
            mine = pieces[5 * (index // 4) :]
            position = place ^ index
            plane = lax.div(position, 4)
            row = pl.multiple_of(lax.rem(position, 4) * size, 16)
            if offset < 3:
                source = mine[offset].at[block, pl.ds(size, size)]
            else:
                at = 2 * block + 1
                source = mine[3 + at // blocks].at[at % blocks]
            to = target.at[plane, block + 1, pl.ds(row, size)]
            pltpu.make_async_copy(source, to, sems.at[plane, block + 1]).start()


def fetch_memory(blocks, line, target, sem):
    count = len(blocks)
    for step, block in enumerate(blocks):
        size = block.shape[0]
        row = pl.multiple_of(lax.rem(line + count - step, count) * size, 16)
        pltpu.make_async_copy(block, target.at[pl.ds(row, size)], sem).start()


def slot_of(offset, half):
    first = SLOTS.index((offset, 0))
    second = SLOTS.index((offset, 1))
    return jnp.where(half == 0, first, second)


def self_mask(meta, nseg, slots):
    shape = (slots, slots)
    query_segment, query_place = segments(meta, 4, nseg, shape, 0)
    key_segment, key_place = segments(meta, 4, nseg, shape, 1)
    return (query_segment == key_segment) & (key_place <= query_place) & (key_place < meta[2])


def self_forward(dims, meta, x_ref, sb, ob, gain, bias, *refs):
    mp, local, heads, scaling, nseg = dims
    pieces, (own_self, own_sp) = refs[:10], refs[10:12]
    qkv, low, z1, first = refs[12:16]
    ws, acc, sems = refs[16:]
    fetch_own((own_self, own_sp), ws, sems.at[0])
    fetch(pieces, meta[0], ws, 0, 96, sems.at[0])
    allowed = self_mask(meta, nseg, x_ref.shape[0])
    acc[...] = x_ref[...].astype(F32) + ob[0:1]

    def step(z, carry):
        arrive(ws.at[z], sems.at[0, z])
        flat = nt(x_ref[...], ws[z, : 3 * local])
        rows = sb[z]
        qkv[z, :, :local] = ((flat[:, :local] + rows[0:1]) * scaling).astype(BF16)
        qkv[z, :, local : 2 * local] = flat[:, local : 2 * local].astype(BF16)
        qkv[z, :, 2 * local :] = (flat[:, 2 * local :] + rows[1:2]).astype(BF16)
        for i in range(heads):
            at = HD * i
            scores = nt(qkv[z, :, at : at + HD], qkv[z, :, local + at : local + at + HD])
            scores = jnp.where(allowed, scores, NEG_FILL)
            weights = jnp.exp(scores - jnp.max(scores, -1, keepdims=True))
            probs = (weights * (1.0 / jnp.sum(weights, -1, keepdims=True))).astype(BF16)
            out = nn(probs, qkv[z, :, 2 * local + at : 2 * local + at + HD])
            low[z, :, at : at + HD] = out.astype(BF16)
        acc[...] += nn(low[z], ws[z, 3 * local :])
        return carry

    lax.fori_loop(0, mp, step, 0)
    z1[...] = acc[...]
    unit, _ = normed(acc[...])
    first[...] = unit * gain[0:1] + bias[0:1]


def put_heads(target, source, heads):
    rows = source.shape[0]
    for i in range(heads):
        columns = slice(HD * i, HD * (i + 1))
        target[rows * i : rows * (i + 1), columns] = source[:, columns]


def masked(scores, allowed):
    shape = scores.shape
    scores = scores.reshape((-1,) + allowed.shape)
    return jnp.where(allowed[None], scores, NEG_FILL).reshape(shape)


def cross_mask(meta, nseg, slots, mem_slots):
    query_segment, _ = segments(meta, 4, nseg, (slots, 1), 0)
    key_segment, key_place = segments(meta, 4 + nseg, nseg, (1, mem_slots), 1)
    key_segment = jnp.where(key_place < meta[3], key_segment, -1)
    return query_segment == key_segment


def fetch_cross(pieces, owns, place, target, sem):
    fetch_own(owns, target, sem)
    fetch(pieces, place, target, 96, 192, sem)


def cross_forward(dims, meta, cb, ob, gain, bias, first, *refs):
    mp, local, heads, scaling, nseg = dims
    blocks, pieces, owns = refs[:mp], refs[mp : mp + 10], refs[mp + 10 : mp + 13]
    cq, low, total, z2, second, kv = refs[mp + 13 : mp + 19]
    wc, mem, acc, stacked, both, sems = refs[mp + 19 :]
    fetch_memory(blocks, meta[1], mem, sems.at[1, 0])
    fetch_cross(pieces, owns, meta[0], wc, sems.at[0])
    slots = first.shape[0]
    allowed = cross_mask(meta, nseg, slots, mem.shape[1])
    acc[...] = first[...] + ob[1:2]
    stacked[...] = jnp.zeros_like(stacked)
    first_low = first[...].astype(BF16)
    arrive(mem, sems.at[1, 0])

    def step(z, carry):
        arrive(wc.at[z], sems.at[0, z])
        rows = cb[z]
        query = ((nt(first_low, wc[z, :local]) + rows[0:1]) * scaling).astype(BF16)
        cq[z] = query
        put_heads(stacked, query, heads)
        flat = nn(wc[z, 2 * local :], mem[...])
        column = jnp.swapaxes(jnp.broadcast_to(rows[1:2], (8, local)), 0, 1)[:, :1]
        keys = flat[:local].astype(BF16)
        values = (flat[local:] + column).astype(BF16)
        both[z, :local] = keys
        both[z, local:] = values
        pltpu.make_async_copy(both.at[z], kv.at[z], sems.at[2, 0]).start()
        scores = masked(nn(stacked[...], keys), allowed)
        peak = jnp.max(scores, -1, keepdims=True)
        weights = jnp.exp(scores - peak)
        mass = jnp.sum(weights, -1, keepdims=True)
        probs = (weights * (1.0 / mass)).astype(BF16)
        total[z] = peak + jnp.log(mass)
        out = nt(probs, values)
        for i in range(heads):
            columns = slice(HD * i, HD * (i + 1))
            low[z, :, columns] = out[slots * i : slots * (i + 1), columns].astype(BF16)
        acc[...] += nn(low[z], wc[z, local : 2 * local])
        return carry

    lax.fori_loop(0, mp, step, 0)
    z2[...] = acc[...]
    unit, _ = normed(acc[...])
    second[...] = unit * gain[1:2] + bias[1:2]
    arrive(both, sems.at[2, 0])


def put_slots(beside, mine, place, z, base, source, sem):
    half = lax.div(z, 2)
    at = lax.rem(z, 2)
    size = source.shape[0] // SUB
    for offset in range(4):
        slot = slot_of(offset, half)
        for target, flip in ((mine, 0), (beside, 4)):
            row = pl.multiple_of((place ^ (offset + flip)) * size, 16)
            to = target.at[slot, at, pl.ds(base, size)]
            pltpu.make_async_copy(source.at[pl.ds(row, size)], to, sem).start()


def ffn_both(dims, meta, second, z2, grad, ib, ob, gain, bias, *refs):
    mp, local, heads, scaling, nseg = dims
    pieces, (own_in, own_out) = refs[:10], refs[10:12]
    result, dz2, sums, shared, own_half = refs[12:17]
    win, wout, acc, act, slope, low, sems = refs[17:]
    place = meta[0]
    width = second.shape[1]
    half = width // 2
    mine = pl.multiple_of(lax.div(place, 4) * half, 128)
    other = pl.multiple_of((1 - lax.div(place, 4)) * half, 128)
    fetch_own((own_in,), win, sems.at[0])
    fetch_own((own_out,), wout, sems.at[1])
    fetch(pieces, place, win, 0, 96, sems.at[0])
    fetch(pieces, place, wout, 96, 192, sems.at[1])
    acc[...] = second[...] + ob[2:3]
    low[...] = second[...].astype(BF16)
    own_half[0] = low[:, pl.ds(mine, half)]
    shared[0, :, width:] = low[:, pl.ds(other, half)]

    def forward(z, carry):
        arrive(win.at[z], sems.at[0, z])
        arrive(wout.at[z], sems.at[1, z])
        inner = nn(low[...], win[z]) + ib[z]
        share = 0.5 * (1.0 + lax.erf(inner * ROOT_HALF))
        act[z] = (inner * share).astype(BF16)
        own_half[z + 1] = act[z, :, pl.ds(mine, half)]
        shared[z + 1, :, width:] = act[z, :, pl.ds(other, half)]
        slope[z] = share + inner * (ROOT_TWO_PI * jnp.exp(-0.5 * inner * inner))
        acc[...] += nn(act[z], wout[z])
        return carry

    lax.fori_loop(0, mp, forward, 0, unroll=True)
    unit, inverse = normed(acc[...])
    result[...] = (unit * gain[2:3] + bias[2:3]).astype(BF16)
    out_grad = grad[...].astype(F32)
    third = norm_back(unit, inverse, gain[2:3], out_grad)
    sums[...] = jnp.zeros_like(sums)
    sums[0:1] = row_sum(third)
    sums[1:2] = row_sum(out_grad * unit)
    sums[2:3] = row_sum(out_grad)
    third_low = third.astype(BF16)
    shared[0, :, :width] = third_low
    acc[...] = third

    def backward(z, carry):
        inner = nt(third_low, wout[z]) * slope[z]
        sums[pl.ds(8 + z, 1)] = row_sum(inner)
        inner_low = inner.astype(BF16)
        acc[...] += nt(inner_low, win[z])
        shared[z + 1, :, :width] = inner_low
        return carry

    lax.fori_loop(0, mp, backward, 0, unroll=True)
    unit, inverse = normed(z2[...])
    grad_rows = acc[...]
    values = norm_back(unit, inverse, gain[1:2], grad_rows)
    dz2[...] = values
    sums[3:4] = row_sum(values)
    sums[4:5] = row_sum(grad_rows * unit)
    sums[5:6] = row_sum(grad_rows)


def ffn_weights(dims, meta, shared, own_half, theirs, to_two, to_four, rest, rows, dw, sems):
    mp = dims[0]
    slots = shared.shape[1]
    width = rows.shape[2] - own_half.shape[2]
    for i in range(mp + 1):
        sem = sems.at[i % mp, i // mp]
        part = rows.at[i, pl.ds(0, slots)]
        pltpu.make_async_copy(shared.at[i, :, pl.ds(0, width)], part.at[:, pl.ds(0, width)], sem).start()
        pltpu.make_async_copy(own_half.at[i], part.at[:, pl.ds(width, width // 2)], sem).start()
        pltpu.make_async_copy(theirs.at[i], rows.at[i, pl.ds(slots, slots)], sem).start()
    arrive(rows.at[0], sems.at[0, 0])
    for z in range(mp):
        i = z + 1
        arrive(rows.at[i], sems.at[i % mp, i // mp])
        dw[z, 0] = tn(rows[0, :, width:], rows[i, :, :width]).astype(BF16)
        dw[z, 1] = tn(rows[i, :, width:], rows[0, :, :width]).astype(BF16)
        size = dw.shape[2] // 4
        for offset in range(4):
            slot = SLOTS.index((offset, z // 2))
            if slot < 4:
                target = (to_two, to_four)[slot // 2].at[slot % 2, z % 2]
            else:
                target = rest.at[slot - 4, z % 2]
            row = pl.multiple_of(((meta[0] ^ offset) & 3) * size, 16)
            for j in (0, 1):
                source = dw.at[z, j, pl.ds(row, size)]
                pltpu.make_async_copy(source, target.at[pl.ds(j * size, size)], sems.at[0, 2]).start()
    arrive(dw, sems.at[0, 2])


def cross_back(dims, meta, dz2, cq, total, z1, gain, *refs):
    mp, local, heads, scaling, nseg = dims
    kv_ref, pieces, owns = refs[0], refs[1:11], refs[11:14]
    dcq, dz1, sums, sums_local, kv_low = refs[14:19]
    mem_out = refs[19 : 19 + mp]
    wc, kv, kv_grad, dmem, acc, queries, grads, sems = refs[19 + mp :]
    for z in range(mp):
        pltpu.make_async_copy(kv_ref.at[z], kv.at[z], sems.at[2, z]).start()
    fetch_halves(pieces, owns, meta[0], wc, sems)
    slots = dz2.shape[0]
    allowed = cross_mask(meta, nseg, slots, kv.shape[2])
    queries[...] = jnp.zeros_like(queries)
    grads[...] = jnp.zeros_like(grads)
    dz2_low = dz2[...].astype(BF16)
    acc[...] = dz2[...]

    def step(z, carry):
        arrive(wc.at[0, z], sems.at[0, z])
        arrive(wc.at[1, z], sems.at[1, z])
        arrive(kv.at[z], sems.at[2, z])
        put_heads(queries, cq[z], heads)
        grad = nt(dz2_low, wc[0, z, local:]).astype(BF16)
        put_heads(grads, grad, heads)
        keys, values = kv[z, :local], kv[z, local:]
        probs = jnp.exp(masked(nn(queries[...], keys), allowed) - total[z])
        probs_low = probs.astype(BF16)
        prob_grad = nn(grads[...], values)
        offset = jnp.sum(probs * prob_grad, -1, keepdims=True)
        score_grad = (probs * (prob_grad - offset)).astype(BF16)
        kv_grad[z, :local] = tn(queries[...], score_grad).astype(BF16)
        kv_grad[z, local:] = tn(grads[...], probs_low).astype(BF16)
        pltpu.make_async_copy(kv_grad.at[z], kv_low.at[z], sems.at[3, 0]).start()
        mass = jnp.sum(probs_low.astype(F32), -1, keepdims=True)
        query_grad = nt(score_grad, keys) * scaling
        for i in range(heads):
            columns = slice(HD * i, HD * (i + 1))
            rows = slice(slots * i, slots * (i + 1))
            part = query_grad[rows, columns]
            dcq[z, :, columns] = part.astype(BF16)
            sums_local[z, 0:1, columns] = row_sum(part)
            sums_local[z, 1:2, columns] = row_sum(mass[rows] * grad[:, columns].astype(F32))
        acc[...] += nn(dcq[z], wc[0, z, :local])
        return carry

    lax.fori_loop(0, mp, step, 0)
    depth = mp * kv_grad.shape[1]
    product = tn(wc[1].reshape(depth, wc.shape[3]), kv_grad[...].reshape(depth, kv.shape[2]))
    dmem[...] = product.astype(BF16)
    for block in range(mp):
        row = pl.multiple_of(lax.rem(meta[1] + block, mp) * local, 16)
        source = dmem.at[pl.ds(row, local)]
        pltpu.make_async_copy(source, mem_out[block], sems.at[3, 1]).start()
    unit, inverse = normed(z1[...])
    grad_rows = acc[...]
    values = norm_back(unit, inverse, gain[0:1], grad_rows)
    dz1[...] = values
    sums[...] = jnp.zeros_like(sums)
    sums[0:1] = row_sum(values)
    sums[1:2] = row_sum(grad_rows * unit)
    sums[2:3] = row_sum(grad_rows)
    arrive(kv_grad, sems.at[3, 0])
    arrive(dmem, sems.at[3, 1])


def head_back(dims, meta, dz1, x_ref, qkv, self_low, dz2, first, dcq, cross_low, *refs):
    mp, local, heads, scaling, nseg = dims
    cross_sums, cross_local, ffn_sums = refs[:3]
    refs = refs[3:]
    kv_ref, blocks, pieces = refs[0], refs[1 : 1 + mp], refs[1 + mp : 11 + mp]
    own_self, own_sp = refs[11 + mp : 13 + mp]
    dx, small, beside, mine = refs[13 + mp : 17 + mp]
    ws, kv, mem, acc, dout, dqkv, dw, sums_local, sems = refs[17 + mp :]
    place = meta[0]
    fetch_own((own_self, own_sp), ws, sems.at[0])
    fetch(pieces, place, ws, 0, 96, sems.at[0])
    fetch_memory(blocks, meta[1], mem, sems.at[2, 0])
    for z in range(mp):
        pltpu.make_async_copy(kv_ref.at[z], kv.at[z], sems.at[1, z]).start()
    allowed = self_mask(meta, nseg, x_ref.shape[0])
    dz1_low = dz1[...].astype(BF16)
    dz2_low = dz2[...].astype(BF16)
    first_low = first[...].astype(BF16)
    acc[...] = dz1[...]
    arrive(mem, sems.at[2, 0])

    def step(z, carry):
        arrive(ws.at[z], sems.at[0, z])
        arrive(kv.at[z], sems.at[1, z])
        dout[...] = nt(dz1_low, ws[z, 3 * local :]).astype(BF16)
        for i in range(heads):
            at = HD * i
            query = qkv[z, :, at : at + HD]
            key = qkv[z, :, local + at : local + at + HD]
            value = qkv[z, :, 2 * local + at : 2 * local + at + HD]
            grad = dout[:, at : at + HD]
            scores = jnp.where(allowed, nt(query, key), NEG_FILL)
            weights = jnp.exp(scores - jnp.max(scores, -1, keepdims=True))
            probs = weights * (1.0 / jnp.sum(weights, -1, keepdims=True))
            prob_grad = nt(grad, value)
            offset = jnp.sum(probs * prob_grad, -1, keepdims=True)
            score_grad = (probs * (prob_grad - offset)).astype(BF16)
            value_grad = tn(probs.astype(BF16), grad)
            query_grad = nn(score_grad, key) * scaling
            dqkv[:, at : at + HD] = query_grad.astype(BF16)
            dqkv[:, local + at : local + at + HD] = tn(score_grad, query).astype(BF16)
            dqkv[:, 2 * local + at : 2 * local + at + HD] = value_grad.astype(BF16)
            sums_local[z, 0:1, at : at + HD] = row_sum(query_grad)
            sums_local[z, 1:2, at : at + HD] = row_sum(value_grad)
        acc[...] += nn(dqkv[...], ws[z, : 3 * local])
        dw[z, 0, : 3 * local] = tn(dqkv[...], x_ref[...]).astype(BF16)
        dw[z, 0, 3 * local :] = tn(self_low[z], dz1_low).astype(BF16)
        put_slots(beside, mine, place, z, 0, dw.at[z, 0], sems.at[3, 0])
        dw[z, 1, :local] = tn(dcq[z], first_low).astype(BF16)
        dw[z, 1, local : 2 * local] = tn(cross_low[z], dz2_low).astype(BF16)
        dw[z, 1, 2 * local :] = nt(kv[z], mem[...]).astype(BF16)
        put_slots(beside, mine, place, z, 96, dw.at[z, 1], sems.at[3, 0])
        return carry

    lax.fori_loop(0, mp, step, 0)
    dx[...] = acc[...]
    small[...] = jnp.zeros_like(small)
    small[0:3] = cross_sums[0:3]
    small[3:9] = ffn_sums[0:6]

    def collect(z, carry):
        row = 9 + 2 * (meta[1] ^ z)
        for i, part in enumerate((sums_local, cross_local)):
            for j in (0, 1):
                at = (2 * i + j) * local
                small[pl.ds(row, 1), at : at + local] = part[z, j : j + 1]
        small[pl.ds(row + 1, 1)] = ffn_sums[pl.ds(8 + z, 1)]
        return carry

    lax.fori_loop(0, mp, collect, 0)
    arrive(dw, sems.at[3, 0])


def place_rows(place, ranges, pieces):
    half = pieces[3].shape[0]

    def taken(offset, start, size):
        mine = pieces[5 * (offset // 4) :]
        offset = offset % 4
        if offset < 3:
            return mine[offset][pl.ds(start, size)]
        if start < half:
            return mine[3][pl.ds(start, size)]
        return mine[4][pl.ds(start - half, size)]

    for offset in range(8):
        position = place ^ offset
        for start, size, targets in ranges:
            if offset % 4 == 3 and start < half < start + size:
                parts = ((start, half - start), (half, start + size - half))
            else:
                parts = ((start, size),)
            for begin, length in parts:
                source = taken(offset, begin, length).astype(F32)
                first = 0
                for target in targets:
                    count = target.shape[0] // size

                    @pl.when((position >= first) & (position < first + count))
                    def _():
                        row = (position - first) * size + (begin - start)
                        target[pl.ds(pl.multiple_of(row, 8), length)] = source

                    first += count


def finish_heads(meta, small, *refs):
    place_rows(meta[0], ((0, 96, refs[10:12]), (96, 96, refs[12:15])), refs[:10])
    shared, sharded = refs[15:18], refs[18:]
    for i, target in enumerate(shared):
        for j, row in enumerate((0, 6, 3)):
            target[j : j + 1] = small[row + i : row + i + 1]
    row = 9 + 2 * meta[1]
    local = sharded[0].shape[1]
    for i in (0, 1):
        for j in (0, 1):
            at = (2 * i + j) * local
            sharded[i][j : j + 1] = small[pl.ds(row, 1), at : at + local]
    sharded[2][...] = small[pl.ds(row + 1, 1)].reshape(sharded[2].shape)


def finish_ffn(meta, *refs):
    gi, go = refs[6:]
    pieces, joined = list(refs[:5]), refs[5]
    row = 0
    for piece in refs[:5]:
        pieces.append(joined.at[pl.ds(row, piece.shape[0])])
        row += piece.shape[0]
    place_rows(meta[0], ((0, 96, (gi,)), (96, 96, (go,))), pieces)


def add_slots(mine, other, to_two, to_four, left, right, out, sems):
    count = out.shape[0]
    for i in range(count):
        pltpu.make_async_copy(mine.at[i], left.at[i], sems.at[0, i]).start()
        pltpu.make_async_copy(other.at[i], right.at[i], sems.at[1, i]).start()
    for i in range(count):
        arrive(left.at[i], sems.at[0, i])
        arrive(right.at[i], sems.at[1, i])
        out[i] = (left[i].astype(F32) + right[i].astype(F32)).astype(BF16)
        target = (to_two, to_four)[i // 2].at[i % 2]
        pltpu.make_async_copy(out.at[i], target, sems.at[2, 0]).start()
    arrive(out, sems.at[2, 0])


def join_columns(meta, *refs):
    blocks, target = refs[:-1], refs[-1]
    count = len(blocks)
    for step, block in enumerate(blocks):
        size = block.shape[1]
        at = pl.multiple_of(lax.rem(meta[1] + count - step, count) * size, 128)
        target[:, pl.ds(at, size)] = block[...].astype(target.dtype)


def join_rows(meta, *refs):
    blocks, target = refs[:-1], refs[-1]
    count = len(blocks)
    for step, block in enumerate(blocks):
        size = block.shape[0]
        at = pl.multiple_of(lax.rem(meta[1] + count - step, count) * size, 16)
        target[pl.ds(at, size)] = block[...].astype(target.dtype)


def shaped(shape, dtype=F32):
    return jax.ShapeDtypeStruct(shape, dtype)


def in_vmem(count):
    return [pl.BlockSpec(memory_space=pltpu.VMEM)] * count


def in_place(count):
    return [pl.BlockSpec(memory_space=pl.ANY)] * count


META = pl.BlockSpec(memory_space=pltpu.SMEM)


ROOM = dict(finish_heads=14, finish_ffn=14, join_result=14, join_hidden=14, join_memory=14)


def call(kernel, in_specs, outs, scratch, flops, moved, name, written=0):
    return pl.pallas_call(
        kernel,
        out_shape=outs,
        in_specs=in_specs,
        out_specs=in_vmem(len(outs) - written) + in_place(written),
        scratch_shapes=scratch,
        name=name,
        compiler_params=pltpu.CompilerParams(vmem_limit_bytes=ROOM.get(name, 60) * 1024 * 1024),
        cost_estimate=pl.CostEstimate(
            flops=flops // 16, bytes_accessed=moved // 4, transcendentals=0
        ),
    )


def solution(mesh):
    dp = mesh.shape["dp"]
    mp = mesh.shape["mp"]

    def swap(value, bit):
        return lax.ppermute(value, "dp", [(i, i ^ bit) for i in range(dp)])

    def shift(value, step):
        return lax.ppermute(value, "mp", [(i, (i + step) % mp) for i in range(mp)])

    def flip(value, bit):
        return lax.ppermute(value, "mp", [(i, i ^ bit) for i in range(mp)])

    def after(value, *others):
        return lax.optimization_barrier((value,) + others)[0] if others else value

    def meet(*values):
        return lax.optimization_barrier(values)

    def near_chips(own):
        return swap(own, 2), swap(own, 4)

    def far_chips(over_two, over_four):
        def halves(piece):
            if piece.ndim == 3:
                piece = piece.reshape(-1, piece.shape[1] // 2, piece.shape[2])
            half = piece.shape[0] // 2
            return piece[:half], piece[half:]

        return swap(halves(over_four)[0], 2), swap(halves(over_two)[1], 4)

    def beside(pieces):
        found = []
        for piece in pieces:
            found.append(swap(after(piece, *found[-1:]), 1))
        return found

    class Group:
        def __init__(self, summed):
            self.summed = summed

        def second(self, from_two, from_four):
            late_two = (self.summed(4) + from_four[0].astype(F32)).astype(BF16)
            late_four = (self.summed(5) + from_two[0].astype(F32)).astype(BF16)
            return late_two, late_four

        def third(self, from_two, from_four, late_two, late_four):
            blocks = []
            for slot, near, late in ((6, from_two, late_four), (7, from_four, late_two)):
                for i in (0, 1):
                    total = self.summed(slot, i) + near[1, i].astype(F32) + late[i].astype(F32)
                    bit = SUB
                    while bit < dp:
                        total = total + swap(total, bit)
                        bit *= 2
                    blocks.append(total)
            return blocks[0], [block.astype(BF16) for block in blocks[1:]]

    def line_sum(total, sent):
        for piece in sent:
            total = total + piece.astype(F32)
        return total.astype(BF16)

    def body(
        hidden,
        memory,
        out_grad,
        dec_starts,
        dec_length,
        mem_starts,
        mem_length,
        self_qkv,
        self_qv_bias,
        self_proj,
        cross_query,
        cross_kv,
        cross_qv_bias,
        cross_proj,
        ffn_in,
        ffn_in_bias,
        ffn_out,
        out_biases,
        norm_gains,
        norm_biases,
    ):
        row_count = dec_starts.shape[0]
        assert row_count == mp == 4 and dp % SUB == 0
        slots = hidden.shape[0] // row_count
        mem_slots = memory.shape[0] // row_count
        width = hidden.shape[1]
        local = self_proj.shape[0]
        heads = local // HD
        inner = ffn_out.shape[0]
        nseg = dec_starts.shape[1]
        dims = (mp, local, heads, HD ** (-0.5), nseg)
        line = lax.axis_index("mp")
        device = lax.axis_index("dp") % SUB
        place = (device & 1) * 4 + device // 2

        def row_of(array, size):
            return lax.dynamic_slice_in_dim(array, line * size, size, 0)

        def slice_of(array):
            size = array.shape[0] // SUB
            return lax.dynamic_slice_in_dim(array, place * size, size, 0)

        meta = jnp.concatenate(
            [
                jnp.stack([place, line]).astype(jnp.int32),
                row_of(dec_length, 1),
                row_of(mem_length, 1),
                row_of(dec_starts, 1)[0],
                row_of(mem_starts, 1)[0],
            ]
        )
        own_self = jnp.swapaxes(self_qkv, 1, 2).reshape(3 * local, width)
        own_cq = cross_query.T
        own_kv = jnp.swapaxes(cross_kv, 1, 2).reshape(2 * local, width)

        bias = jnp.concatenate(
            [self_qv_bias.reshape(-1), cross_qv_bias.reshape(-1), ffn_in_bias]
        ).reshape(-1, width)
        terms = []
        rest = bias
        for _ in range(3):
            term = lax.reduce_precision(rest, 8, 7)
            terms.append(term.astype(BF16))
            rest = rest - term
        bias_rows = 3 * bias.shape[0]
        terms = jnp.concatenate(terms + [jnp.zeros((16 - bias_rows, width), BF16)])
        head_piece = jnp.concatenate(
            [
                slice_of(jnp.concatenate([own_self, self_proj])),
                slice_of(jnp.concatenate([own_cq, cross_proj, own_kv])),
                terms,
            ]
        )
        ffn_piece = jnp.concatenate([slice_of(ffn_in), slice_of(ffn_out)])
        memory_t = memory.T
        memory_blocks = [
            lax.dynamic_slice_in_dim(memory_t, ((line + step) % mp) * mem_slots, mem_slots, 1)
            for step in range(mp)
        ]
        head_line = [flip(head_piece, step) for step in range(1, mp)]
        rows = head_piece.shape[0] - 16
        head_own = jnp.stack([piece[:rows] for piece in head_line])
        head_near = near_chips(head_own)
        ffn_piece = after(ffn_piece, *head_line)
        ffn_line = [flip(ffn_piece, step) for step in range(1, mp)]
        biases = [bias]
        for piece in head_line:
            term = piece[rows : rows + bias_rows].reshape(3, -1, width).astype(F32)
            biases.append((term[0] + term[1]) + term[2])
        biases = jnp.stack(biases).reshape(mp, -1)
        self_bias = biases[:, : 2 * local].reshape(mp, 2, local)
        cross_bias = biases[:, 2 * local : 4 * local].reshape(mp, 2, local)
        inner_bias = biases[:, None, 4 * local :]
        hidden_row = row_of(hidden, slots)
        grad_row = row_of(out_grad, slots)
        early = (meta, self_bias, cross_bias, inner_bias, hidden_row, grad_row)
        head_own, head_near, ffn_line, memory_blocks, early = meet(
            head_own, head_near, ffn_line, memory_blocks, early
        )
        meta, self_bias, cross_bias, inner_bias, hidden_row, grad_row = early
        head_far = far_chips(*head_near)
        head_beside = [swap(head_own, 1), swap(head_near[0], 1)]
        memory_blocks[1] = shift(memory_blocks[1], 1)
        ffn_own = jnp.stack(ffn_line)
        head_own, head_near, head_far, head_beside, ffn_own, memory_blocks = meet(
            head_own, head_near, head_far, head_beside, ffn_own, memory_blocks
        )
        head_beside += beside((head_near[1], *head_far))
        head_pieces = (head_own, *head_near, *head_far, *head_beside)
        ffn_near = near_chips(ffn_own)
        memory_blocks[2] = shift(memory_blocks[2], 2)
        params = (out_biases, norm_gains, norm_biases)
        dma = pltpu.SemaphoreType.DMA((4, mp))
        squares = VMEM((mp, 2, width, width), BF16)
        weights_shape = VMEM((mp, 4 * local, width), BF16)
        flat_shape = VMEM((slots, width), F32)
        kv_shape = VMEM((mp, 2 * local, mem_slots), BF16)
        stack_shape = VMEM((heads * slots, local), BF16)
        row_shape = shaped((slots, width))
        low_shape = shaped((mp, slots, local), BF16)
        head_slots = shaped((8, 2, 4 * local // SUB, width), BF16)
        ffn_slots = shaped((8, 2, 2 * width // SUB, width), BF16)
        matmul = 2 * slots * width * width
        plain = width * width * 2

        def spread_line(rows):
            return [rows] + [shift(rows, step) for step in range(1, mp)]

        def bound(kernel):
            return lambda *refs: kernel(dims, *refs)

        qkv, self_low, z1, first = call(
            bound(self_forward),
            [META] + in_vmem(5) + in_place(12),
            (shaped((mp, slots, 3 * local), BF16), low_shape, row_shape, row_shape),
            [weights_shape, flat_shape, dma],
            20 * matmul,
            8 * plain,
            "self_forward",
        )(meta, hidden_row, self_bias, *params, *head_pieces, own_self, self_proj)
        ffn_own, ffn_near, memory_blocks, qkv, self_low, z1, first = meet(
            ffn_own, ffn_near, memory_blocks, qkv, self_low, z1, first
        )
        ffn_far = far_chips(*ffn_near)
        memory_blocks[3] = shift(memory_blocks[3], 3)
        ffn_far, ffn_beside, memory_blocks, first = meet(
            ffn_far, [swap(ffn_own, 1)], memory_blocks, first
        )
        ffn_beside += [swap(piece, 1) for piece in (*ffn_near, *ffn_far)]
        ffn_pieces = (ffn_own, *ffn_near, *ffn_far, *ffn_beside)
        cross_q, cross_low, cross_total, z2, second, kv = call(
            bound(cross_forward),
            [META] + in_vmem(5) + in_place(mp + 13),
            (
                low_shape,
                low_shape,
                shaped((mp, heads * slots, 1)),
                row_shape,
                row_shape,
                shaped((mp, 2 * local, mem_slots), BF16),
            ),
            [
                weights_shape,
                VMEM((width, mem_slots), BF16),
                flat_shape,
                stack_shape,
                kv_shape,
                dma,
            ],
            40 * matmul,
            8 * plain,
            "cross_forward",
            1,
        )(
            meta,
            cross_bias,
            *params,
            first,
            *memory_blocks,
            *head_pieces,
            own_cq,
            cross_proj,
            own_kv,
        )
        shared_shape = (mp + 1, slots, width + width // 2)
        result, dz2, ffn_sums, ffn_shared, ffn_half = call(
            bound(ffn_both),
            [META] + in_vmem(7) + in_place(12),
            (
                shaped((slots, width), BF16),
                row_shape,
                shaped((16, width)),
                shaped(shared_shape, BF16),
                shaped((mp + 1, slots, width // 2), BF16),
            ),
            [
                VMEM((mp, width, inner), BF16),
                VMEM((mp, inner, width), BF16),
                flat_shape,
                VMEM((mp, slots, inner), BF16),
                VMEM((mp, slots, inner), F32),
                VMEM((slots, width), BF16),
                dma,
            ],
            40 * matmul,
            10 * plain,
            "ffn_both",
        )(meta, second, z2, grad_row, inner_bias, *params, *ffn_pieces, ffn_in, ffn_out)
        ffn_theirs = swap(ffn_shared, 1)
        result_blocks = spread_line(result)
        cross_dq, dz1, cross_sums, cross_local, kv_low, *memory_grads = call(
            bound(cross_back),
            [META] + in_vmem(5) + in_place(14),
            (
                low_shape,
                row_shape,
                shaped((8, width)),
                shaped((mp, 2, local)),
                shaped((mp, 2 * local, mem_slots), BF16),
                *[shaped((local, mem_slots), BF16)] * mp,
            ),
            [
                VMEM((2, mp, 2 * local, width), BF16),
                kv_shape,
                kv_shape,
                VMEM((width, mem_slots), BF16),
                flat_shape,
                stack_shape,
                stack_shape,
                dma,
            ],
            50 * matmul,
            12 * plain,
            "cross_back",
            1 + mp,
        )(
            meta,
            dz2,
            cross_q,
            cross_total,
            z1,
            norm_gains,
            kv,
            *head_pieces,
            own_cq,
            cross_proj,
            own_kv,
        )
        result_blocks, memory_grads, kv_low, dz1, ffn_theirs = meet(
            result_blocks, memory_grads, kv_low, dz1, ffn_theirs
        )
        memory_out = [memory_grads[0]]
        memory_out += [shift(memory_grads[step], step) for step in (1, 2)]
        pair_slots = shaped((2, 2, 2 * width // SUB, width), BF16)
        to_two, to_four, ffn_rest = call(
            bound(ffn_weights),
            [META] + in_place(3),
            (pair_slots, pair_slots, shaped((4, 2, 2 * width // SUB, width), BF16)),
            [
                VMEM((mp + 1, 2 * slots, width + width // 2), BF16),
                VMEM((mp, 2, width // 2, width), BF16),
                dma,
            ],
            16 * matmul,
            8 * plain,
            "ffn_weights",
            3,
        )(meta, ffn_shared, ffn_half, ffn_theirs)
        ffn_from = swap(to_two, 2), swap(to_four, 4)
        dz1 = after(dz1, to_two)
        hidden_grad, small, head_beside, head_mine = call(
            bound(head_back),
            [META] + in_vmem(11) + in_place(mp + 13),
            (row_shape, shaped((24, width)), ffn_slots, ffn_slots),
            [
                weights_shape,
                kv_shape,
                VMEM((width, mem_slots), BF16),
                flat_shape,
                VMEM((slots, local), BF16),
                VMEM((slots, 3 * local), BF16),
                squares,
                VMEM((mp, 2, local), F32),
                dma,
            ],
            60 * matmul,
            24 * plain,
            "head_back",
            2,
        )(
            meta,
            dz1,
            hidden_row,
            qkv,
            self_low,
            dz2,
            first,
            cross_dq,
            cross_low,
            cross_sums,
            cross_local,
            ffn_sums,
            kv_low,
            *memory_blocks,
            *head_pieces,
            own_self,
            self_proj,
        )
        ffn_from, memory_out, memory_last, hidden_grad, small, head_beside, head_mine = meet(
            ffn_from, memory_out, memory_grads[3], hidden_grad, small, head_beside, head_mine
        )
        head_other = swap(head_beside, 1)
        ffn_group = Group(lambda slot, *at: ffn_rest[(slot - 4, *at)].astype(F32))
        late_two, late_four = ffn_group.second(*ffn_from)
        ffn_late = swap(late_two, 2), swap(late_four, 4)
        small = small + flip(small, 1)
        memory_out.append(shift(after(memory_last, small), 3))
        four_slots = VMEM((4, 2, 2 * width // SUB, width), BF16)
        to_two, to_four = call(
            add_slots,
            in_place(2),
            (pair_slots, pair_slots),
            [four_slots, four_slots, four_slots, dma],
            0,
            4 * plain,
            "add_slots",
            2,
        )(head_mine, head_other)
        to_two, to_four, head_other, ffn_late, memory_out, small = meet(
            to_two, to_four, head_other, ffn_late, memory_out, small
        )
        ffn_total, ffn_blocks = ffn_group.third(*ffn_from, *ffn_late)

        def head_summed(*slots):
            return head_mine[slots].astype(F32) + head_other[slots].astype(F32)

        head_group = Group(head_summed)
        head_from = swap(to_two, 2), swap(to_four, 4)
        ffn_sent = [flip(ffn_blocks[step - 1], step) for step in range(1, mp)]

        def joined(kernel, blocks, shape, dtype, name):
            return call(
                kernel, [META] + in_vmem(mp), (shaped(shape, dtype),), [], 0, 2 * plain, name
            )(meta, *blocks)[0]

        rows_shape = (mp * slots, width)
        memory_grad = joined(
            join_columns, memory_out, (local, mp * mem_slots), F32, "join_memory"
        )
        result = joined(join_rows, result_blocks, rows_shape, BF16, "join_result")
        head_from, ffn_sent, memory_grad, result, hidden_grad = meet(
            head_from, ffn_sent, memory_grad, result, hidden_grad
        )
        late_two, late_four = head_group.second(*head_from)
        head_late = swap(late_two, 2), swap(late_four, 4)
        hidden_low = hidden_grad.astype(BF16)
        hidden_blocks = [hidden_low, shift(hidden_low, 1), None, shift(hidden_low, 3)]
        small = after(small, hidden_blocks[1])
        bit = 2
        while bit < mp:
            small = small + flip(small, bit)
            bit *= 2
        ffn_low = line_sum(ffn_total, ffn_sent)
        small = small + swap(small, 1)
        bit = SUB
        while bit < dp:
            small = small + swap(small, bit)
            bit *= 2
        head_late, ffn_low, small, hidden_blocks = meet(
            head_late, ffn_low, small, hidden_blocks
        )
        head_total, head_blocks = head_group.third(*head_from, *head_late)
        ffn_low, head_blocks = meet(ffn_low, head_blocks)
        head_sent = [flip(head_blocks[step - 1], step) for step in range(1, mp)]
        ffn_near = near_chips(ffn_low)
        small, *ffn_near = meet(small, *ffn_near)
        small = small + swap(small, 2)
        small = small + swap(small, 4)
        ffn_near[0], _ = meet(ffn_near[0], head_sent[0])
        ffn_far = far_chips(*ffn_near)
        ffn_reduced = (ffn_low, *ffn_near, *ffn_far)
        ffn_joined = jnp.concatenate(ffn_reduced)
        head_sent, ffn_reduced, ffn_joined, small, hidden_blocks = meet(
            head_sent, ffn_reduced, ffn_joined, small, hidden_blocks
        )
        head_low = line_sum(head_total, head_sent)
        head_near = near_chips(head_low)
        hidden_blocks[2] = shift(hidden_blocks[0], 2)
        ffn_joined = swap(ffn_joined, 1)
        grad_in, grad_out = call(
            finish_ffn,
            [META] + in_vmem(6),
            (shaped((width, inner)), shaped((inner, width))),
            [],
            0,
            plain,
            "finish_ffn",
        )(meta, *ffn_reduced, ffn_joined)
        head_near, grad_in, grad_out, hidden_blocks = meet(
            head_near, grad_in, grad_out, hidden_blocks
        )
        hidden_grad = joined(join_rows, hidden_blocks, rows_shape, F32, "join_hidden")
        head_far = far_chips(*head_near)
        head_beside = [swap(piece, 1) for piece in (head_low, *head_near)]
        head_far, head_beside, hidden_grad = meet(head_far, head_beside, hidden_grad)
        head_beside += [swap(piece, 1) for piece in head_far]
        finished = call(
            finish_heads,
            [META] + in_vmem(11),
            (
                shaped((3 * local, width)),
                shaped((local, width)),
                shaped((local, width)),
                shaped((local, width)),
                shaped((2 * local, width)),
                shaped((3, width)),
                shaped((3, width)),
                shaped((3, width)),
                shaped((2, local)),
                shaped((2, local)),
                shaped((inner,)),
            ),
            [],
            0,
            plain,
            "finish_heads",
        )(meta, small, head_low, *head_near, *head_far, *head_beside)
        grad_self, grad_sp, grad_cq, grad_cp, grad_kv = finished[:5]
        return (
            result,
            hidden_grad,
            memory_grad.T,
            jnp.swapaxes(grad_self.reshape(3, local, width), 1, 2),
            finished[8],
            grad_sp,
            grad_cq.T,
            jnp.swapaxes(grad_kv.reshape(2, local, width), 1, 2),
            finished[9],
            grad_cp,
            grad_in,
            finished[10],
            grad_out,
            *finished[5:8],
        )

    return jax.shard_map(
        body,
        mesh=mesh,
        in_specs=(
            P("dp", None),
            P("dp", "mp"),
            P("dp", None),
            P("dp", None),
            P("dp"),
            P("dp", None),
            P("dp"),
            P(None, None, "mp"),
            P(None, "mp"),
            P("mp", None),
            P(None, "mp"),
            P(None, None, "mp"),
            P(None, "mp"),
            P("mp", None),
            P(None, "mp"),
            P("mp"),
            P("mp", None),
            P(),
            P(),
            P(),
        ),
        out_specs=(
            P("dp", None),
            P("dp", None),
            P("dp", "mp"),
            P(None, None, "mp"),
            P(None, "mp"),
            P("mp", None),
            P(None, "mp"),
            P(None, None, "mp"),
            P(None, "mp"),
            P("mp", None),
            P(None, "mp"),
            P("mp"),
            P("mp", None),
            P(),
            P(),
            P(),
        ),
        check_vma=False,
    )
```

```python
import jax
import jax.numpy as jnp
from jax import lax
from jax.experimental import pallas as pl
from jax.experimental.pallas import tpu as pltpu
from jax.sharding import PartitionSpec as P

HD = 64
SUB = 8
NEG_FILL = -1000000000.0
EPSILON = 1e-05
F32 = jnp.float32
BF16 = jnp.bfloat16
VMEM = pltpu.VMEM
ROOT_HALF = 0.7071067811865476
ROOT_TWO_PI = 0.3989422804014327
SLOTS = ((3, 0), (1, 0), (3, 1), (2, 1), (1, 1), (2, 0), (0, 0), (0, 1))


def nn(left, right):
    return lax.dot_general(left, right, (((1,), (0,)), ((), ())), preferred_element_type=F32)


def nt(left, right):
    return lax.dot_general(left, right, (((1,), (1,)), ((), ())), preferred_element_type=F32)


def tn(left, right):
    return lax.dot_general(left, right, (((0,), (0,)), ((), ())), preferred_element_type=F32)


def normed(values):
    average = jnp.mean(values, -1, keepdims=True)
    centered = values - average
    variance = jnp.mean(centered * centered, -1, keepdims=True)
    inverse = lax.rsqrt(variance + EPSILON)
    return centered * inverse, inverse


def norm_back(unit, inverse, gain, grad):
    scaled = grad * gain
    return (
        scaled
        - jnp.mean(scaled, -1, keepdims=True)
        - unit * jnp.mean(scaled * unit, -1, keepdims=True)
    ) * inverse


def row_sum(values):
    return jnp.sum(values, 0, keepdims=True)


def segments(meta, start, count, shape, axis):
    places = lax.broadcasted_iota(jnp.int32, shape, axis)
    found = jnp.zeros(shape, jnp.int32) - 1
    for j in range(count):
        found = found + (meta[start + j] <= places).astype(jnp.int32)
    return found, places


def fetch(pieces, place, target, low, high, sems):
    size = high - low
    blocks, rows = pieces[0].shape[:2]
    half = rows // 2
    for block in range(blocks):
        sem = sems.at[block + 1]
        for beside in (0, 1):
            whole = pieces[5 * beside : 5 * beside + 3]
            split = pieces[5 * beside + 3 : 5 * beside + 5]
            for offset in range(4):
                row = (place ^ (offset + 4 * beside)) * size
                if offset < 3:
                    source = whole[offset].at[block, pl.ds(low, size)]
                    to = target.at[block + 1, pl.ds(pl.multiple_of(row, 16), size)]
                    pltpu.make_async_copy(source, to, sem).start()
                    continue
                for part in range(low // half, high // half):
                    at = 2 * block + part
                    source = split[at // blocks].at[at % blocks]
                    start = pl.multiple_of(row + part * half - low, 16)
                    to = target.at[block + 1, pl.ds(start, half)]
                    pltpu.make_async_copy(source, to, sem).start()


def fetch_own(sources, target, sems):
    row = 0
    for source in sources:
        size = source.shape[0]
        pltpu.make_async_copy(source, target.at[0, pl.ds(row, size)], sems.at[0]).start()
        row += size


def arrive(target, sem):
    pltpu.make_async_copy(target, target, sem).wait()


def fetch_halves(pieces, owns, place, target, sems):
    own_cq, own_cp, own_kv = owns
    size = own_cq.shape[0]
    pltpu.make_async_copy(own_cq, target.at[0, 0, pl.ds(0, size)], sems.at[0, 0]).start()
    pltpu.make_async_copy(own_cp, target.at[0, 0, pl.ds(size, size)], sems.at[0, 0]).start()
    pltpu.make_async_copy(own_kv, target.at[1, 0], sems.at[1, 0]).start()
    blocks, rows = pieces[0].shape[:2]
    size = rows // 2
    for block in range(blocks):
        for index in range(8):
            offset = index % 4
            mine = pieces[5 * (index // 4) :]
            position = place ^ index
            plane = lax.div(position, 4)
            row = pl.multiple_of(lax.rem(position, 4) * size, 16)
            if offset < 3:
                source = mine[offset].at[block, pl.ds(size, size)]
            else:
                at = 2 * block + 1
                source = mine[3 + at // blocks].at[at % blocks]
            to = target.at[plane, block + 1, pl.ds(row, size)]
            pltpu.make_async_copy(source, to, sems.at[plane, block + 1]).start()


def fetch_memory(blocks, line, target, sem):
    count = len(blocks)
    for step, block in enumerate(blocks):
        size = block.shape[0]
        row = pl.multiple_of(lax.rem(line + count - step, count) * size, 16)
        pltpu.make_async_copy(block, target.at[pl.ds(row, size)], sem).start()


def slot_of(offset, half):
    first = SLOTS.index((offset, 0))
    second = SLOTS.index((offset, 1))
    return jnp.where(half == 0, first, second)


def self_mask(meta, nseg, slots):
    shape = (slots, slots)
    query_segment, query_place = segments(meta, 4, nseg, shape, 0)
    key_segment, key_place = segments(meta, 4, nseg, shape, 1)
    return (query_segment == key_segment) & (key_place <= query_place) & (key_place < meta[2])


def self_forward(dims, meta, x_ref, sb, ob, gain, bias, *refs):
    mp, local, heads, scaling, nseg = dims
    pieces, (own_self, own_sp) = refs[:10], refs[10:12]
    qkv, low, z1, first = refs[12:16]
    ws, acc, sems = refs[16:]
    fetch_own((own_self, own_sp), ws, sems.at[0])
    fetch(pieces, meta[0], ws, 0, 96, sems.at[0])
    allowed = self_mask(meta, nseg, x_ref.shape[0])
    acc[...] = x_ref[...].astype(F32) + ob[0:1]

    def step(z, carry):
        arrive(ws.at[z], sems.at[0, z])
        flat = nt(x_ref[...], ws[z, : 3 * local])
        rows = sb[z]
        qkv[z, :, :local] = ((flat[:, :local] + rows[0:1]) * scaling).astype(BF16)
        qkv[z, :, local : 2 * local] = flat[:, local : 2 * local].astype(BF16)
        qkv[z, :, 2 * local :] = (flat[:, 2 * local :] + rows[1:2]).astype(BF16)
        for i in range(heads):
            at = HD * i
            scores = nt(qkv[z, :, at : at + HD], qkv[z, :, local + at : local + at + HD])
            scores = jnp.where(allowed, scores, NEG_FILL)
            weights = jnp.exp(scores - jnp.max(scores, -1, keepdims=True))
            probs = (weights * (1.0 / jnp.sum(weights, -1, keepdims=True))).astype(BF16)
            out = nn(probs, qkv[z, :, 2 * local + at : 2 * local + at + HD])
            low[z, :, at : at + HD] = out.astype(BF16)
        acc[...] += nn(low[z], ws[z, 3 * local :])
        return carry

    lax.fori_loop(0, mp, step, 0)
    z1[...] = acc[...]
    unit, _ = normed(acc[...])
    first[...] = unit * gain[0:1] + bias[0:1]


def put_heads(target, source, heads):
    rows = source.shape[0]
    for i in range(heads):
        columns = slice(HD * i, HD * (i + 1))
        target[rows * i : rows * (i + 1), columns] = source[:, columns]


def masked(scores, allowed):
    shape = scores.shape
    scores = scores.reshape((-1,) + allowed.shape)
    return jnp.where(allowed[None], scores, NEG_FILL).reshape(shape)


def cross_mask(meta, nseg, slots, mem_slots):
    query_segment, _ = segments(meta, 4, nseg, (slots, 1), 0)
    key_segment, key_place = segments(meta, 4 + nseg, nseg, (1, mem_slots), 1)
    key_segment = jnp.where(key_place < meta[3], key_segment, -1)
    return query_segment == key_segment


def fetch_cross(pieces, owns, place, target, sem):
    fetch_own(owns, target, sem)
    fetch(pieces, place, target, 96, 192, sem)


def cross_forward(dims, meta, cb, ob, gain, bias, first, *refs):
    mp, local, heads, scaling, nseg = dims
    blocks, pieces, owns = refs[:mp], refs[mp : mp + 10], refs[mp + 10 : mp + 13]
    cq, low, total, z2, second, kv = refs[mp + 13 : mp + 19]
    wc, mem, acc, stacked, both, sems = refs[mp + 19 :]
    fetch_memory(blocks, meta[1], mem, sems.at[1, 0])
    fetch_cross(pieces, owns, meta[0], wc, sems.at[0])
    slots = first.shape[0]
    allowed = cross_mask(meta, nseg, slots, mem.shape[1])
    acc[...] = first[...] + ob[1:2]
    stacked[...] = jnp.zeros_like(stacked)
    first_low = first[...].astype(BF16)
    arrive(mem, sems.at[1, 0])

    def step(z, carry):
        arrive(wc.at[z], sems.at[0, z])
        rows = cb[z]
        query = ((nt(first_low, wc[z, :local]) + rows[0:1]) * scaling).astype(BF16)
        cq[z] = query
        put_heads(stacked, query, heads)
        flat = nn(wc[z, 2 * local :], mem[...])
        column = jnp.swapaxes(jnp.broadcast_to(rows[1:2], (8, local)), 0, 1)[:, :1]
        keys = flat[:local].astype(BF16)
        values = (flat[local:] + column).astype(BF16)
        both[z, :local] = keys
        both[z, local:] = values
        pltpu.make_async_copy(both.at[z], kv.at[z], sems.at[2, 0]).start()
        scores = masked(nn(stacked[...], keys), allowed)
        peak = jnp.max(scores, -1, keepdims=True)
        weights = jnp.exp(scores - peak)
        mass = jnp.sum(weights, -1, keepdims=True)
        probs = (weights * (1.0 / mass)).astype(BF16)
        total[z] = peak + jnp.log(mass)
        out = nt(probs, values)
        for i in range(heads):
            columns = slice(HD * i, HD * (i + 1))
            low[z, :, columns] = out[slots * i : slots * (i + 1), columns].astype(BF16)
        acc[...] += nn(low[z], wc[z, local : 2 * local])
        return carry

    lax.fori_loop(0, mp, step, 0)
    z2[...] = acc[...]
    unit, _ = normed(acc[...])
    second[...] = unit * gain[1:2] + bias[1:2]
    arrive(both, sems.at[2, 0])


def put_slots(beside, mine, place, z, base, source, sem):
    half = lax.div(z, 2)
    at = lax.rem(z, 2)
    size = source.shape[0] // SUB
    for offset in range(4):
        slot = slot_of(offset, half)
        for target, flip in ((mine, 0), (beside, 4)):
            row = pl.multiple_of((place ^ (offset + flip)) * size, 16)
            to = target.at[slot, at, pl.ds(base, size)]
            pltpu.make_async_copy(source.at[pl.ds(row, size)], to, sem).start()


def ffn_both(dims, meta, second, z2, grad, ib, ob, gain, bias, *refs):
    mp, local, heads, scaling, nseg = dims
    pieces, (own_in, own_out) = refs[:10], refs[10:12]
    result, dz2, sums, shared, own_half = refs[12:17]
    win, wout, acc, act, slope, low, sems = refs[17:]
    place = meta[0]
    width = second.shape[1]
    half = width // 2
    mine = pl.multiple_of(lax.div(place, 4) * half, 128)
    other = pl.multiple_of((1 - lax.div(place, 4)) * half, 128)
    fetch_own((own_in,), win, sems.at[0])
    fetch_own((own_out,), wout, sems.at[1])
    fetch(pieces, place, win, 0, 96, sems.at[0])
    fetch(pieces, place, wout, 96, 192, sems.at[1])
    acc[...] = second[...] + ob[2:3]
    low[...] = second[...].astype(BF16)
    own_half[0] = low[:, pl.ds(mine, half)]
    shared[0, :, width:] = low[:, pl.ds(other, half)]

    def forward(z, carry):
        arrive(win.at[z], sems.at[0, z])
        arrive(wout.at[z], sems.at[1, z])
        inner = nn(low[...], win[z]) + ib[z]
        share = 0.5 * (1.0 + lax.erf(inner * ROOT_HALF))
        act[z] = (inner * share).astype(BF16)
        own_half[z + 1] = act[z, :, pl.ds(mine, half)]
        shared[z + 1, :, width:] = act[z, :, pl.ds(other, half)]
        slope[z] = share + inner * (ROOT_TWO_PI * jnp.exp(-0.5 * inner * inner))
        acc[...] += nn(act[z], wout[z])
        return carry

    lax.fori_loop(0, mp, forward, 0, unroll=True)
    unit, inverse = normed(acc[...])
    result[...] = (unit * gain[2:3] + bias[2:3]).astype(BF16)
    out_grad = grad[...].astype(F32)
    third = norm_back(unit, inverse, gain[2:3], out_grad)
    sums[...] = jnp.zeros_like(sums)
    sums[0:1] = row_sum(third)
    sums[1:2] = row_sum(out_grad * unit)
    sums[2:3] = row_sum(out_grad)
    third_low = third.astype(BF16)
    shared[0, :, :width] = third_low
    acc[...] = third

    def backward(z, carry):
        inner = nt(third_low, wout[z]) * slope[z]
        sums[pl.ds(8 + z, 1)] = row_sum(inner)
        inner_low = inner.astype(BF16)
        acc[...] += nt(inner_low, win[z])
        shared[z + 1, :, :width] = inner_low
        return carry

    lax.fori_loop(0, mp, backward, 0, unroll=True)
    unit, inverse = normed(z2[...])
    grad_rows = acc[...]
    values = norm_back(unit, inverse, gain[1:2], grad_rows)
    dz2[...] = values
    sums[3:4] = row_sum(values)
    sums[4:5] = row_sum(grad_rows * unit)
    sums[5:6] = row_sum(grad_rows)


def ffn_weights(dims, meta, shared, own_half, theirs, to_two, to_four, rest, rows, dw, sems):
    mp = dims[0]
    slots = shared.shape[1]
    width = rows.shape[2] - own_half.shape[2]
    for i in range(mp + 1):
        sem = sems.at[i % mp, i // mp]
        part = rows.at[i, pl.ds(0, slots)]
        pltpu.make_async_copy(shared.at[i, :, pl.ds(0, width)], part.at[:, pl.ds(0, width)], sem).start()
        pltpu.make_async_copy(own_half.at[i], part.at[:, pl.ds(width, width // 2)], sem).start()
        pltpu.make_async_copy(theirs.at[i], rows.at[i, pl.ds(slots, slots)], sem).start()
    arrive(rows.at[0], sems.at[0, 0])
    for z in range(mp):
        i = z + 1
        arrive(rows.at[i], sems.at[i % mp, i // mp])
        dw[z, 0] = tn(rows[0, :, width:], rows[i, :, :width]).astype(BF16)
        dw[z, 1] = tn(rows[i, :, width:], rows[0, :, :width]).astype(BF16)
        size = dw.shape[2] // 4
        for offset in range(4):
            slot = SLOTS.index((offset, z // 2))
            if slot < 4:
                target = (to_two, to_four)[slot // 2].at[slot % 2, z % 2]
            else:
                target = rest.at[slot - 4, z % 2]
            row = pl.multiple_of(((meta[0] ^ offset) & 3) * size, 16)
            for j in (0, 1):
                source = dw.at[z, j, pl.ds(row, size)]
                pltpu.make_async_copy(source, target.at[pl.ds(j * size, size)], sems.at[0, 2]).start()
    arrive(dw, sems.at[0, 2])


def cross_back(dims, meta, dz2, cq, total, z1, gain, *refs):
    mp, local, heads, scaling, nseg = dims
    kv_ref, pieces, owns = refs[0], refs[1:11], refs[11:14]
    dcq, dz1, sums, sums_local, kv_low = refs[14:19]
    mem_out = refs[19 : 19 + mp]
    wc, kv, kv_grad, dmem, acc, queries, grads, sems = refs[19 + mp :]
    for z in range(mp):
        pltpu.make_async_copy(kv_ref.at[z], kv.at[z], sems.at[2, z]).start()
    fetch_halves(pieces, owns, meta[0], wc, sems)
    slots = dz2.shape[0]
    allowed = cross_mask(meta, nseg, slots, kv.shape[2])
    queries[...] = jnp.zeros_like(queries)
    grads[...] = jnp.zeros_like(grads)
    dz2_low = dz2[...].astype(BF16)
    acc[...] = dz2[...]

    def step(z, carry):
        arrive(wc.at[0, z], sems.at[0, z])
        arrive(wc.at[1, z], sems.at[1, z])
        arrive(kv.at[z], sems.at[2, z])
        put_heads(queries, cq[z], heads)
        grad = nt(dz2_low, wc[0, z, local:]).astype(BF16)
        put_heads(grads, grad, heads)
        keys, values = kv[z, :local], kv[z, local:]
        probs = jnp.exp(masked(nn(queries[...], keys), allowed) - total[z])
        probs_low = probs.astype(BF16)
        prob_grad = nn(grads[...], values)
        offset = jnp.sum(probs * prob_grad, -1, keepdims=True)
        score_grad = (probs * (prob_grad - offset)).astype(BF16)
        kv_grad[z, :local] = tn(queries[...], score_grad).astype(BF16)
        kv_grad[z, local:] = tn(grads[...], probs_low).astype(BF16)
        pltpu.make_async_copy(kv_grad.at[z], kv_low.at[z], sems.at[3, 0]).start()
        mass = jnp.sum(probs_low.astype(F32), -1, keepdims=True)
        query_grad = nt(score_grad, keys) * scaling
        for i in range(heads):
            columns = slice(HD * i, HD * (i + 1))
            rows = slice(slots * i, slots * (i + 1))
            part = query_grad[rows, columns]
            dcq[z, :, columns] = part.astype(BF16)
            sums_local[z, 0:1, columns] = row_sum(part)
            sums_local[z, 1:2, columns] = row_sum(mass[rows] * grad[:, columns].astype(F32))
        acc[...] += nn(dcq[z], wc[0, z, :local])
        return carry

    lax.fori_loop(0, mp, step, 0)
    depth = mp * kv_grad.shape[1]
    product = tn(wc[1].reshape(depth, wc.shape[3]), kv_grad[...].reshape(depth, kv.shape[2]))
    dmem[...] = product.astype(BF16)
    for block in range(mp):
        row = pl.multiple_of(lax.rem(meta[1] + block, mp) * local, 16)
        source = dmem.at[pl.ds(row, local)]
        pltpu.make_async_copy(source, mem_out[block], sems.at[3, 1]).start()
    unit, inverse = normed(z1[...])
    grad_rows = acc[...]
    values = norm_back(unit, inverse, gain[0:1], grad_rows)
    dz1[...] = values
    sums[...] = jnp.zeros_like(sums)
    sums[0:1] = row_sum(values)
    sums[1:2] = row_sum(grad_rows * unit)
    sums[2:3] = row_sum(grad_rows)
    arrive(kv_grad, sems.at[3, 0])
    arrive(dmem, sems.at[3, 1])


def head_back(dims, meta, dz1, x_ref, qkv, self_low, dz2, first, dcq, cross_low, *refs):
    mp, local, heads, scaling, nseg = dims
    cross_sums, cross_local, ffn_sums = refs[:3]
    refs = refs[3:]
    kv_ref, blocks, pieces = refs[0], refs[1 : 1 + mp], refs[1 + mp : 11 + mp]
    own_self, own_sp = refs[11 + mp : 13 + mp]
    dx, small, beside, mine = refs[13 + mp : 17 + mp]
    ws, kv, mem, acc, dout, dqkv, dw, sums_local, sems = refs[17 + mp :]
    place = meta[0]
    fetch_own((own_self, own_sp), ws, sems.at[0])
    fetch(pieces, place, ws, 0, 96, sems.at[0])
    fetch_memory(blocks, meta[1], mem, sems.at[2, 0])
    for z in range(mp):
        pltpu.make_async_copy(kv_ref.at[z], kv.at[z], sems.at[1, z]).start()
    allowed = self_mask(meta, nseg, x_ref.shape[0])
    dz1_low = dz1[...].astype(BF16)
    dz2_low = dz2[...].astype(BF16)
    first_low = first[...].astype(BF16)
    acc[...] = dz1[...]
    arrive(mem, sems.at[2, 0])

    def step(z, carry):
        arrive(ws.at[z], sems.at[0, z])
        arrive(kv.at[z], sems.at[1, z])
        dout[...] = nt(dz1_low, ws[z, 3 * local :]).astype(BF16)
        for i in range(heads):
            at = HD * i
            query = qkv[z, :, at : at + HD]
            key = qkv[z, :, local + at : local + at + HD]
            value = qkv[z, :, 2 * local + at : 2 * local + at + HD]
            grad = dout[:, at : at + HD]
            scores = jnp.where(allowed, nt(query, key), NEG_FILL)
            weights = jnp.exp(scores - jnp.max(scores, -1, keepdims=True))
            probs = weights * (1.0 / jnp.sum(weights, -1, keepdims=True))
            prob_grad = nt(grad, value)
            offset = jnp.sum(probs * prob_grad, -1, keepdims=True)
            score_grad = (probs * (prob_grad - offset)).astype(BF16)
            value_grad = tn(probs.astype(BF16), grad)
            query_grad = nn(score_grad, key) * scaling
            dqkv[:, at : at + HD] = query_grad.astype(BF16)
            dqkv[:, local + at : local + at + HD] = tn(score_grad, query).astype(BF16)
            dqkv[:, 2 * local + at : 2 * local + at + HD] = value_grad.astype(BF16)
            sums_local[z, 0:1, at : at + HD] = row_sum(query_grad)
            sums_local[z, 1:2, at : at + HD] = row_sum(value_grad)
        acc[...] += nn(dqkv[...], ws[z, : 3 * local])
        dw[z, 0, : 3 * local] = tn(dqkv[...], x_ref[...]).astype(BF16)
        dw[z, 0, 3 * local :] = tn(self_low[z], dz1_low).astype(BF16)
        put_slots(beside, mine, place, z, 0, dw.at[z, 0], sems.at[3, 0])
        dw[z, 1, :local] = tn(dcq[z], first_low).astype(BF16)
        dw[z, 1, local : 2 * local] = tn(cross_low[z], dz2_low).astype(BF16)
        dw[z, 1, 2 * local :] = nt(kv[z], mem[...]).astype(BF16)
        put_slots(beside, mine, place, z, 96, dw.at[z, 1], sems.at[3, 0])
        return carry

    lax.fori_loop(0, mp, step, 0)
    dx[...] = acc[...]
    small[...] = jnp.zeros_like(small)
    small[0:3] = cross_sums[0:3]
    small[3:9] = ffn_sums[0:6]

    def collect(z, carry):
        row = 9 + 2 * (meta[1] ^ z)
        for i, part in enumerate((sums_local, cross_local)):
            for j in (0, 1):
                at = (2 * i + j) * local
                small[pl.ds(row, 1), at : at + local] = part[z, j : j + 1]
        small[pl.ds(row + 1, 1)] = ffn_sums[pl.ds(8 + z, 1)]
        return carry

    lax.fori_loop(0, mp, collect, 0)
    arrive(dw, sems.at[3, 0])


def place_rows(place, ranges, pieces):
    half = pieces[3].shape[0]

    def taken(offset, start, size):
        mine = pieces[5 * (offset // 4) :]
        offset = offset % 4
        if offset < 3:
            return mine[offset][pl.ds(start, size)]
        if start < half:
            return mine[3][pl.ds(start, size)]
        return mine[4][pl.ds(start - half, size)]

    for offset in range(8):
        position = place ^ offset
        for start, size, targets in ranges:
            if offset % 4 == 3 and start < half < start + size:
                parts = ((start, half - start), (half, start + size - half))
            else:
                parts = ((start, size),)
            for begin, length in parts:
                source = taken(offset, begin, length).astype(F32)
                first = 0
                for target in targets:
                    count = target.shape[0] // size

                    @pl.when((position >= first) & (position < first + count))
                    def _():
                        row = (position - first) * size + (begin - start)
                        target[pl.ds(pl.multiple_of(row, 8), length)] = source

                    first += count


def finish_heads(meta, small, *refs):
    place_rows(meta[0], ((0, 96, refs[10:12]), (96, 96, refs[12:15])), refs[:10])
    shared, sharded = refs[15:18], refs[18:]
    for i, target in enumerate(shared):
        for j, row in enumerate((0, 6, 3)):
            target[j : j + 1] = small[row + i : row + i + 1]
    row = 9 + 2 * meta[1]
    local = sharded[0].shape[1]
    for i in (0, 1):
        for j in (0, 1):
            at = (2 * i + j) * local
            sharded[i][j : j + 1] = small[pl.ds(row, 1), at : at + local]
    sharded[2][...] = small[pl.ds(row + 1, 1)].reshape(sharded[2].shape)


def finish_ffn(meta, *refs):
    gi, go = refs[6:]
    pieces, joined = list(refs[:5]), refs[5]
    row = 0
    for piece in refs[:5]:
        pieces.append(joined.at[pl.ds(row, piece.shape[0])])
        row += piece.shape[0]
    place_rows(meta[0], ((0, 96, (gi,)), (96, 96, (go,))), pieces)


def add_slots(mine, other, to_two, to_four, left, right, out, sems):
    count = out.shape[0]
    for i in range(count):
        pltpu.make_async_copy(mine.at[i], left.at[i], sems.at[0, i]).start()
        pltpu.make_async_copy(other.at[i], right.at[i], sems.at[1, i]).start()
    for i in range(count):
        arrive(left.at[i], sems.at[0, i])
        arrive(right.at[i], sems.at[1, i])
        out[i] = (left[i].astype(F32) + right[i].astype(F32)).astype(BF16)
        target = (to_two, to_four)[i // 2].at[i % 2]
        pltpu.make_async_copy(out.at[i], target, sems.at[2, 0]).start()
    arrive(out, sems.at[2, 0])


def join_columns(meta, *refs):
    blocks, target = refs[:-1], refs[-1]
    count = len(blocks)
    for step, block in enumerate(blocks):
        size = block.shape[1]
        at = pl.multiple_of(lax.rem(meta[1] + count - step, count) * size, 128)
        target[:, pl.ds(at, size)] = block[...].astype(target.dtype)


def join_rows(meta, *refs):
    blocks, target = refs[:-1], refs[-1]
    count = len(blocks)
    for step, block in enumerate(blocks):
        size = block.shape[0]
        at = pl.multiple_of(lax.rem(meta[1] + count - step, count) * size, 16)
        target[pl.ds(at, size)] = block[...].astype(target.dtype)


def shaped(shape, dtype=F32):
    return jax.ShapeDtypeStruct(shape, dtype)


def in_vmem(count):
    return [pl.BlockSpec(memory_space=pltpu.VMEM)] * count


def in_place(count):
    return [pl.BlockSpec(memory_space=pl.ANY)] * count


META = pl.BlockSpec(memory_space=pltpu.SMEM)


ROOM = dict(finish_heads=14, finish_ffn=14, join_result=14, join_hidden=14, join_memory=14)


def call(kernel, in_specs, outs, scratch, flops, moved, name, written=0):
    return pl.pallas_call(
        kernel,
        out_shape=outs,
        in_specs=in_specs,
        out_specs=in_vmem(len(outs) - written) + in_place(written),
        scratch_shapes=scratch,
        name=name,
        compiler_params=pltpu.CompilerParams(vmem_limit_bytes=ROOM.get(name, 60) * 1024 * 1024),
        cost_estimate=pl.CostEstimate(
            flops=flops // 16, bytes_accessed=moved // 4, transcendentals=0
        ),
    )


def solution(mesh):
    dp = mesh.shape["dp"]
    mp = mesh.shape["mp"]

    def swap(value, bit):
        return lax.ppermute(value, "dp", [(i, i ^ bit) for i in range(dp)])

    def shift(value, step):
        return lax.ppermute(value, "mp", [(i, (i + step) % mp) for i in range(mp)])

    def flip(value, bit):
        return lax.ppermute(value, "mp", [(i, i ^ bit) for i in range(mp)])

    def after(value, *others):
        return lax.optimization_barrier((value,) + others)[0] if others else value

    def meet(*values):
        return lax.optimization_barrier(values)

    def near_chips(own):
        return swap(own, 2), swap(own, 4)

    def far_chips(over_two, over_four):
        def halves(piece):
            if piece.ndim == 3:
                piece = piece.reshape(-1, piece.shape[1] // 2, piece.shape[2])
            half = piece.shape[0] // 2
            return piece[:half], piece[half:]

        return swap(halves(over_four)[0], 2), swap(halves(over_two)[1], 4)

    def beside(pieces):
        found = []
        for piece in pieces:
            found.append(swap(after(piece, *found[-1:]), 1))
        return found

    class Group:
        def __init__(self, summed):
            self.summed = summed

        def second(self, from_two, from_four):
            late_two = (self.summed(4) + from_four[0].astype(F32)).astype(BF16)
            late_four = (self.summed(5) + from_two[0].astype(F32)).astype(BF16)
            return late_two, late_four

        def third(self, from_two, from_four, late_two, late_four):
            blocks = []
            for slot, near, late in ((6, from_two, late_four), (7, from_four, late_two)):
                for i in (0, 1):
                    total = self.summed(slot, i) + near[1, i].astype(F32) + late[i].astype(F32)
                    bit = SUB
                    while bit < dp:
                        total = total + swap(total, bit)
                        bit *= 2
                    blocks.append(total)
            return blocks[0], [block.astype(BF16) for block in blocks[1:]]

    def line_sum(total, sent):
        for piece in sent:
            total = total + piece.astype(F32)
        return total.astype(BF16)

    def body(
        hidden,
        memory,
        out_grad,
        dec_starts,
        dec_length,
        mem_starts,
        mem_length,
        self_qkv,
        self_qv_bias,
        self_proj,
        cross_query,
        cross_kv,
        cross_qv_bias,
        cross_proj,
        ffn_in,
        ffn_in_bias,
        ffn_out,
        out_biases,
        norm_gains,
        norm_biases,
    ):
        row_count = dec_starts.shape[0]
        assert row_count == mp == 4 and dp % SUB == 0
        slots = hidden.shape[0] // row_count
        mem_slots = memory.shape[0] // row_count
        width = hidden.shape[1]
        local = self_proj.shape[0]
        heads = local // HD
        inner = ffn_out.shape[0]
        nseg = dec_starts.shape[1]
        dims = (mp, local, heads, HD ** (-0.5), nseg)
        line = lax.axis_index("mp")
        device = lax.axis_index("dp") % SUB
        place = (device & 1) * 4 + device // 2

        def row_of(array, size):
            return lax.dynamic_slice_in_dim(array, line * size, size, 0)

        def slice_of(array):
            size = array.shape[0] // SUB
            return lax.dynamic_slice_in_dim(array, place * size, size, 0)

        meta = jnp.concatenate(
            [
                jnp.stack([place, line]).astype(jnp.int32),
                row_of(dec_length, 1),
                row_of(mem_length, 1),
                row_of(dec_starts, 1)[0],
                row_of(mem_starts, 1)[0],
            ]
        )
        own_self = jnp.swapaxes(self_qkv, 1, 2).reshape(3 * local, width)
        own_cq = cross_query.T
        own_kv = jnp.swapaxes(cross_kv, 1, 2).reshape(2 * local, width)

        bias = jnp.concatenate(
            [self_qv_bias.reshape(-1), cross_qv_bias.reshape(-1), ffn_in_bias]
        ).reshape(-1, width)
        terms = []
        rest = bias
        for _ in range(3):
            term = lax.reduce_precision(rest, 8, 7)
            terms.append(term.astype(BF16))
            rest = rest - term
        bias_rows = 3 * bias.shape[0]
        terms = jnp.concatenate(terms + [jnp.zeros((16 - bias_rows, width), BF16)])
        head_piece = jnp.concatenate(
            [
                slice_of(jnp.concatenate([own_self, self_proj])),
                slice_of(jnp.concatenate([own_cq, cross_proj, own_kv])),
                terms,
            ]
        )
        ffn_piece = jnp.concatenate([slice_of(ffn_in), slice_of(ffn_out)])
        memory_t = memory.T
        memory_blocks = [
            lax.dynamic_slice_in_dim(memory_t, ((line + step) % mp) * mem_slots, mem_slots, 1)
            for step in range(mp)
        ]
        head_line = [flip(head_piece, step) for step in range(1, mp)]
        rows = head_piece.shape[0] - 16
        head_own = jnp.stack([piece[:rows] for piece in head_line])
        head_near = near_chips(head_own)
        ffn_piece = after(ffn_piece, *head_line)
        ffn_line = [flip(ffn_piece, step) for step in range(1, mp)]
        biases = [bias]
        for piece in head_line:
            term = piece[rows : rows + bias_rows].reshape(3, -1, width).astype(F32)
            biases.append((term[0] + term[1]) + term[2])
        biases = jnp.stack(biases).reshape(mp, -1)
        self_bias = biases[:, : 2 * local].reshape(mp, 2, local)
        cross_bias = biases[:, 2 * local : 4 * local].reshape(mp, 2, local)
        inner_bias = biases[:, None, 4 * local :]
        hidden_row = row_of(hidden, slots)
        grad_row = row_of(out_grad, slots)
        early = (meta, self_bias, cross_bias, inner_bias, hidden_row, grad_row)
        head_own, head_near, ffn_line, memory_blocks, early = meet(
            head_own, head_near, ffn_line, memory_blocks, early
        )
        meta, self_bias, cross_bias, inner_bias, hidden_row, grad_row = early
        head_far = far_chips(*head_near)
        head_beside = [swap(head_own, 1), swap(head_near[0], 1)]
        memory_blocks[1] = shift(memory_blocks[1], 1)
        ffn_own = jnp.stack(ffn_line)
        head_own, head_near, head_far, head_beside, ffn_own, memory_blocks = meet(
            head_own, head_near, head_far, head_beside, ffn_own, memory_blocks
        )
        head_beside += beside((head_near[1], *head_far))
        head_pieces = (head_own, *head_near, *head_far, *head_beside)
        ffn_near = near_chips(ffn_own)
        memory_blocks[2] = shift(memory_blocks[2], 2)
        params = (out_biases, norm_gains, norm_biases)
        dma = pltpu.SemaphoreType.DMA((4, mp))
        squares = VMEM((mp, 2, width, width), BF16)
        weights_shape = VMEM((mp, 4 * local, width), BF16)
        flat_shape = VMEM((slots, width), F32)
        kv_shape = VMEM((mp, 2 * local, mem_slots), BF16)
        stack_shape = VMEM((heads * slots, local), BF16)
        row_shape = shaped((slots, width))
        low_shape = shaped((mp, slots, local), BF16)
        head_slots = shaped((8, 2, 4 * local // SUB, width), BF16)
        ffn_slots = shaped((8, 2, 2 * width // SUB, width), BF16)
        matmul = 2 * slots * width * width
        plain = width * width * 2

        def spread_line(rows):
            return [rows] + [shift(rows, step) for step in range(1, mp)]

        def bound(kernel):
            return lambda *refs: kernel(dims, *refs)

        qkv, self_low, z1, first = call(
            bound(self_forward),
            [META] + in_vmem(5) + in_place(12),
            (shaped((mp, slots, 3 * local), BF16), low_shape, row_shape, row_shape),
            [weights_shape, flat_shape, dma],
            20 * matmul,
            8 * plain,
            "self_forward",
        )(meta, hidden_row, self_bias, *params, *head_pieces, own_self, self_proj)
        ffn_own, ffn_near, memory_blocks, qkv, self_low, z1, first = meet(
            ffn_own, ffn_near, memory_blocks, qkv, self_low, z1, first
        )
        ffn_far = far_chips(*ffn_near)
        memory_blocks[3] = shift(memory_blocks[3], 3)
        ffn_far, ffn_beside, memory_blocks, first = meet(
            ffn_far, [swap(ffn_own, 1)], memory_blocks, first
        )
        ffn_beside += [swap(piece, 1) for piece in (*ffn_near, *ffn_far)]
        ffn_pieces = (ffn_own, *ffn_near, *ffn_far, *ffn_beside)
        cross_q, cross_low, cross_total, z2, second, kv = call(
            bound(cross_forward),
            [META] + in_vmem(5) + in_place(mp + 13),
            (
                low_shape,
                low_shape,
                shaped((mp, heads * slots, 1)),
                row_shape,
                row_shape,
                shaped((mp, 2 * local, mem_slots), BF16),
            ),
            [
                weights_shape,
                VMEM((width, mem_slots), BF16),
                flat_shape,
                stack_shape,
                kv_shape,
                dma,
            ],
            40 * matmul,
            8 * plain,
            "cross_forward",
            1,
        )(
            meta,
            cross_bias,
            *params,
            first,
            *memory_blocks,
            *head_pieces,
            own_cq,
            cross_proj,
            own_kv,
        )
        shared_shape = (mp + 1, slots, width + width // 2)
        result, dz2, ffn_sums, ffn_shared, ffn_half = call(
            bound(ffn_both),
            [META] + in_vmem(7) + in_place(12),
            (
                shaped((slots, width), BF16),
                row_shape,
                shaped((16, width)),
                shaped(shared_shape, BF16),
                shaped((mp + 1, slots, width // 2), BF16),
            ),
            [
                VMEM((mp, width, inner), BF16),
                VMEM((mp, inner, width), BF16),
                flat_shape,
                VMEM((mp, slots, inner), BF16),
                VMEM((mp, slots, inner), F32),
                VMEM((slots, width), BF16),
                dma,
            ],
            40 * matmul,
            10 * plain,
            "ffn_both",
        )(meta, second, z2, grad_row, inner_bias, *params, *ffn_pieces, ffn_in, ffn_out)
        ffn_theirs = swap(ffn_shared, 1)
        result_blocks = spread_line(result)
        cross_dq, dz1, cross_sums, cross_local, kv_low, *memory_grads = call(
            bound(cross_back),
            [META] + in_vmem(5) + in_place(14),
            (
                low_shape,
                row_shape,
                shaped((8, width)),
                shaped((mp, 2, local)),
                shaped((mp, 2 * local, mem_slots), BF16),
                *[shaped((local, mem_slots), BF16)] * mp,
            ),
            [
                VMEM((2, mp, 2 * local, width), BF16),
                kv_shape,
                kv_shape,
                VMEM((width, mem_slots), BF16),
                flat_shape,
                stack_shape,
                stack_shape,
                dma,
            ],
            50 * matmul,
            12 * plain,
            "cross_back",
            1 + mp,
        )(
            meta,
            dz2,
            cross_q,
            cross_total,
            z1,
            norm_gains,
            kv,
            *head_pieces,
            own_cq,
            cross_proj,
            own_kv,
        )
        result_blocks, memory_grads, kv_low, dz1, ffn_theirs = meet(
            result_blocks, memory_grads, kv_low, dz1, ffn_theirs
        )
        memory_out = [memory_grads[0]]
        memory_out += [shift(memory_grads[step], step) for step in (1, 2)]
        pair_slots = shaped((2, 2, 2 * width // SUB, width), BF16)
        to_two, to_four, ffn_rest = call(
            bound(ffn_weights),
            [META] + in_place(3),
            (pair_slots, pair_slots, shaped((4, 2, 2 * width // SUB, width), BF16)),
            [
                VMEM((mp + 1, 2 * slots, width + width // 2), BF16),
                VMEM((mp, 2, width // 2, width), BF16),
                dma,
            ],
            16 * matmul,
            8 * plain,
            "ffn_weights",
            3,
        )(meta, ffn_shared, ffn_half, ffn_theirs)
        ffn_from = swap(to_two, 2), swap(to_four, 4)
        dz1 = after(dz1, to_two)
        hidden_grad, small, head_beside, head_mine = call(
            bound(head_back),
            [META] + in_vmem(11) + in_place(mp + 13),
            (row_shape, shaped((24, width)), ffn_slots, ffn_slots),
            [
                weights_shape,
                kv_shape,
                VMEM((width, mem_slots), BF16),
                flat_shape,
                VMEM((slots, local), BF16),
                VMEM((slots, 3 * local), BF16),
                squares,
                VMEM((mp, 2, local), F32),
                dma,
            ],
            60 * matmul,
            24 * plain,
            "head_back",
            2,
        )(
            meta,
            dz1,
            hidden_row,
            qkv,
            self_low,
            dz2,
            first,
            cross_dq,
            cross_low,
            cross_sums,
            cross_local,
            ffn_sums,
            kv_low,
            *memory_blocks,
            *head_pieces,
            own_self,
            self_proj,
        )
        ffn_from, memory_out, memory_last, hidden_grad, small, head_beside, head_mine = meet(
            ffn_from, memory_out, memory_grads[3], hidden_grad, small, head_beside, head_mine
        )
        head_other = swap(head_beside, 1)
        ffn_group = Group(lambda slot, *at: ffn_rest[(slot - 4, *at)].astype(F32))
        late_two, late_four = ffn_group.second(*ffn_from)
        ffn_late = swap(late_two, 2), swap(late_four, 4)
        small = small + flip(small, 1)
        memory_out.append(shift(after(memory_last, small), 3))
        four_slots = VMEM((4, 2, 2 * width // SUB, width), BF16)
        to_two, to_four = call(
            add_slots,
            in_place(2),
            (pair_slots, pair_slots),
            [four_slots, four_slots, four_slots, dma],
            0,
            4 * plain,
            "add_slots",
            2,
        )(head_mine, head_other)
        to_two, to_four, head_other, ffn_late, memory_out, small = meet(
            to_two, to_four, head_other, ffn_late, memory_out, small
        )
        ffn_total, ffn_blocks = ffn_group.third(*ffn_from, *ffn_late)

        def head_summed(*slots):
            return head_mine[slots].astype(F32) + head_other[slots].astype(F32)

        head_group = Group(head_summed)
        head_from = swap(to_two, 2), swap(to_four, 4)
        ffn_sent = [flip(ffn_blocks[step - 1], step) for step in range(1, mp)]

        def joined(kernel, blocks, shape, dtype, name):
            return call(
                kernel, [META] + in_vmem(mp), (shaped(shape, dtype),), [], 0, 2 * plain, name
            )(meta, *blocks)[0]

        rows_shape = (mp * slots, width)
        memory_grad = joined(
            join_columns, memory_out, (local, mp * mem_slots), F32, "join_memory"
        )
        result = joined(join_rows, result_blocks, rows_shape, BF16, "join_result")
        head_from, ffn_sent, memory_grad, result, hidden_grad = meet(
            head_from, ffn_sent, memory_grad, result, hidden_grad
        )
        late_two, late_four = head_group.second(*head_from)
        head_late = swap(late_two, 2), swap(late_four, 4)
        hidden_low = hidden_grad.astype(BF16)
        hidden_blocks = [hidden_low, shift(hidden_low, 1), None, shift(hidden_low, 3)]
        small = after(small, hidden_blocks[3])
        bit = 2
        while bit < mp:
            small = small + flip(small, bit)
            bit *= 2
        ffn_low = line_sum(ffn_total, ffn_sent)
        small = small + swap(small, 1)
        bit = SUB
        while bit < dp:
            small = small + swap(small, bit)
            bit *= 2
        head_late, ffn_low, small, hidden_blocks = meet(
            head_late, ffn_low, small, hidden_blocks
        )
        head_total, head_blocks = head_group.third(*head_from, *head_late)
        ffn_low, head_blocks = meet(ffn_low, head_blocks)
        head_sent = [flip(head_blocks[step - 1], step) for step in range(1, mp)]
        ffn_near = near_chips(ffn_low)
        small, *ffn_near = meet(small, *ffn_near)
        small = small + swap(small, 2)
        small = small + swap(small, 4)
        ffn_near[0], _ = meet(ffn_near[0], head_sent[0])
        ffn_far = far_chips(*ffn_near)
        ffn_reduced = (ffn_low, *ffn_near, *ffn_far)
        ffn_joined = jnp.concatenate(ffn_reduced)
        head_sent, ffn_reduced, ffn_joined, small, hidden_blocks = meet(
            head_sent, ffn_reduced, ffn_joined, small, hidden_blocks
        )
        head_low = line_sum(head_total, head_sent)
        head_near = near_chips(head_low)
        hidden_blocks[2] = shift(hidden_blocks[0], 2)
        ffn_joined = swap(ffn_joined, 1)
        grad_in, grad_out = call(
            finish_ffn,
            [META] + in_vmem(6),
            (shaped((width, inner)), shaped((inner, width))),
            [],
            0,
            plain,
            "finish_ffn",
        )(meta, *ffn_reduced, ffn_joined)
        head_near, grad_in, grad_out, hidden_blocks = meet(
            head_near, grad_in, grad_out, hidden_blocks
        )
        hidden_grad = joined(join_rows, hidden_blocks, rows_shape, F32, "join_hidden")
        head_far = far_chips(*head_near)
        head_beside = [swap(piece, 1) for piece in (head_low, *head_near)]
        head_far, head_beside, hidden_grad = meet(head_far, head_beside, hidden_grad)
        head_beside += [swap(piece, 1) for piece in head_far]
        finished = call(
            finish_heads,
            [META] + in_vmem(11),
            (
                shaped((3 * local, width)),
                shaped((local, width)),
                shaped((local, width)),
                shaped((local, width)),
                shaped((2 * local, width)),
                shaped((3, width)),
                shaped((3, width)),
                shaped((3, width)),
                shaped((2, local)),
                shaped((2, local)),
                shaped((inner,)),
            ),
            [],
            0,
            plain,
            "finish_heads",
        )(meta, small, head_low, *head_near, *head_far, *head_beside)
        grad_self, grad_sp, grad_cq, grad_cp, grad_kv = finished[:5]
        return (
            result,
            hidden_grad,
            memory_grad.T,
            jnp.swapaxes(grad_self.reshape(3, local, width), 1, 2),
            finished[8],
            grad_sp,
            grad_cq.T,
            jnp.swapaxes(grad_kv.reshape(2, local, width), 1, 2),
            finished[9],
            grad_cp,
            grad_in,
            finished[10],
            grad_out,
            *finished[5:8],
        )

    return jax.shard_map(
        body,
        mesh=mesh,
        in_specs=(
            P("dp", None),
            P("dp", "mp"),
            P("dp", None),
            P("dp", None),
            P("dp"),
            P("dp", None),
            P("dp"),
            P(None, None, "mp"),
            P(None, "mp"),
            P("mp", None),
            P(None, "mp"),
            P(None, None, "mp"),
            P(None, "mp"),
            P("mp", None),
            P(None, "mp"),
            P("mp"),
            P("mp", None),
            P(),
            P(),
            P(),
        ),
        out_specs=(
            P("dp", None),
            P("dp", None),
            P("dp", "mp"),
            P(None, None, "mp"),
            P(None, "mp"),
            P("mp", None),
            P(None, "mp"),
            P(None, None, "mp"),
            P(None, "mp"),
            P("mp", None),
            P(None, "mp"),
            P("mp"),
            P("mp", None),
            P(),
            P(),
            P(),
        ),
        check_vma=False,
    )
```
